32 devices in a mesh: band: 16 (over z, y, x), head: 2 (over core).
Axes of the slice: x: 2, y: 2, z: 4, core: 2. Of those that a mesh axis runs over, the one named last changes fastest.
Arguments:
- tokens: bfloat16 [2, 4096, 1024], P(None, 'band'), may hold values from -6 to 6
- text_states: bfloat16 [2, 2048, 1024], P(None, 'band'), may hold values from -6 to 6
- cotangent: bfloat16 [2, 4096, 1024], P(None, 'band'), may hold values from -18 to 18
- earlier: int32 [2, 16], P(None, 'band'), may hold values from 0 to 3, as said below
- proj_master: float32 [6, 1024, 1024], P(None, 'band', 'head'), may hold values from -0.1875 to 0.1875
- out_master: float32 [2, 1024, 1024], P(None, 'band', 'head'), may hold values from -0.75 to 0.75
- mlp_master: float32 [2, 1024, 4096], P(None, 'band', 'head'), may hold values from -0.1875 to 0.1875
- gain_master: float32 [3, 1024], P(None, 'band'), may hold values from 0.4 to 2.4
- proj_first: float32 [6, 1024, 1024], P(None, 'band', 'head'), may hold values from -0.00015258789 to 0.00015258789
- proj_second: float32 [6, 1024, 1024], P(None, 'band', 'head'), may hold values from 2.9802323e-09 to 1.1920929e-08
- out_first: float32 [2, 1024, 1024], P(None, 'band', 'head'), may hold values from -0.00015258789 to 0.00015258789
- out_second: float32 [2, 1024, 1024], P(None, 'band', 'head'), may hold values from 2.9802323e-09 to 1.1920929e-08
- mlp_first: float32 [2, 1024, 4096], P(None, 'band', 'head'), may hold values from -0.00015258789 to 0.00015258789
- mlp_second: float32 [2, 1024, 4096], P(None, 'band', 'head'), may hold values from 2.9802323e-09 to 1.1920929e-08
- gain_first: float32 [3, 1024], P(None, 'band'), may hold values from -0.0004272461 to 0.0004272461
- gain_second: float32 [3, 1024], P(None, 'band'), may hold values from 2.3841858e-08 to 9.536743e-08
Outputs:
- block_out: bfloat16 [2, 4096, 1024], P(None, 'band')
- grad_tokens: float32 [2, 4096, 1024], P(None, 'band')
- grad_text: float32 [2, 2048, 1024], P(None, 'band')
- grad_norm: float32 [], replicated
- new_proj: float32 [6, 1024, 1024], P(None, 'band', 'head')
- new_proj_first: float32 [6, 1024, 1024], P(None, 'band', 'head')
- new_proj_second: float32 [6, 1024, 1024], P(None, 'band', 'head')
- new_out: float32 [2, 1024, 1024], P(None, 'band', 'head')
- new_out_first: float32 [2, 1024, 1024], P(None, 'band', 'head')
- new_out_second: float32 [2, 1024, 1024], P(None, 'band', 'head')
- new_mlp: float32 [2, 1024, 4096], P(None, 'band', 'head')
- new_mlp_first: float32 [2, 1024, 4096], P(None, 'band', 'head')
- new_mlp_second: float32 [2, 1024, 4096], P(None, 'band', 'head')
- new_gain: float32 [3, 1024], P(None, 'band')
- new_gain_first: float32 [3, 1024], P(None, 'band')
- new_gain_second: float32 [3, 1024], P(None, 'band')
The draws below stay inside these ranges and needn't reach their ends.
Inputs may be any that keep to these rules, and one draw needn't show every extreme that they name: `earlier`: in each stream the 16 bands hold 3 grids of 4 consecutive bands and 4 grids of one band; a band's entry is its place inside its grid, so a grid of 4 bands carries 0 to 3 on consecutive bands and a grid of one band carries 0. Each stream begins with a grid of 4 bands; band 16 // 2 lies in a grid of 4 bands, at place 1 in even streams and at place 3 in odd ones; the other grids stand in an order drawn from the seed.
All inputs are finite; a program needn't handle non-finite values.
Results may differ from the reference program's by a relative error of at most 0.02.
The reference program's roundings to bfloat16 on the way count: a program that leaves them out, or rounds other values in their place, can miss the bound.
Values may be sent and summed in bfloat16 or wider, within the bound.
A program may use at most 192 MiB of HBM per device.

```python
import math
import jax
import jax.numpy as jnp
from jax import lax

D = 1024
HEADS = 16
HEAD_DIM = 64
FF = 4096
TEXT = 128
TOK_DEV = 256
STREAMS = 2
SEQ_BANDS = 4
STEP = 10
BANDS = 16
TOKENS = 4096
TEXT_ALL = 2048
BIG_GRIDS = 3
SMALL_GRIDS = 4


def draw_earlier(key, part):
    rows = []
    for stream in range(STREAMS):
        place = 1 + 2 * (stream % 2)
        first_len = BANDS // 2 - place - SEQ_BANDS
        first_big = first_len // SEQ_BANDS
        first_small = first_len % SEQ_BANDS
        rest_big = BIG_GRIDS - 2 - first_big
        rest_small = SMALL_GRIDS - first_small
        stream_key = jax.random.fold_in(key, 7 + stream)
        key_first, key_rest = jax.random.split(stream_key)
        first_spans = jax.random.permutation(key_first, jnp.array([SEQ_BANDS] * first_big + [1] * first_small, dtype=jnp.int32))
        rest_spans = jax.random.permutation(key_rest, jnp.array([SEQ_BANDS] * rest_big + [1] * rest_small, dtype=jnp.int32))
        lead = jnp.array([SEQ_BANDS], dtype=jnp.int32)
        grid_spans = jnp.concatenate([lead, first_spans, lead, rest_spans]).astype(jnp.int32)
        grid_ends = jnp.cumsum(grid_spans).astype(jnp.int32)
        grid_starts = grid_ends - grid_spans
        band_place = jnp.arange(BANDS, dtype=jnp.int32)
        inside = (band_place[:, None] >= grid_starts[None, :]) & (band_place[:, None] < grid_ends[None, :])
        rows.append(jnp.sum(jnp.where(inside, band_place[:, None] - grid_starts[None, :], 0), axis=1).astype(jnp.int32))
    return jnp.stack(rows)


def draw_cotangent(key, part):
    ramp_place = jnp.arange(D, dtype=jnp.float32) / (D - 1)
    base = jnp.clip(jax.random.normal(jax.random.fold_in(key, 11), (STREAMS, TOKENS, D), jnp.float32), -6.0, 6.0)
    ramp = 1.0 + 2.0 * ramp_place
    return (base * ramp).astype(jnp.bfloat16)


def draw_gain_master(key, part):
    ramp_place = jnp.arange(D, dtype=jnp.float32) / (D - 1)
    rough = jnp.exp(jax.random.uniform(jax.random.fold_in(key, 13), (3, D), jnp.float32, jnp.log(0.8), jnp.log(1.25)))
    ramp = 0.6 * jnp.exp(jnp.log(3.0) * ramp_place)
    return (rough * ramp[None, :]).astype(jnp.float32)


def levels(own_key, shape, cuts, smallest, largest):
    loudness = 1.0
    for axis_at, parts in cuts:
        draws = jax.random.uniform(jax.random.fold_in(jax.random.fold_in(own_key, 6), axis_at), (parts,), jnp.float32, smallest / len(cuts), largest / len(cuts))
        loudness = loudness * jnp.repeat(jnp.exp(draws), shape[axis_at] // parts).reshape((-1,) + (1,) * (len(shape) - 1 - axis_at))
    return loudness


def bell_draw(key, dims, width, limit, cuts=(), kind=jnp.bfloat16):
    loudness = levels(key, dims, cuts, -0.22, 0.18) if cuts else 1.0
    drawn = jax.random.normal(key, dims, jnp.float32) * width * loudness
    return jnp.minimum(jnp.maximum(drawn, -limit), limit).astype(kind)


def setup_inputs(seed: int = 0) -> dict:
    splits = jax.random.split(jax.random.key(seed), 17)
    tokens = bell_draw(splits[0], (STREAMS, TOKENS, D), 1.0, 6.0, ((1, 16),))
    text_states = bell_draw(splits[1], (STREAMS, TEXT_ALL, D), 1.0, 6.0, ((1, 16),))
    cotangent = draw_cotangent(jax.random.fold_in(splits[16], 71), 0)
    earlier = draw_earlier(jax.random.fold_in(splits[16], 71), 0)
    proj_master = bell_draw(splits[4], (6, D, D), D ** -0.5, 0.1875, ((1, 16), (2, 2)), jnp.float32)
    out_master = bell_draw(splits[5], (2, D, D), (D // 16) ** -0.5, 0.75, ((1, 16), (2, 2)), jnp.float32)
    mlp_master = bell_draw(splits[6], (2, D, FF), D ** -0.5, 0.1875, ((1, 16), (2, 2)), jnp.float32)
    gain_master = draw_gain_master(jax.random.fold_in(splits[16], 71), 0)
    proj_first = bell_draw(splits[8], (6, D, D), (0.11 / (8 * D * D + 2 * D * FF) ** 0.5), 0.00015258789, ((1, 16), (2, 2)), jnp.float32)
    proj_second = jnp.clip(jnp.exp(math.log(1.1920929132713809e-08) - 1.3862944 * jax.random.uniform(splits[9], (6, D, D), jnp.float32) ** levels(splits[9], (6, D, D), ((1, 16), (2, 2)), -0.2, 0.2)), 2.9802322831784522e-09, 1.1920929132713809e-08)
    out_first = bell_draw(splits[10], (2, D, D), (0.11 / (8 * D * D + 2 * D * FF) ** 0.5), 0.00015258789, ((1, 16), (2, 2)), jnp.float32)
    out_second = jnp.clip(jnp.exp(math.log(1.1920929132713809e-08) - 1.3862944 * jax.random.uniform(splits[11], (2, D, D), jnp.float32) ** levels(splits[11], (2, D, D), ((1, 16), (2, 2)), -0.2, 0.2)), 2.9802322831784522e-09, 1.1920929132713809e-08)
    mlp_first = bell_draw(splits[12], (2, D, FF), (0.11 / (8 * D * D + 2 * D * FF) ** 0.5), 0.00015258789, ((1, 16), (2, 2)), jnp.float32)
    mlp_second = jnp.clip(jnp.exp(math.log(1.1920929132713809e-08) - 1.3862944 * jax.random.uniform(splits[13], (2, D, FF), jnp.float32) ** levels(splits[13], (2, D, FF), ((1, 16), (2, 2)), -0.2, 0.2)), 2.9802322831784522e-09, 1.1920929132713809e-08)
    gain_first = bell_draw(splits[14], (3, D), (0.3 / (8 * D * D + 2 * D * FF) ** 0.5), 0.0004272461, ((1, 16),), jnp.float32)
    gain_second = jnp.clip(jnp.exp(math.log(9.536743306171047e-08) - 1.3862944 * jax.random.uniform(splits[15], (3, D), jnp.float32) ** levels(splits[15], (3, D), ((1, 16),), -0.2, 0.2)), 2.3841858265427618e-08, 9.536743306171047e-08)
    return {"tokens": tokens, "text_states": text_states, "cotangent": cotangent, "earlier": earlier, "proj_master": proj_master, "out_master": out_master, "mlp_master": mlp_master, "gain_master": gain_master, "proj_first": proj_first, "proj_second": proj_second, "out_first": out_first, "out_second": out_second, "mlp_first": mlp_first, "mlp_second": mlp_second, "gain_first": gain_first, "gain_second": gain_second}


EPS = 1e-05
NEG = -1e+30
CLIP = 1.0
BETA_ONE = 0.9
BETA_TWO = 0.95
ADAM_EPS = 1e-08
DECAY = 0.1
GAIN_RATE = 0.5

@jax.custom_vjp
def low(v):
    return lax.optimization_barrier(v.astype(jnp.bfloat16)).astype(jnp.float32)

@jax.custom_vjp
def low_back(v):
    return v

def low_keep(v):
    return (low(v), None)

def low_pass(kept, grad):
    return (grad,)

def back_keep(v):
    return (v, None)

def back_low(kept, grad):
    return (low(grad),)
low.defvjp(low_keep, low_pass)
low_back.defvjp(back_keep, back_low)

def round_both(values):
    return low_back(low(values))

def product(former, latter):
    return jnp.dot(former, latter, precision=lax.Precision.HIGHEST, preferred_element_type=jnp.float32)

def product_t(former, latter):
    return lax.dot_general(former, latter, (((1,), (1,)), ((), ())), precision=lax.Precision.HIGHEST, preferred_element_type=jnp.float32)

def norm_rows(values, gain_row):
    centre = values - lax.optimization_barrier(jnp.mean(values, axis=-1, keepdims=True))
    spread = lax.optimization_barrier(jnp.mean(centre * centre, axis=-1, keepdims=True))
    return centre * lax.rsqrt(spread + EPS) * gain_row

def forward(inputs, text_in, proj, outs, mlp, gains, earlier):
    proj_w = low(proj)
    out_w = low(outs)
    mlp_w = low(mlp)
    gain_w = low(gains)
    row_count = STREAMS * BANDS * TOK_DEV
    flat_rows = inputs.reshape(row_count, D)
    normed_one = low(norm_rows(flat_rows, gain_w[0]))
    queries = round_both(product(normed_one, proj_w[0]))
    keys_all = round_both(product(normed_one, proj_w[1]))
    values = round_both(product(normed_one, proj_w[2]))
    band_shape = (STREAMS, BANDS, TOK_DEV, HEADS, HEAD_DIM)
    query_bands = queries.reshape(band_shape)
    padding = jnp.zeros((STREAMS, SEQ_BANDS - 1, TOK_DEV, HEADS, HEAD_DIM), jnp.float32)
    key_pad = jnp.concatenate([padding, keys_all.reshape(band_shape)], axis=1)
    value_pad = jnp.concatenate([padding, values.reshape(band_shape)], axis=1)
    row_ids = jnp.arange(TOK_DEV, dtype=jnp.int32)[:, None]
    col_ids = jnp.arange(SEQ_BANDS * TOK_DEV, dtype=jnp.int32)[None, :]
    behind_ids = SEQ_BANDS - 1 - col_ids // TOK_DEV
    position = col_ids % TOK_DEV

    def one_band(band_index):
        stream_id = band_index // BANDS
        band_id = band_index % BANDS
        zero_index = jnp.zeros((), jnp.int32)
        corner = (stream_id, band_id, zero_index, zero_index, zero_index)
        key_win = lax.dynamic_slice(key_pad, corner, (1, SEQ_BANDS, TOK_DEV, HEADS, HEAD_DIM)).reshape(SEQ_BANDS * TOK_DEV, HEADS, HEAD_DIM)
        value_win = lax.dynamic_slice(value_pad, corner, (1, SEQ_BANDS, TOK_DEV, HEADS, HEAD_DIM)).reshape(SEQ_BANDS * TOK_DEV, HEADS, HEAD_DIM)
        query_win = lax.dynamic_slice(query_bands, corner, (1, 1, TOK_DEV, HEADS, HEAD_DIM)).reshape(TOK_DEV, HEADS, HEAD_DIM)
        offset = lax.dynamic_slice(earlier, (stream_id, band_id), (1, 1))[0, 0]
        allowed = (behind_ids <= offset) & ((behind_ids > 0) | (position <= row_ids))
        scores = low_back(jnp.einsum('qhd,khd->hqk', query_win, key_win, precision=lax.Precision.HIGHEST) * HEAD_DIM ** (-0.5))
        scores = jnp.where(allowed[None], scores, NEG)
        attention = jax.nn.softmax(scores, axis=-1)
        result = jnp.einsum('hqk,khd->qhd', low(attention), value_win, precision=lax.Precision.HIGHEST)
        return round_both(result)
    band_list = jnp.arange(STREAMS * BANDS, dtype=jnp.int32)
    attended = lax.map(jax.checkpoint(one_band), band_list).reshape(row_count, D)
    hidden_one = flat_rows + low_back(product_t(attended, out_w[0]))
    normed_two = low(norm_rows(hidden_one, gain_w[1]))
    cross_queries = round_both(product(normed_two, proj_w[3])).reshape(STREAMS * BANDS, TOK_DEV, HEADS, HEAD_DIM)
    text_rows = text_in.reshape(STREAMS * BANDS * TEXT, D)
    cross_keys = round_both(product(text_rows, proj_w[4])).reshape(STREAMS * BANDS, TEXT, HEADS, HEAD_DIM)
    cross_values = round_both(product(text_rows, proj_w[5])).reshape(STREAMS * BANDS, TEXT, HEADS, HEAD_DIM)

    def one_cross(band_index):
        stream_id = band_index // BANDS
        band_id = band_index % BANDS
        offset = lax.dynamic_slice(earlier, (stream_id, band_id), (1, 1))[0, 0]
        slot_index = (band_index - offset).astype(jnp.int32)
        query_win = lax.dynamic_index_in_dim(cross_queries, band_index, keepdims=False)
        key_win = lax.dynamic_index_in_dim(cross_keys, slot_index, keepdims=False)
        value_win = lax.dynamic_index_in_dim(cross_values, slot_index, keepdims=False)
        scores = low_back(jnp.einsum('qhd,khd->hqk', query_win, key_win, precision=lax.Precision.HIGHEST) * HEAD_DIM ** (-0.5))
        attention = jax.nn.softmax(scores, axis=-1)
        result = jnp.einsum('hqk,khd->qhd', low(attention), value_win, precision=lax.Precision.HIGHEST)
        return round_both(result)
    crossed = lax.map(jax.checkpoint(one_cross), band_list).reshape(row_count, D)
    hidden_two = hidden_one + low_back(product_t(crossed, out_w[1]))
    normed_three = low(norm_rows(hidden_two, gain_w[2]))
    before = low_back(product(normed_three, mlp_w[0]))
    activated = low(jax.nn.gelu(before, approximate=False))
    result_rows = hidden_two + low_back(product_t(activated, mlp_w[1]))
    return result_rows.reshape(STREAMS, BANDS * TOK_DEV, D)

def adamw_update(weight, moment_one, moment_two, gradient, step_rate, decay_rate):
    moment_one_new = BETA_ONE * moment_one + (1.0 - BETA_ONE) * gradient
    moment_two_new = BETA_TWO * moment_two + (1.0 - BETA_TWO) * gradient * gradient
    unbiased_one = moment_one_new / (1.0 - BETA_ONE ** STEP)
    unbiased_two = moment_two_new / (1.0 - BETA_TWO ** STEP)
    weight_new = weight - step_rate * (unbiased_one / (jnp.sqrt(unbiased_two) + ADAM_EPS) + decay_rate * weight)
    return (weight_new, moment_one_new, moment_two_new)

def reference(tokens, text_states, cotangent, earlier, proj_master, out_master, mlp_master, gain_master, proj_first, proj_second, out_first, out_second, mlp_first, mlp_second, gain_first, gain_second):

    def wrapped(inputs, text_in, proj, outs, mlp, gains):
        return forward(inputs, text_in, proj, outs, mlp, gains, earlier)
    block_rows, pull_back = jax.vjp(wrapped, tokens.astype(jnp.float32), text_states.astype(jnp.float32), proj_master, out_master, mlp_master, gain_master)
    grad_tokens, grad_text, proj_grad, out_grad, mlp_grad, gain_grad = pull_back(cotangent.astype(jnp.float32))
    squares = jnp.sum(proj_grad * proj_grad) + jnp.sum(out_grad * out_grad) + jnp.sum(mlp_grad * mlp_grad) + jnp.sum(gain_grad * gain_grad)
    grad_norm = jnp.sqrt(squares)
    factor = jnp.minimum(1.0, CLIP / grad_norm)
    matrix_rate = 2.0 * D ** (-0.5)
    new_proj = adamw_update(proj_master, proj_first, proj_second, proj_grad * factor, matrix_rate, DECAY)
    new_out = adamw_update(out_master, out_first, out_second, out_grad * factor, matrix_rate, DECAY)
    new_mlp = adamw_update(mlp_master, mlp_first, mlp_second, mlp_grad * factor, matrix_rate, DECAY)
    new_gain = adamw_update(gain_master, gain_first, gain_second, gain_grad * factor, GAIN_RATE, 0.0)
    return (block_rows.astype(jnp.bfloat16), grad_tokens, grad_text, grad_norm, new_proj[0], new_proj[1], new_proj[2], new_out[0], new_out[1], new_out[2], new_mlp[0], new_mlp[1], new_mlp[2], new_gain[0], new_gain[1], new_gain[2])
```

```python
from functools import partial

import jax
import jax.numpy as jnp
from jax import lax
from jax.experimental import pallas as pl
from jax.experimental.pallas import tpu as pltpu
from jax.sharding import PartitionSpec as P

D = 1024
HEAD_DIM = 64
SEQ_BANDS = 4
STEP = 10


EPS = 1e-05
NEG = -1e30
CLIP = 1.0
BETA_ONE = 0.9
BETA_TWO = 0.95
ADAM_EPS = 1e-08
DECAY = 0.1
GAIN_RATE = 0.5


MESH = pl.DeviceIdType.MESH
ORDERS = ((2, 0, 1), (1, 0, 2))
GROUP = 4


def band_dims(bands):
    inner = 4 if bands >= 64 else 2
    return (bands // (inner * inner), inner, inner)


def strides_of(dims):
    return (dims[1] * dims[2], dims[2], 1)


def place_of(dims):
    band = lax.axis_index("band")
    return band, (
        band // (dims[1] * dims[2]),
        (band // dims[2]) % dims[1],
        band % dims[2],
    )


def stage_list(dims, order):
    return [(phase, step) for phase in range(3) for step in range(dims[order[phase]] - 1)]


def block_of(ref, lead, place, order, phase, index, columns):
    at = list(place)
    for done in range(phase):
        at[order[done]] = slice(None)
    at[order[phase]] = index
    return ref.at[(*lead, *at, slice(None), columns)]


def greet(dims, place, band, head, extra):
    barrier = pltpu.get_barrier_semaphore()
    strides = strides_of(dims)
    total = jnp.int32(0)
    peers = []
    for axis in range(3):
        for sign in (1, -1):
            there = place[axis] + sign
            peers.append(((there >= 0) & (there < dims[axis]), band + sign * strides[axis], head))
    peers += extra
    for present, peer_band, peer_head in peers:
        @pl.when(present)
        def _():
            pl.semaphore_signal(barrier, inc=1, device_id=(peer_band, peer_head), device_id_type=MESH)
        total = total + present.astype(jnp.int32)
    pl.semaphore_wait(barrier, total)


def gather_kernel(dims, has_context, *refs):
    if has_context:
        (w_ref, gain_ref, ctx_ref, out_ref, gains_ref, ctx_out,
         own_sem, send_sem, recv_sem, gsend, grecv, prev_ref, up_sem, csend, crecv, psend, precv) = refs
    else:
        (w_ref, gain_ref, out_ref, gains_ref, own_sem, send_sem, recv_sem, gsend, grecv) = refs
    band, place = place_of(dims)
    head = lax.axis_index("head")
    strides = strides_of(dims)
    count = w_ref.shape[0]
    half = w_ref.shape[2] // 2
    bands = dims[0] * dims[1] * dims[2]
    true = band >= 0
    extra = []
    if has_context:
        base = (band // GROUP) * GROUP
        mine = band % GROUP
        for shift in range(1, GROUP):
            extra.append((true, base + (mine + shift) % GROUP, head))
        extra.append((band + GROUP < bands, band + GROUP, head))
        extra.append((band >= GROUP, band - GROUP, head))
        extra.append((true, band, 1 - head))
    greet(dims, place, band, head, extra)

    own = [
        pltpu.make_async_copy(w_ref, out_ref.at[:, place[0], place[1], place[2]], own_sem.at[0]),
        pltpu.make_async_copy(gain_ref, gains_ref.at[place[0], place[1], place[2]], own_sem.at[1]),
    ]
    for copy in own:
        copy.start()

    def up_copy():
        return pltpu.make_async_remote_copy(
            ctx_ref, prev_ref, up_sem.at[0], up_sem.at[1], device_id=(band + GROUP, head), device_id_type=MESH
        )

    def peer_copy(back, source):
        return pltpu.make_async_remote_copy(
            source, ctx_out.at[head, back - 1], csend.at[back - 1], crecv.at[back - 1],
            device_id=(base + (mine + back) % GROUP, head), device_id_type=MESH,
        )

    def pair_copy(back):
        return pltpu.make_async_remote_copy(
            ctx_out.at[head, back - 1], ctx_out.at[head, back - 1], psend.at[back - 1], precv.at[back - 1],
            device_id=(band, 1 - head), device_id_type=MESH,
        )

    if has_context:
        @pl.when(band + GROUP < bands)
        def _():
            up_copy().start()
        for back in range(1, GROUP):
            @pl.when(mine + back < GROUP)
            def _():
                peer_copy(back, ctx_ref).start()

    def piece(color, m, phase, step, way, incoming):
        order = ORDERS[color]
        axis = order[phase]
        size, at = dims[axis], place[axis]
        toward = 1 if way == 0 else -1
        stage = stage_list(dims, order).index((phase, step))
        if incoming:
            index = at - toward * (step + 1)
            present = (index >= 0) & (index < size)
        else:
            index = at - toward * step
            present = (index >= 0) & (index < size) & (at + toward >= 0) & (at + toward < size)
        columns = pl.ds(color * half, half)
        target = (band + toward * strides[axis], head)
        land = block_of(out_ref, (m,), place, order, phase, index, columns)
        source = w_ref.at[m, :, columns] if stage == 0 else land
        copy = pltpu.make_async_remote_copy(
            source, land, send_sem.at[color, stage, way, m], recv_sem.at[color, stage, way, m],
            device_id=target, device_id_type=MESH,
        )
        return present, copy

    def gain_piece(phase, step, way, incoming):
        order = ORDERS[0]
        axis = order[phase]
        size, at = dims[axis], place[axis]
        toward = 1 if way == 0 else -1
        stage = stage_list(dims, order).index((phase, step))
        if incoming:
            index = at - toward * (step + 1)
            present = (index >= 0) & (index < size)
        else:
            index = at - toward * step
            present = (index >= 0) & (index < size) & (at + toward >= 0) & (at + toward < size)
        land = block_of(gains_ref, (), place, order, phase, index, slice(None))
        source = gain_ref if stage == 0 else land
        copy = pltpu.make_async_remote_copy(
            source, land, gsend.at[stage, way], grecv.at[stage, way],
            device_id=(band + toward * strides[axis], head), device_id_type=MESH,
        )
        return present, copy

    stages = [stage_list(dims, order) for order in ORDERS]
    depth = len(stages[0])

    def context_step(t):
        @pl.when(t == 1)
        def _():
            @pl.when(band >= GROUP)
            def _():
                pltpu.make_async_remote_copy(
                    ctx_ref, prev_ref, up_sem.at[0], up_sem.at[1], device_id=(band - GROUP, head), device_id_type=MESH
                ).wait_recv()
            for back in range(1, GROUP):
                @pl.when((mine + back >= GROUP) & (band >= GROUP))
                def _():
                    peer_copy(back, prev_ref).start()
        @pl.when(t == 4)
        def _():
            for back in range(1, GROUP):
                @pl.when((mine >= back) | (band >= GROUP))
                def _():
                    peer_copy(back, ctx_ref).wait_recv()
                    pair_copy(back).start()

    def gains_step(t):
        for stage in range(depth + 1):
            @pl.when(t == stage)
            def _():
                if stage == 1:
                    for copy in own:
                        copy.wait()
                if stage > 0:
                    for way in range(2):
                        present, copy = gain_piece(*stages[0][stage - 1], way, True)
                        @pl.when(present)
                        def _():
                            copy.wait_recv()
                if stage < depth:
                    for way in range(2):
                        present, copy = gain_piece(*stages[0][stage], way, False)
                        @pl.when(present)
                        def _():
                            copy.start()

    def body(t, carry):
        gains_step(t)
        if has_context:
            context_step(t)
        for stage in range(depth, -1, -1):
            m = t - stage
            @pl.when((m >= 0) & (m < count))
            def _():
                for color in range(2):
                    if stage > 0:
                        for way in range(2):
                            present, copy = piece(color, m, *stages[color][stage - 1], way, True)
                            @pl.when(present)
                            def _():
                                copy.wait_recv()
                    if stage < depth:
                        for way in range(2):
                            present, copy = piece(color, m, *stages[color][stage], way, False)
                            @pl.when(present)
                            def _():
                                copy.start()
        return carry

    lax.fori_loop(0, count + depth, body, 0)

    if has_context:
        for back in range(1, GROUP):
            @pl.when((mine >= back) | (band >= GROUP))
            def _():
                pltpu.make_async_remote_copy(
                    ctx_out.at[1 - head, back - 1], ctx_out.at[1 - head, back - 1], psend.at[back - 1],
                    precv.at[back - 1], device_id=(band, 1 - head), device_id_type=MESH,
                ).wait_recv()
                pair_copy(back).wait_send()
            @pl.when((mine + back < GROUP) | (band >= GROUP))
            def _():
                peer_copy(back, ctx_ref).wait_send()
        @pl.when(band + GROUP < bands)
        def _():
            up_copy().wait_send()

    for stage in range(depth):
        for way in range(2):
            present, copy = gain_piece(*stages[0][stage], way, False)
            @pl.when(present)
            def _():
                copy.wait_send()

    def drain(m, carry):
        for stage in range(depth):
            for color in range(2):
                for way in range(2):
                    present, copy = piece(color, m, *stages[color][stage], way, False)
                    @pl.when(present)
                    def _():
                        copy.wait_send()
        return carry

    lax.fori_loop(0, count, drain, 0)


def gather_weights(bands, shard, gain_tile, context, collective_id):
    dims = band_dims(bands)
    count, rows, width = shard.shape
    depth = len(stage_list(dims, ORDERS[0]))
    vmem = pl.BlockSpec(memory_space=pltpu.VMEM)
    anyspace = pl.BlockSpec(memory_space=pl.ANY)
    has_context = context is not None
    out_shape = [
        jax.ShapeDtypeStruct((count, *dims, rows, width), shard.dtype),
        jax.ShapeDtypeStruct((*dims, *gain_tile.shape), gain_tile.dtype),
    ]
    scratch = [
        pltpu.SemaphoreType.DMA((2,)),
        pltpu.SemaphoreType.DMA((2, depth, 2, count)),
        pltpu.SemaphoreType.DMA((2, depth, 2, count)),
        pltpu.SemaphoreType.DMA((depth, 2)),
        pltpu.SemaphoreType.DMA((depth, 2)),
    ]
    args = [shard, gain_tile]
    if has_context:
        args.append(context)
        out_shape.append(jax.ShapeDtypeStruct((2, GROUP - 1, *context.shape), context.dtype))
        scratch += [
            pltpu.VMEM(context.shape, context.dtype),
            pltpu.SemaphoreType.DMA((2,)),
            pltpu.SemaphoreType.DMA((GROUP - 1,)),
            pltpu.SemaphoreType.DMA((GROUP - 1,)),
            pltpu.SemaphoreType.DMA((GROUP - 1,)),
            pltpu.SemaphoreType.DMA((GROUP - 1,)),
        ]
    return pl.pallas_call(
        partial(gather_kernel, dims, has_context),
        out_shape=out_shape,
        in_specs=[vmem] * len(args),
        out_specs=[anyspace] * len(out_shape),
        scratch_shapes=scratch,
        compiler_params=pltpu.CompilerParams(collective_id=collective_id, has_side_effects=True),
        name="gather_weights",
    )(*args)


def reduce_kernel(dims, has_context, *refs):
    if has_context:
        (g_ref, back_ref, out_ref, back_out, gv, load_sem, last_ref, mid_ref, first_ref, send_sem, recv_sem,
         landed, relay, from_up, csend, crecv, up_sem) = refs
    else:
        (g_ref, out_ref, gv, load_sem, last_ref, mid_ref, first_ref, send_sem, recv_sem) = refs
    band, place = place_of(dims)
    head = lax.axis_index("head")
    strides = strides_of(dims)
    count = g_ref.shape[0]
    half = g_ref.shape[-1] // 2
    bands = dims[0] * dims[1] * dims[2]
    true = band >= 0
    orders = tuple(order[::-1] for order in ORDERS)
    lands = (last_ref, mid_ref, first_ref)

    def load(m):
        return pltpu.make_async_copy(g_ref.at[m], gv.at[m], load_sem.at[m])

    def load_all(m, carry):
        load(m).start()
        return carry

    lax.fori_loop(0, count, load_all, 0)

    extra = []
    if has_context:
        base = (band // GROUP) * GROUP
        mine = band % GROUP
        for shift in range(1, GROUP):
            extra.append((true, base + (mine + shift) % GROUP, head))
        extra.append((band + GROUP < bands, band + GROUP, head))
        extra.append((band >= GROUP, band - GROUP, head))
    greet(dims, place, band, head, extra)

    def peer_copy(back):
        return pltpu.make_async_remote_copy(
            back_ref.at[back - 1], landed.at[back - 1], csend.at[back - 1], crecv.at[back - 1],
            device_id=(base + (mine + GROUP - back) % GROUP, head), device_id_type=MESH,
        )

    def down_copy(target):
        return pltpu.make_async_remote_copy(
            relay, from_up, up_sem.at[0], up_sem.at[1], device_id=(target, head), device_id_type=MESH
        )

    if has_context:
        for back in range(1, GROUP):
            @pl.when((mine >= back) | (band >= GROUP))
            def _():
                peer_copy(back).start()

    def slot(size, step, way):
        return 0 if size == 2 else step * 2 + way

    def own_block(m, color, phase, index):
        order = orders[color]
        at = list(place)
        for later in range(phase + 1, 3):
            at[order[later]] = slice(None)
        at[order[phase]] = index
        return gv.at[(m, *at, slice(None), pl.ds(color * half, half))]

    def landing(m, color, phase, step, way):
        size = dims[orders[color][phase]]
        return lands[phase].at[m, color, slot(size, step, way)]

    def outgoing(m, color, phase, step, way):
        axis = orders[color][phase]
        size, at = dims[axis], place[axis]
        toward = 1 if way == 0 else -1
        rank = at if way == 0 else size - 1 - at
        index = size - 1 - step + at if way == 0 else step + at - (size - 1)
        present = (rank <= step) & (at + toward >= 0) & (at + toward < size)
        stage = stage_list(dims, orders[color]).index((phase, step))
        target = (band + toward * strides[axis], head)

        def copy(source):
            return pltpu.make_async_remote_copy(
                source, landing(m, color, phase, step, way),
                send_sem.at[color, stage, way, m], recv_sem.at[color, stage, way, m],
                device_id=target, device_id_type=MESH,
            )

        return present, rank, index, copy

    def arrived(m, color, phase, step, way):
        axis = orders[color][phase]
        size, at = dims[axis], place[axis]
        before = at - 1 if way == 0 else at + 1
        rank = before if way == 0 else size - 1 - before
        present = (before >= 0) & (before < size) & (rank <= step)
        _, _, _, copy = outgoing(m, color, phase, step, way)
        return present, copy(landing(m, color, phase, step, way))

    def add_into(target, source):
        lead = target.shape[:-2]
        if len(lead) == 0:
            target[...] = target[...] + source[...]
        elif len(lead) == 1:
            for i in range(lead[0]):
                target[i] = target[i] + source[i]
        else:
            for i in range(lead[0]):
                for j in range(lead[1]):
                    target[i, j] = target[i, j] + source[i, j]

    stages = [stage_list(dims, order) for order in orders]
    depth = len(stages[0])

    def send(m, color, phase, step):
        axis = orders[color][phase]
        size = dims[axis]
        for way in range(2):
            present, rank, index, copy = outgoing(m, color, phase, step, way)
            @pl.when(present & (rank == 0))
            def _():
                copy(own_block(m, color, phase, index)).start()
            if step > 0:
                @pl.when(present & (rank > 0))
                def _():
                    from_before = landing(m, color, phase, step - 1, way)
                    add_into(from_before, own_block(m, color, phase, index))
                    copy(from_before).start()

    def settle(m, color, phase, step):
        axis = orders[color][phase]
        size = dims[axis]
        for way in range(2):
            present, copy = arrived(m, color, phase, step, way)
            @pl.when(present)
            def _():
                copy.wait_recv()
                if step == size - 2:
                    landed_here = landing(m, color, phase, step, way)
                    if phase < 2:
                        add_into(own_block(m, color, phase, place[axis]), landed_here)
                    else:
                        columns = pl.ds(color * half, half)
                        if size == 2:
                            own = own_block(m, color, phase, place[axis])
                            out_ref[m, :, columns] = own[...].astype(jnp.float32) + landed_here[...].astype(jnp.float32)
                        else:
                            add_into(own_block(m, color, phase, place[axis]), landed_here)
        if phase == 2 and step == size - 2 and size > 2:
            columns = pl.ds(color * half, half)
            out_ref[m, :, columns] = own_block(m, color, phase, place[axis])[...].astype(jnp.float32)

    def body(t, carry):
        for stage in range(depth, -1, -1):
            m = t - stage
            @pl.when((m >= 0) & (m < count))
            def _():
                if stage == 0:
                    load(m).wait()
                for color in range(2):
                    if stage > 0:
                        settle(m, color, *stages[color][stage - 1])
                    if stage < depth:
                        send(m, color, *stages[color][stage])
        if has_context:
            @pl.when(t == 1)
            def _():
                for back in range(1, GROUP):
                    @pl.when((mine + back < GROUP) | (band >= GROUP))
                    def _():
                        peer_copy(back).wait_recv()
                @pl.when((mine > 0) & (band >= GROUP))
                def _():
                    for cut in range(0, relay.shape[0], 64):
                        rows = pl.ds(cut, 64)
                        total = landed[GROUP - 2, rows, :].astype(jnp.float32)
                        for back in range(1, GROUP - 1):
                            total = total + jnp.where(mine + back >= GROUP, landed[back - 1, rows, :].astype(jnp.float32), 0.0)
                        relay[rows, :] = total.astype(relay.dtype)
                    down_copy(band - GROUP).start()
            @pl.when(t == 4)
            def _():
                @pl.when((mine > 0) & (band + GROUP < bands))
                def _():
                    down_copy(band + GROUP).wait_recv()
                for cut in range(0, relay.shape[0], 64):
                    rows = pl.ds(cut, 64)
                    total = jnp.where((mine > 0) & (band + GROUP < bands), from_up[rows, :].astype(jnp.float32), 0.0)
                    for back in range(1, GROUP):
                        total = total + jnp.where(mine + back < GROUP, landed[back - 1, rows, :].astype(jnp.float32), 0.0)
                    back_out[rows, :] = total
        return carry

    lax.fori_loop(0, count + depth, body, 0)

    if has_context:
        for back in range(1, GROUP):
            @pl.when((mine >= back) | (band >= GROUP))
            def _():
                peer_copy(back).wait_send()
        @pl.when((mine > 0) & (band >= GROUP))
        def _():
            down_copy(band - GROUP).wait_send()

    def drain(m, carry):
        for stage in range(depth):
            for color in range(2):
                phase, step = stages[color][stage]
                for way in range(2):
                    present, rank, index, copy = outgoing(m, color, phase, step, way)
                    @pl.when(present)
                    def _():
                        copy(own_block(m, color, phase, index)).wait_send()
        return carry

    lax.fori_loop(0, count, drain, 0)


def reduce_grads(bands, grads, returned, collective_id):
    dims = band_dims(bands)
    count, depth_rows, width = grads.shape
    rows = depth_rows // bands
    half = width // 2
    depth = len(stage_list(dims, ORDERS[0]))
    vmem = pl.BlockSpec(memory_space=pltpu.VMEM)
    anyspace = pl.BlockSpec(memory_space=pl.ANY)
    slots = lambda size: 1 if size == 2 else 2 * (size - 1)
    inner = dims[1]
    has_context = returned is not None
    grads = grads.reshape(count, *dims, rows, width)
    scratch = [
        pltpu.VMEM(grads.shape, grads.dtype),
        pltpu.SemaphoreType.DMA((count,)),
        pltpu.VMEM((count, 2, slots(inner), dims[0], inner, rows, half), grads.dtype),
        pltpu.VMEM((count, 2, slots(dims[0]), inner, rows, half), grads.dtype),
        pltpu.VMEM((count, 2, slots(inner), rows, half), grads.dtype),
        pltpu.SemaphoreType.DMA((2, depth, 2, count)),
        pltpu.SemaphoreType.DMA((2, depth, 2, count)),
    ]
    args = [grads]
    in_specs = [anyspace]
    out_shape = [jax.ShapeDtypeStruct((count, rows, width), jnp.float32)]
    if has_context:
        args.append(returned)
        in_specs.append(vmem)
        ctx_shape = returned.shape[1:]
        out_shape.append(jax.ShapeDtypeStruct(ctx_shape, jnp.float32))
        scratch += [
            pltpu.VMEM(returned.shape, returned.dtype),
            pltpu.VMEM(ctx_shape, returned.dtype),
            pltpu.VMEM(ctx_shape, returned.dtype),
            pltpu.SemaphoreType.DMA((GROUP - 1,)),
            pltpu.SemaphoreType.DMA((GROUP - 1,)),
            pltpu.SemaphoreType.DMA((2,)),
        ]
    return pl.pallas_call(
        partial(reduce_kernel, dims, has_context),
        out_shape=out_shape,
        in_specs=in_specs,
        out_specs=[vmem] * len(out_shape),
        scratch_shapes=scratch,
        compiler_params=pltpu.CompilerParams(
            collective_id=collective_id, has_side_effects=True, vmem_limit_bytes=67043328
        ),
        name="reduce_grads",
    )(*args)


def from_behind(x, axis, by):
    size = lax.axis_size(axis)
    pairs = [(i, i + by) for i in range(size) if 0 <= i + by < size]
    return lax.ppermute(x, axis, pairs)


def norm_rows(values, gain_row):
    centre = values - jnp.mean(values, axis=-1, keepdims=True)
    spread = jnp.mean(centre * centre, axis=-1, keepdims=True)
    return centre * lax.rsqrt(spread + EPS) * gain_row


def matmul(former, latter):
    return jnp.dot(former, latter, preferred_element_type=jnp.float32)


def matmul_t(former, latter):
    return lax.dot_general(
        former, latter, (((1,), (1,)), ((), ())), preferred_element_type=jnp.float32
    )


def inner_t(former, latter):
    return lax.dot_general(
        former, latter, (((0,), (0,)), ((), ())), preferred_element_type=jnp.float32
    )


def head_total(partials):
    return lax.psum(partials, "head")


def earlier_bands(key_pair):
    return [from_behind(key_pair, "band", behind) for behind in range(1, SEQ_BANDS)]


def caption_from_first(caption_pair):
    return [from_behind(caption_pair, "band", behind) for behind in range(1, SEQ_BANDS)]


def caption_back(masked_pair, behind):
    return from_behind(masked_pair.astype(jnp.bfloat16), "band", -behind).astype(masked_pair.dtype)


def log_sum(scores):
    row_max = jnp.max(scores, axis=-1, keepdims=True)
    return row_max + jnp.log(jnp.sum(jnp.exp(scores - row_max), axis=-1, keepdims=True))


def pair_scores(queries, key_block):
    return jnp.einsum("qhd,khd->hqk", queries, key_block, preferred_element_type=jnp.float32)


def pair_zero(queries, key_block):
    return jnp.zeros((queries.shape[1], queries.shape[0], key_block.shape[0]), jnp.float32)


def mix_values(weights, values):
    return jnp.einsum("hqk,khd->qhd", weights, values, preferred_element_type=jnp.float32)


def mix_nothing(weights, values):
    return jnp.zeros((weights.shape[1], values.shape[1], values.shape[2]), jnp.float32)


def spread_back(weights, rows_side):
    return jnp.einsum("hqk,qhd->khd", weights, rows_side, preferred_element_type=jnp.float32)


def spread_none(weights, rows_side):
    return jnp.zeros((weights.shape[2], rows_side.shape[1], rows_side.shape[2]), jnp.float32)


def masked_scores(queries, key_list, offset):
    score_scale = HEAD_DIM ** (-0.5)
    band_rows = queries.shape[0]
    row_ids = lax.broadcasted_iota(jnp.int32, (band_rows, band_rows), 0)
    col_ids = lax.broadcasted_iota(jnp.int32, (band_rows, band_rows), 1)
    own_scores = pair_scores(queries, key_list[0]) * score_scale
    blocks = [jnp.where((col_ids <= row_ids)[None], own_scores, NEG)]
    for behind in range(1, SEQ_BANDS):
        valid = behind <= offset
        far_block = lax.cond(valid, pair_scores, pair_zero, queries, key_list[behind]) * score_scale
        blocks.append(jnp.where(valid, far_block, NEG))
    return jnp.concatenate(blocks, axis=2)


def self_forward(queries, key_list, value_list, offset):
    band_rows = queries.shape[0]
    scores = masked_scores(queries, key_list, offset)
    log_total = log_sum(scores)
    weights = jnp.exp(scores - log_total).astype(jnp.bfloat16)
    result = mix_values(weights[:, :, :band_rows], value_list[0])
    for behind in range(1, SEQ_BANDS):
        weight_block = weights[:, :, behind * band_rows : (behind + 1) * band_rows]
        result = result + lax.cond(
            behind <= offset, mix_values, mix_nothing, weight_block, value_list[behind]
        )
    return (result.astype(jnp.bfloat16), log_total)


def self_backward(queries, key_list, value_list, offset, log_total, grad_out):
    score_scale = HEAD_DIM ** (-0.5)
    band_rows = queries.shape[0]
    probs_full = jnp.exp(masked_scores(queries, key_list, offset) - log_total)
    probs_low = probs_full.astype(jnp.bfloat16)
    grad_blocks = [pair_scores(grad_out, value_list[0])]
    for behind in range(1, SEQ_BANDS):
        grad_blocks.append(
            lax.cond(behind <= offset, pair_scores, pair_zero, grad_out, value_list[behind])
        )
    grad_probs = jnp.concatenate(grad_blocks, axis=2)
    centred = grad_probs - jnp.sum(grad_probs * probs_full, axis=-1, keepdims=True)
    grad_scores = (probs_full * centred).astype(jnp.bfloat16)
    grad_query = mix_values(grad_scores[:, :, :band_rows], key_list[0])
    key_grads = [spread_back(grad_scores[:, :, :band_rows], queries) * score_scale]
    value_grads = [spread_back(probs_low[:, :, :band_rows], grad_out)]
    for behind in range(1, SEQ_BANDS):
        valid = behind <= offset
        score_block = grad_scores[:, :, behind * band_rows : (behind + 1) * band_rows]
        prob_block = probs_low[:, :, behind * band_rows : (behind + 1) * band_rows]
        grad_query = grad_query + lax.cond(
            valid, mix_values, mix_nothing, score_block, key_list[behind]
        )
        key_grads.append(
            lax.cond(valid, spread_back, spread_none, score_block, queries) * score_scale
        )
        value_grads.append(lax.cond(valid, spread_back, spread_none, prob_block, grad_out))
    return (grad_query * score_scale, key_grads, value_grads)


def adamw_update(weight, moment_one, moment_two, gradient, step_rate, decay_rate):
    moment_one_new = BETA_ONE * moment_one + (1.0 - BETA_ONE) * gradient
    moment_two_new = BETA_TWO * moment_two + (1.0 - BETA_TWO) * gradient * gradient
    unbiased_one = moment_one_new / (1.0 - BETA_ONE**STEP)
    unbiased_two = moment_two_new / (1.0 - BETA_TWO**STEP)
    weight_new = weight - step_rate * (
        unbiased_one / (jnp.sqrt(unbiased_two) + ADAM_EPS) + decay_rate * weight
    )
    return (weight_new, moment_one_new, moment_two_new)


def local(
    tokens,
    text_states,
    cotangent,
    earlier,
    proj_master,
    out_master,
    mlp_master,
    gain_master,
    proj_first,
    proj_second,
    out_first,
    out_second,
    mlp_first,
    mlp_second,
    gain_first,
    gain_second,
):
    streams, band_rows, model_width = tokens.shape
    row_count = streams * band_rows
    text_rows = text_states.shape[1]
    proj_low = proj_master.astype(jnp.bfloat16)
    out_low = out_master.astype(jnp.bfloat16)
    mlp_low = mlp_master.astype(jnp.bfloat16)
    gain_low = gain_master.astype(jnp.bfloat16)
    bands = lax.axis_size("band")
    shard_rows, width = proj_low.shape[1:]
    chunks = mlp_low.shape[2] // width
    mlp_cut = mlp_low.reshape(2, shard_rows, chunks, width).transpose(0, 2, 1, 3)
    shard = jnp.concatenate([proj_low, out_low, mlp_cut.reshape(2 * chunks, shard_rows, width)])
    gain_tile = jnp.pad(gain_low.astype(jnp.float32), ((0, 5), (0, 128 - shard_rows)))
    gathered, gain_tiles = gather_weights(bands, shard, gain_tile, None, 1)
    gathered = gathered.reshape(shard.shape[0], model_width, width)
    proj_w, out_w = gathered[:6], gathered[6:8]
    mlp_w = gathered[8:].reshape(2, chunks, model_width, width).transpose(0, 2, 1, 3)
    mlp_w = mlp_w.reshape(2, model_width, chunks * width)
    gains = gain_tiles.reshape(bands, 8, 128)[:, :3, :shard_rows].transpose(1, 0, 2).reshape(3, model_width)
    local_width = proj_w.shape[2]
    local_heads = local_width // HEAD_DIM
    score_scale = HEAD_DIM ** (-0.5)
    head_shape = (streams, band_rows, local_heads, HEAD_DIM)
    text_shape = (streams, text_rows, local_heads, HEAD_DIM)
    offsets = earlier[:, 0]
    inputs = tokens.astype(jnp.float32).reshape(row_count, model_width)
    normed_one = norm_rows(inputs, gains[0]).astype(jnp.bfloat16)
    queries = matmul(normed_one, proj_w[0]).astype(jnp.bfloat16).reshape(head_shape)
    key_rows = matmul(normed_one, proj_w[1]).astype(jnp.bfloat16)
    value_rows = matmul(normed_one, proj_w[2]).astype(jnp.bfloat16)
    own_pair = jnp.stack([key_rows.reshape(head_shape), value_rows.reshape(head_shape)])
    pair_list = [own_pair] + earlier_bands(own_pair)
    attended_list = []
    total_list = []
    for stream in range(streams):
        offset = earlier[stream, 0]
        result, log_total = self_forward(
            queries[stream],
            [neighbour[0, stream] for neighbour in pair_list],
            [neighbour[1, stream] for neighbour in pair_list],
            offset,
        )
        attended_list.append(result)
        total_list.append(log_total)
    attended = jnp.stack(attended_list).reshape(row_count, local_width)
    hidden_one = inputs + head_total(matmul_t(attended, out_w[0]))
    normed_two = norm_rows(hidden_one, gains[1]).astype(jnp.bfloat16)
    cross_queries = matmul(normed_two, proj_w[3]).astype(jnp.bfloat16).reshape(head_shape)
    text_flat = text_states.reshape(streams * text_rows, model_width)
    slot_keys = matmul(text_flat, proj_w[4]).astype(jnp.bfloat16).reshape(text_shape)
    slot_values = matmul(text_flat, proj_w[5]).astype(jnp.bfloat16).reshape(text_shape)
    caption_pair = jnp.stack([slot_keys, slot_values])
    moved_list = caption_from_first(caption_pair)
    chosen = caption_pair
    for behind in range(1, SEQ_BANDS):
        chosen = jnp.where(
            (offsets == behind)[None, :, None, None, None], moved_list[behind - 1], chosen
        )
    cross_keys = chosen[0]
    cross_values = chosen[1]
    cross_scores = (
        jnp.einsum("sqhd,skhd->shqk", cross_queries, cross_keys, preferred_element_type=jnp.float32)
        * score_scale
    )
    cross_probs = jnp.exp(cross_scores - log_sum(cross_scores))
    cross_low = cross_probs.astype(jnp.bfloat16)
    crossed = (
        jnp.einsum("shqk,skhd->sqhd", cross_low, cross_values, preferred_element_type=jnp.float32)
        .astype(jnp.bfloat16)
        .reshape(row_count, local_width)
    )
    hidden_two = hidden_one + head_total(matmul_t(crossed, out_w[1]))
    normed_three = norm_rows(hidden_two, gains[2]).astype(jnp.bfloat16)
    before = matmul(normed_three, mlp_w[0])
    activated = jax.nn.gelu(before, approximate=False).astype(jnp.bfloat16)
    block_out = (
        (hidden_two + head_total(matmul_t(activated, mlp_w[1])))
        .astype(jnp.bfloat16)
        .reshape(streams, band_rows, model_width)
    )
    incoming = cotangent.astype(jnp.float32).reshape(row_count, model_width)
    incoming_low = cotangent.reshape(row_count, model_width)
    grad_down = inner_t(incoming_low, activated)
    grad_act = matmul(incoming_low, mlp_w[1])
    _, gelu_pull = jax.vjp(partial(jax.nn.gelu, approximate=False), before)
    grad_before = gelu_pull(grad_act)[0].astype(jnp.bfloat16)
    grad_up = inner_t(normed_three, grad_before)
    mlp_grad_local = jnp.stack([grad_up, grad_down])
    grad_normed_three = head_total(matmul_t(grad_before, mlp_w[0]))
    _, pull_three = jax.vjp(norm_rows, hidden_two, gains[2])
    back_two, gain_grad_three = pull_three(grad_normed_three)
    grad_two = incoming + back_two
    grad_two_low = grad_two.astype(jnp.bfloat16)
    grad_cross_out = inner_t(grad_two_low, crossed)
    grad_crossed = matmul(grad_two_low, out_w[1]).astype(jnp.bfloat16).reshape(head_shape)
    cross_dp = jnp.einsum(
        "sqhd,skhd->shqk", grad_crossed, cross_values, preferred_element_type=jnp.float32
    )
    cross_ds = (
        cross_probs * (cross_dp - jnp.sum(cross_dp * cross_probs, axis=-1, keepdims=True))
    ).astype(jnp.bfloat16)
    grad_cq = (
        (
            jnp.einsum("shqk,skhd->sqhd", cross_ds, cross_keys, preferred_element_type=jnp.float32)
            * score_scale
        )
        .astype(jnp.bfloat16)
        .reshape(row_count, local_width)
    )
    key_part = (
        jnp.einsum("shqk,sqhd->skhd", cross_ds, cross_queries, preferred_element_type=jnp.float32)
        * score_scale
    )
    value_part = jnp.einsum(
        "shqk,sqhd->skhd", cross_low, grad_crossed, preferred_element_type=jnp.float32
    )
    grad_caption = jnp.stack([key_part, value_part])
    caption_total = jnp.where((offsets == 0)[None, :, None, None, None], grad_caption, 0.0)
    for behind in range(1, SEQ_BANDS):
        masked_pair = jnp.where((offsets == behind)[None, :, None, None, None], grad_caption, 0.0)
        caption_total = caption_total + caption_back(masked_pair, behind)
    grad_ck = caption_total[0].astype(jnp.bfloat16).reshape(streams * text_rows, local_width)
    grad_cv = caption_total[1].astype(jnp.bfloat16).reshape(streams * text_rows, local_width)
    text_partial = matmul_t(grad_ck, proj_w[4]) + matmul_t(grad_cv, proj_w[5])
    grad_normed_two, grad_text = head_total((matmul_t(grad_cq, proj_w[3]), text_partial))
    _, pull_two = jax.vjp(norm_rows, hidden_one, gains[1])
    back_one, gain_grad_two = pull_two(grad_normed_two)
    grad_one = grad_two + back_one
    grad_one_low = grad_one.astype(jnp.bfloat16)
    grad_self_out = inner_t(grad_one_low, attended)
    grad_attended = matmul(grad_one_low, out_w[0]).astype(jnp.bfloat16).reshape(head_shape)
    query_grads = []
    key_grads = []
    value_grads = []
    for stream in range(streams):
        offset = earlier[stream, 0]
        grad_query, key_blocks, value_blocks = self_backward(
            queries[stream],
            [neighbour[0, stream] for neighbour in pair_list],
            [neighbour[1, stream] for neighbour in pair_list],
            offset,
            total_list[stream],
            grad_attended[stream],
        )
        query_grads.append(grad_query)
        key_grads.append(key_blocks)
        value_grads.append(value_blocks)
    grad_pairs = [
        jnp.stack(
            [
                jnp.stack([key_grads[stream][behind] for stream in range(streams)]),
                jnp.stack([value_grads[stream][behind] for stream in range(streams)]),
            ]
        )
        for behind in range(SEQ_BANDS)
    ]
    pair_total = grad_pairs[0]
    for behind in range(1, SEQ_BANDS):
        pair_total = pair_total + from_behind(
            grad_pairs[behind].astype(jnp.bfloat16), "band", -behind
        ).astype(jnp.float32)
    grad_queries = jnp.stack(query_grads).astype(jnp.bfloat16).reshape(row_count, local_width)
    grad_keys = pair_total[0].astype(jnp.bfloat16).reshape(row_count, local_width)
    grad_values = pair_total[1].astype(jnp.bfloat16).reshape(row_count, local_width)
    proj_grad_local = jnp.stack(
        [
            inner_t(normed_one, grad_queries),
            inner_t(normed_one, grad_keys),
            inner_t(normed_one, grad_values),
            inner_t(normed_two, grad_cq),
            inner_t(text_flat, grad_ck),
            inner_t(text_flat, grad_cv),
        ]
    )
    norm_partial = (
        matmul_t(grad_queries, proj_w[0])
        + matmul_t(grad_keys, proj_w[1])
        + matmul_t(grad_values, proj_w[2])
    )
    grad_normed_one = head_total(norm_partial)
    _, pull_one = jax.vjp(norm_rows, inputs, gains[0])
    back_zero, gain_grad_one = pull_one(grad_normed_one)
    grad_tokens = (grad_one + back_zero).reshape(streams, band_rows, model_width)
    out_grad_local = jnp.stack([grad_self_out, grad_cross_out])
    gain_grad_local = jnp.stack([gain_grad_one, gain_grad_two, gain_grad_three])
    mlp_parts = mlp_grad_local.astype(jnp.bfloat16).reshape(2, model_width, chunks, width).transpose(0, 2, 1, 3)
    grads = jnp.concatenate(
        [
            proj_grad_local.astype(jnp.bfloat16),
            out_grad_local.astype(jnp.bfloat16),
            mlp_parts.reshape(2 * chunks, model_width, width),
        ]
    )
    (summed,) = reduce_grads(bands, grads, None, 2)
    proj_grad, out_grad = summed[:6], summed[6:8]
    mlp_grad = summed[8:].reshape(2, chunks, shard_rows, width).transpose(0, 2, 1, 3)
    mlp_grad = mlp_grad.reshape(2, shard_rows, chunks * width)
    gain_grad = lax.psum_scatter(gain_grad_local, "band", scatter_dimension=1, tiled=True)
    local_squares = (
        jnp.sum(proj_grad * proj_grad)
        + jnp.sum(out_grad * out_grad)
        + jnp.sum(mlp_grad * mlp_grad)
        + 0.5 * jnp.sum(gain_grad * gain_grad)
    )
    grad_norm = jnp.sqrt(lax.psum(local_squares, ("band", "head")))
    factor = jnp.minimum(1.0, CLIP / grad_norm)
    matrix_rate = 2.0 * D ** (-0.5)
    new_proj = adamw_update(
        proj_master, proj_first, proj_second, proj_grad * factor, matrix_rate, DECAY
    )
    new_out = adamw_update(out_master, out_first, out_second, out_grad * factor, matrix_rate, DECAY)
    new_mlp = adamw_update(mlp_master, mlp_first, mlp_second, mlp_grad * factor, matrix_rate, DECAY)
    new_gain = adamw_update(
        gain_master, gain_first, gain_second, gain_grad * factor, GAIN_RATE, 0.0
    )
    grad_text_out = grad_text.reshape(streams, text_rows, model_width)
    return (
        block_out,
        grad_tokens,
        grad_text_out,
        grad_norm,
        new_proj[0],
        new_proj[1],
        new_proj[2],
        new_out[0],
        new_out[1],
        new_out[2],
        new_mlp[0],
        new_mlp[1],
        new_mlp[2],
        new_gain[0],
        new_gain[1],
        new_gain[2],
    )


def solution(mesh):
    return jax.shard_map(
        local,
        mesh=mesh,
        in_specs=(
            P(None, "band", None),
            P(None, "band", None),
            P(None, "band", None),
            P(None, "band"),
            P(None, "band", "head"),
            P(None, "band", "head"),
            P(None, "band", "head"),
            P(None, "band"),
            P(None, "band", "head"),
            P(None, "band", "head"),
            P(None, "band", "head"),
            P(None, "band", "head"),
            P(None, "band", "head"),
            P(None, "band", "head"),
            P(None, "band"),
            P(None, "band"),
        ),
        out_specs=(
            P(None, "band", None),
            P(None, "band", None),
            P(None, "band", None),
            P(),
            P(None, "band", "head"),
            P(None, "band", "head"),
            P(None, "band", "head"),
            P(None, "band", "head"),
            P(None, "band", "head"),
            P(None, "band", "head"),
            P(None, "band", "head"),
            P(None, "band", "head"),
            P(None, "band", "head"),
            P(None, "band"),
            P(None, "band"),
            P(None, "band"),
        ),
        check_vma=False,
    )
```

```python
from functools import partial

import jax
import jax.numpy as jnp
from jax import lax
from jax.experimental import pallas as pl
from jax.experimental.pallas import tpu as pltpu
from jax.sharding import PartitionSpec as P

D = 1024
HEAD_DIM = 64
SEQ_BANDS = 4
STEP = 10


EPS = 1e-05
NEG = -1e30
CLIP = 1.0
BETA_ONE = 0.9
BETA_TWO = 0.95
ADAM_EPS = 1e-08
DECAY = 0.1
GAIN_RATE = 0.5
LANES = 128


MESH = pl.DeviceIdType.MESH
ORDERS = ((2, 0, 1), (1, 0, 2))
GROUP = 4


def band_dims(bands):
    inner = 4 if bands >= 64 else 2
    return (bands // (inner * inner), inner, inner)


def strides_of(dims):
    return (dims[1] * dims[2], dims[2], 1)


def place_of(dims):
    band = lax.axis_index("band")
    return band, (
        band // (dims[1] * dims[2]),
        (band // dims[2]) % dims[1],
        band % dims[2],
    )


def stage_list(dims, order):
    return [(phase, step) for phase in range(3) for step in range(dims[order[phase]] - 1)]


def block_of(ref, lead, place, order, phase, index, columns):
    at = list(place)
    for done in range(phase):
        at[order[done]] = slice(None)
    at[order[phase]] = index
    return ref.at[(*lead, *at, slice(None), columns)]


def greet(dims, place, band, head, extra):
    barrier = pltpu.get_barrier_semaphore()
    strides = strides_of(dims)
    total = jnp.int32(0)
    peers = []
    for axis in range(3):
        for sign in (1, -1):
            there = place[axis] + sign
            peers.append(((there >= 0) & (there < dims[axis]), band + sign * strides[axis], head))
    peers += extra
    for present, peer_band, peer_head in peers:
        @pl.when(present)
        def _():
            pl.semaphore_signal(barrier, inc=1, device_id=(peer_band, peer_head), device_id_type=MESH)
        total = total + present.astype(jnp.int32)
    pl.semaphore_wait(barrier, total)


def gather_kernel(dims, has_context, *refs):
    if has_context:
        (w_ref, gain_ref, ctx_ref, out_ref, gains_ref, ctx_out,
         own_sem, send_sem, recv_sem, gsend, grecv, prev_ref, up_sem, csend, crecv, psend, precv) = refs
    else:
        (w_ref, gain_ref, out_ref, gains_ref, own_sem, send_sem, recv_sem, gsend, grecv) = refs
    band, place = place_of(dims)
    head = lax.axis_index("head")
    strides = strides_of(dims)
    count = w_ref.shape[0]
    half = w_ref.shape[2] // 2
    bands = dims[0] * dims[1] * dims[2]
    true = band >= 0
    extra = []
    if has_context:
        base = (band // GROUP) * GROUP
        mine = band % GROUP
        for shift in range(1, GROUP):
            extra.append((true, base + (mine + shift) % GROUP, head))
        extra.append((band + GROUP < bands, band + GROUP, head))
        extra.append((band >= GROUP, band - GROUP, head))
        extra.append((true, band, 1 - head))
    greet(dims, place, band, head, extra)

    own = [
        pltpu.make_async_copy(w_ref, out_ref.at[:, place[0], place[1], place[2]], own_sem.at[0]),
        pltpu.make_async_copy(gain_ref, gains_ref.at[place[0], place[1], place[2]], own_sem.at[1]),
    ]
    for copy in own:
        copy.start()

    def up_copy():
        return pltpu.make_async_remote_copy(
            ctx_ref, prev_ref, up_sem.at[0], up_sem.at[1], device_id=(band + GROUP, head), device_id_type=MESH
        )

    def peer_copy(back, source):
        return pltpu.make_async_remote_copy(
            source, ctx_out.at[head, back - 1], csend.at[back - 1], crecv.at[back - 1],
            device_id=(base + (mine + back) % GROUP, head), device_id_type=MESH,
        )

    def pair_copy(back):
        return pltpu.make_async_remote_copy(
            ctx_out.at[head, back - 1], ctx_out.at[head, back - 1], psend.at[back - 1], precv.at[back - 1],
            device_id=(band, 1 - head), device_id_type=MESH,
        )

    if has_context:
        @pl.when(band + GROUP < bands)
        def _():
            up_copy().start()
        for back in range(1, GROUP):
            @pl.when(mine + back < GROUP)
            def _():
                peer_copy(back, ctx_ref).start()

    def piece(color, m, phase, step, way, incoming):
        order = ORDERS[color]
        axis = order[phase]
        size, at = dims[axis], place[axis]
        toward = 1 if way == 0 else -1
        stage = stage_list(dims, order).index((phase, step))
        if incoming:
            index = at - toward * (step + 1)
            present = (index >= 0) & (index < size)
        else:
            index = at - toward * step
            present = (index >= 0) & (index < size) & (at + toward >= 0) & (at + toward < size)
        columns = pl.ds(color * half, half)
        target = (band + toward * strides[axis], head)
        land = block_of(out_ref, (m,), place, order, phase, index, columns)
        source = w_ref.at[m, :, columns] if stage == 0 else land
        copy = pltpu.make_async_remote_copy(
            source, land, send_sem.at[color, stage, way, m], recv_sem.at[color, stage, way, m],
            device_id=target, device_id_type=MESH,
        )
        return present, copy

    def gain_piece(phase, step, way, incoming):
        order = ORDERS[0]
        axis = order[phase]
        size, at = dims[axis], place[axis]
        toward = 1 if way == 0 else -1
        stage = stage_list(dims, order).index((phase, step))
        if incoming:
            index = at - toward * (step + 1)
            present = (index >= 0) & (index < size)
        else:
            index = at - toward * step
            present = (index >= 0) & (index < size) & (at + toward >= 0) & (at + toward < size)
        land = block_of(gains_ref, (), place, order, phase, index, slice(None))
        source = gain_ref if stage == 0 else land
        copy = pltpu.make_async_remote_copy(
            source, land, gsend.at[stage, way], grecv.at[stage, way],
            device_id=(band + toward * strides[axis], head), device_id_type=MESH,
        )
        return present, copy

    stages = [stage_list(dims, order) for order in ORDERS]
    depth = len(stages[0])

    def context_step(t):
        @pl.when(t == 1)
        def _():
            @pl.when(band >= GROUP)
            def _():
                pltpu.make_async_remote_copy(
                    ctx_ref, prev_ref, up_sem.at[0], up_sem.at[1], device_id=(band - GROUP, head), device_id_type=MESH
                ).wait_recv()
            for back in range(1, GROUP):
                @pl.when((mine + back >= GROUP) & (band >= GROUP))
                def _():
                    peer_copy(back, prev_ref).start()
        @pl.when(t == 4)
        def _():
            for back in range(1, GROUP):
                @pl.when((mine >= back) | (band >= GROUP))
                def _():
                    peer_copy(back, ctx_ref).wait_recv()
                    pair_copy(back).start()

    def gains_step(t):
        for stage in range(depth + 1):
            @pl.when(t == stage)
            def _():
                if stage == 1:
                    for copy in own:
                        copy.wait()
                if stage > 0:
                    for way in range(2):
                        present, copy = gain_piece(*stages[0][stage - 1], way, True)
                        @pl.when(present)
                        def _():
                            copy.wait_recv()
                if stage < depth:
                    for way in range(2):
                        present, copy = gain_piece(*stages[0][stage], way, False)
                        @pl.when(present)
                        def _():
                            copy.start()

    def body(t, carry):
        gains_step(t)
        if has_context:
            context_step(t)
        for stage in range(depth, -1, -1):
            m = t - stage
            @pl.when((m >= 0) & (m < count))
            def _():
                for color in range(2):
                    if stage > 0:
                        for way in range(2):
                            present, copy = piece(color, m, *stages[color][stage - 1], way, True)
                            @pl.when(present)
                            def _():
                                copy.wait_recv()
                    if stage < depth:
                        for way in range(2):
                            present, copy = piece(color, m, *stages[color][stage], way, False)
                            @pl.when(present)
                            def _():
                                copy.start()
        return carry

    lax.fori_loop(0, count + depth, body, 0)

    if has_context:
        for back in range(1, GROUP):
            @pl.when((mine >= back) | (band >= GROUP))
            def _():
                pltpu.make_async_remote_copy(
                    ctx_out.at[1 - head, back - 1], ctx_out.at[1 - head, back - 1], psend.at[back - 1],
                    precv.at[back - 1], device_id=(band, 1 - head), device_id_type=MESH,
                ).wait_recv()
                pair_copy(back).wait_send()
            @pl.when((mine + back < GROUP) | (band >= GROUP))
            def _():
                peer_copy(back, ctx_ref).wait_send()
        @pl.when(band + GROUP < bands)
        def _():
            up_copy().wait_send()

    for stage in range(depth):
        for way in range(2):
            present, copy = gain_piece(*stages[0][stage], way, False)
            @pl.when(present)
            def _():
                copy.wait_send()

    def drain(m, carry):
        for stage in range(depth):
            for color in range(2):
                for way in range(2):
                    present, copy = piece(color, m, *stages[color][stage], way, False)
                    @pl.when(present)
                    def _():
                        copy.wait_send()
        return carry

    lax.fori_loop(0, count, drain, 0)


def gather_weights(bands, shard, gain_tile, context, collective_id):
    dims = band_dims(bands)
    count, rows, width = shard.shape
    depth = len(stage_list(dims, ORDERS[0]))
    vmem = pl.BlockSpec(memory_space=pltpu.VMEM)
    anyspace = pl.BlockSpec(memory_space=pl.ANY)
    has_context = context is not None
    out_shape = [
        jax.ShapeDtypeStruct((count, *dims, rows, width), shard.dtype),
        jax.ShapeDtypeStruct((*dims, *gain_tile.shape), gain_tile.dtype),
    ]
    scratch = [
        pltpu.SemaphoreType.DMA((2,)),
        pltpu.SemaphoreType.DMA((2, depth, 2, count)),
        pltpu.SemaphoreType.DMA((2, depth, 2, count)),
        pltpu.SemaphoreType.DMA((depth, 2)),
        pltpu.SemaphoreType.DMA((depth, 2)),
    ]
    args = [shard, gain_tile]
    if has_context:
        args.append(context)
        out_shape.append(jax.ShapeDtypeStruct((2, GROUP - 1, *context.shape), context.dtype))
        scratch += [
            pltpu.VMEM(context.shape, context.dtype),
            pltpu.SemaphoreType.DMA((2,)),
            pltpu.SemaphoreType.DMA((GROUP - 1,)),
            pltpu.SemaphoreType.DMA((GROUP - 1,)),
            pltpu.SemaphoreType.DMA((GROUP - 1,)),
            pltpu.SemaphoreType.DMA((GROUP - 1,)),
        ]
    return pl.pallas_call(
        partial(gather_kernel, dims, has_context),
        out_shape=out_shape,
        in_specs=[vmem] * len(args),
        out_specs=[anyspace] * len(out_shape),
        scratch_shapes=scratch,
        compiler_params=pltpu.CompilerParams(collective_id=collective_id, has_side_effects=True),
        name="gather_weights",
    )(*args)


def reduce_kernel(dims, has_context, *refs):
    if has_context:
        (g_ref, back_ref, out_ref, back_out, gv, load_sem, last_ref, mid_ref, first_ref, send_sem, recv_sem,
         landed, relay, from_up, csend, crecv, up_sem) = refs
    else:
        (g_ref, out_ref, gv, load_sem, last_ref, mid_ref, first_ref, send_sem, recv_sem) = refs
    band, place = place_of(dims)
    head = lax.axis_index("head")
    strides = strides_of(dims)
    count = g_ref.shape[0]
    half = g_ref.shape[-1] // 2
    bands = dims[0] * dims[1] * dims[2]
    true = band >= 0
    orders = tuple(order[::-1] for order in ORDERS)
    lands = (last_ref, mid_ref, first_ref)

    def load(m):
        return pltpu.make_async_copy(g_ref.at[m], gv.at[m], load_sem.at[m])

    def load_all(m, carry):
        load(m).start()
        return carry

    lax.fori_loop(0, count, load_all, 0)

    extra = []
    if has_context:
        base = (band // GROUP) * GROUP
        mine = band % GROUP
        for shift in range(1, GROUP):
            extra.append((true, base + (mine + shift) % GROUP, head))
        extra.append((band + GROUP < bands, band + GROUP, head))
        extra.append((band >= GROUP, band - GROUP, head))
    greet(dims, place, band, head, extra)

    def peer_copy(back):
        return pltpu.make_async_remote_copy(
            back_ref.at[back - 1], landed.at[back - 1], csend.at[back - 1], crecv.at[back - 1],
            device_id=(base + (mine + GROUP - back) % GROUP, head), device_id_type=MESH,
        )

    def down_copy(target):
        return pltpu.make_async_remote_copy(
            relay, from_up, up_sem.at[0], up_sem.at[1], device_id=(target, head), device_id_type=MESH
        )

    if has_context:
        for back in range(1, GROUP):
            @pl.when((mine >= back) | (band >= GROUP))
            def _():
                peer_copy(back).start()

    def slot(size, step, way):
        return 0 if size == 2 else step * 2 + way

    def own_block(m, color, phase, index):
        order = orders[color]
        at = list(place)
        for later in range(phase + 1, 3):
            at[order[later]] = slice(None)
        at[order[phase]] = index
        return gv.at[(m, *at, slice(None), pl.ds(color * half, half))]

    def landing(m, color, phase, step, way):
        size = dims[orders[color][phase]]
        return lands[phase].at[m, color, slot(size, step, way)]

    def outgoing(m, color, phase, step, way):
        axis = orders[color][phase]
        size, at = dims[axis], place[axis]
        toward = 1 if way == 0 else -1
        rank = at if way == 0 else size - 1 - at
        index = size - 1 - step + at if way == 0 else step + at - (size - 1)
        present = (rank <= step) & (at + toward >= 0) & (at + toward < size)
        stage = stage_list(dims, orders[color]).index((phase, step))
        target = (band + toward * strides[axis], head)

        def copy(source):
            return pltpu.make_async_remote_copy(
                source, landing(m, color, phase, step, way),
                send_sem.at[color, stage, way, m], recv_sem.at[color, stage, way, m],
                device_id=target, device_id_type=MESH,
            )

        return present, rank, index, copy

    def arrived(m, color, phase, step, way):
        axis = orders[color][phase]
        size, at = dims[axis], place[axis]
        before = at - 1 if way == 0 else at + 1
        rank = before if way == 0 else size - 1 - before
        present = (before >= 0) & (before < size) & (rank <= step)
        _, _, _, copy = outgoing(m, color, phase, step, way)
        return present, copy(landing(m, color, phase, step, way))

    def add_into(target, source):
        lead = target.shape[:-2]
        if len(lead) == 0:
            target[...] = target[...] + source[...]
        elif len(lead) == 1:
            for i in range(lead[0]):
                target[i] = target[i] + source[i]
        else:
            for i in range(lead[0]):
                for j in range(lead[1]):
                    target[i, j] = target[i, j] + source[i, j]

    stages = [stage_list(dims, order) for order in orders]
    depth = len(stages[0])

    def send(m, color, phase, step):
        axis = orders[color][phase]
        size = dims[axis]
        for way in range(2):
            present, rank, index, copy = outgoing(m, color, phase, step, way)
            @pl.when(present & (rank == 0))
            def _():
                copy(own_block(m, color, phase, index)).start()
            if step > 0:
                @pl.when(present & (rank > 0))
                def _():
                    from_before = landing(m, color, phase, step - 1, way)
                    add_into(from_before, own_block(m, color, phase, index))
                    copy(from_before).start()

    def settle(m, color, phase, step):
        axis = orders[color][phase]
        size = dims[axis]
        for way in range(2):
            present, copy = arrived(m, color, phase, step, way)
            @pl.when(present)
            def _():
                copy.wait_recv()
                if step == size - 2:
                    landed_here = landing(m, color, phase, step, way)
                    if phase < 2:
                        add_into(own_block(m, color, phase, place[axis]), landed_here)
                    else:
                        columns = pl.ds(color * half, half)
                        if size == 2:
                            own = own_block(m, color, phase, place[axis])
                            out_ref[m, :, columns] = own[...].astype(jnp.float32) + landed_here[...].astype(jnp.float32)
                        else:
                            add_into(own_block(m, color, phase, place[axis]), landed_here)
        if phase == 2 and step == size - 2 and size > 2:
            columns = pl.ds(color * half, half)
            out_ref[m, :, columns] = own_block(m, color, phase, place[axis])[...].astype(jnp.float32)

    def body(t, carry):
        for stage in range(depth, -1, -1):
            m = t - stage
            @pl.when((m >= 0) & (m < count))
            def _():
                if stage == 0:
                    load(m).wait()
                for color in range(2):
                    if stage > 0:
                        settle(m, color, *stages[color][stage - 1])
                    if stage < depth:
                        send(m, color, *stages[color][stage])
        if has_context:
            @pl.when(t == 1)
            def _():
                for back in range(1, GROUP):
                    @pl.when((mine + back < GROUP) | (band >= GROUP))
                    def _():
                        peer_copy(back).wait_recv()
                @pl.when((mine > 0) & (band >= GROUP))
                def _():
                    for cut in range(0, relay.shape[0], 64):
                        rows = pl.ds(cut, 64)
                        total = landed[GROUP - 2, rows, :].astype(jnp.float32)
                        for back in range(1, GROUP - 1):
                            total = total + jnp.where(mine + back >= GROUP, landed[back - 1, rows, :].astype(jnp.float32), 0.0)
                        relay[rows, :] = total.astype(relay.dtype)
                    down_copy(band - GROUP).start()
            @pl.when(t == 4)
            def _():
                @pl.when((mine > 0) & (band + GROUP < bands))
                def _():
                    down_copy(band + GROUP).wait_recv()
                for cut in range(0, relay.shape[0], 64):
                    rows = pl.ds(cut, 64)
                    total = jnp.where((mine > 0) & (band + GROUP < bands), from_up[rows, :].astype(jnp.float32), 0.0)
                    for back in range(1, GROUP):
                        total = total + jnp.where(mine + back < GROUP, landed[back - 1, rows, :].astype(jnp.float32), 0.0)
                    back_out[rows, :] = total
        return carry

    lax.fori_loop(0, count + depth, body, 0)

    if has_context:
        for back in range(1, GROUP):
            @pl.when((mine >= back) | (band >= GROUP))
            def _():
                peer_copy(back).wait_send()
        @pl.when((mine > 0) & (band >= GROUP))
        def _():
            down_copy(band - GROUP).wait_send()

    def drain(m, carry):
        for stage in range(depth):
            for color in range(2):
                phase, step = stages[color][stage]
                for way in range(2):
                    present, rank, index, copy = outgoing(m, color, phase, step, way)
                    @pl.when(present)
                    def _():
                        copy(own_block(m, color, phase, index)).wait_send()
        return carry

    lax.fori_loop(0, count, drain, 0)


def reduce_grads(bands, grads, returned, collective_id):
    dims = band_dims(bands)
    count, depth_rows, width = grads.shape
    rows = depth_rows // bands
    half = width // 2
    depth = len(stage_list(dims, ORDERS[0]))
    vmem = pl.BlockSpec(memory_space=pltpu.VMEM)
    anyspace = pl.BlockSpec(memory_space=pl.ANY)
    slots = lambda size: 1 if size == 2 else 2 * (size - 1)
    inner = dims[1]
    has_context = returned is not None
    grads = grads.reshape(count, *dims, rows, width)
    scratch = [
        pltpu.VMEM(grads.shape, grads.dtype),
        pltpu.SemaphoreType.DMA((count,)),
        pltpu.VMEM((count, 2, slots(inner), dims[0], inner, rows, half), grads.dtype),
        pltpu.VMEM((count, 2, slots(dims[0]), inner, rows, half), grads.dtype),
        pltpu.VMEM((count, 2, slots(inner), rows, half), grads.dtype),
        pltpu.SemaphoreType.DMA((2, depth, 2, count)),
        pltpu.SemaphoreType.DMA((2, depth, 2, count)),
    ]
    args = [grads]
    in_specs = [anyspace]
    out_shape = [jax.ShapeDtypeStruct((count, rows, width), jnp.float32)]
    if has_context:
        args.append(returned)
        in_specs.append(vmem)
        ctx_shape = returned.shape[1:]
        out_shape.append(jax.ShapeDtypeStruct(ctx_shape, jnp.float32))
        scratch += [
            pltpu.VMEM(returned.shape, returned.dtype),
            pltpu.VMEM(ctx_shape, returned.dtype),
            pltpu.VMEM(ctx_shape, returned.dtype),
            pltpu.SemaphoreType.DMA((GROUP - 1,)),
            pltpu.SemaphoreType.DMA((GROUP - 1,)),
            pltpu.SemaphoreType.DMA((2,)),
        ]
    return pl.pallas_call(
        partial(reduce_kernel, dims, has_context),
        out_shape=out_shape,
        in_specs=in_specs,
        out_specs=[vmem] * len(out_shape),
        scratch_shapes=scratch,
        compiler_params=pltpu.CompilerParams(
            collective_id=collective_id, has_side_effects=True, vmem_limit_bytes=67043328
        ),
        name="reduce_grads",
    )(*args)


def norm_rows(values, gain_row):
    centre = values - jnp.mean(values, axis=-1, keepdims=True)
    spread = jnp.mean(centre * centre, axis=-1, keepdims=True)
    return centre * lax.rsqrt(spread + EPS) * gain_row


def matmul(former, latter):
    return jnp.dot(former, latter, preferred_element_type=jnp.float32)


def matmul_t(former, latter):
    return lax.dot_general(
        former, latter, (((1,), (1,)), ((), ())), preferred_element_type=jnp.float32
    )


def inner_t(former, latter):
    return lax.dot_general(
        former, latter, (((0,), (0,)), ((), ())), preferred_element_type=jnp.float32
    )


def heads_of(block):
    lane = lax.broadcasted_iota(jnp.int32, block.shape, 1) // HEAD_DIM
    return [
        block * (lane == one).astype(jnp.float32).astype(block.dtype) for one in range(LANES // HEAD_DIM)
    ]


def shifted(scores, causal, behind):
    if not causal or behind > 0:
        return scores
    key_ids = lax.broadcasted_iota(jnp.int32, scores.shape, 0)
    query_ids = lax.broadcasted_iota(jnp.int32, scores.shape, 1)
    return jnp.where(key_ids <= query_ids, scores, NEG)


def attend_body(reach, causal, q_ref, k_ref, v_ref, out_ref, total_ref):
    scale = HEAD_DIM**-0.5
    values_t = [v_ref[behind].T for behind in range(reach)]
    outs = []
    for one, q_one in enumerate(heads_of(q_ref[...])):
        scores = [shifted(matmul_t(k_ref[behind], q_one) * scale, causal, behind) for behind in range(reach)]
        top = jnp.max(scores[0], axis=0, keepdims=True)
        for block in scores[1:]:
            top = jnp.maximum(top, jnp.max(block, axis=0, keepdims=True))
        raised = [jnp.exp(block - top) for block in scores]
        total = jnp.sum(raised[0], axis=0, keepdims=True)
        for block in raised[1:]:
            total = total + jnp.sum(block, axis=0, keepdims=True)
        share = 1.0 / total
        mixed = None
        for behind in range(reach):
            part = matmul(values_t[behind], (raised[behind] * share).astype(jnp.bfloat16))
            mixed = part if mixed is None else mixed + part
        outs.append(mixed[one * HEAD_DIM : (one + 1) * HEAD_DIM])
        total_ref[one : one + 1, :] = top + jnp.log(total)
    out_ref[...] = jnp.concatenate(outs, axis=0).T.astype(jnp.bfloat16)


def attend_back_body(reach, causal, q_ref, k_ref, v_ref, total_ref, g_ref, dq_ref, dk_ref, dv_ref):
    scale = HEAD_DIM**-0.5
    keys_t = [k_ref[behind].T for behind in range(reach)]
    q_heads, g_heads = heads_of(q_ref[...]), heads_of(g_ref[...])
    query_grads = []
    key_grads, value_grads = [None] * reach, [None] * reach
    for one in range(len(q_heads)):
        q_one, g_one = q_heads[one], g_heads[one]
        log_total = total_ref[one : one + 1, :]
        probs, grads, centre = [], [], None
        for behind in range(reach):
            scores = shifted(matmul_t(k_ref[behind], q_one) * scale, causal, behind)
            probs.append(jnp.exp(scores - log_total))
            grads.append(matmul_t(v_ref[behind], g_one))
            part = jnp.sum(grads[-1] * probs[-1], axis=0, keepdims=True)
            centre = part if centre is None else centre + part
        query_grad = None
        for behind in range(reach):
            grad_scores = (probs[behind] * (grads[behind] - centre)).astype(jnp.bfloat16)
            part = matmul(keys_t[behind], grad_scores)
            query_grad = part if query_grad is None else query_grad + part
            key_part = matmul(grad_scores, q_one)
            value_part = matmul(probs[behind].astype(jnp.bfloat16), g_one)
            key_grads[behind] = key_part if one == 0 else key_grads[behind] + key_part
            value_grads[behind] = value_part if one == 0 else value_grads[behind] + value_part
        query_grads.append(query_grad[one * HEAD_DIM : (one + 1) * HEAD_DIM])
    dq_ref[...] = (jnp.concatenate(query_grads, axis=0).T * scale).astype(jnp.bfloat16)
    for behind in range(dk_ref.shape[0]):
        if behind < reach:
            dk_ref[behind] = (key_grads[behind] * scale).astype(jnp.bfloat16)
            dv_ref[behind] = value_grads[behind].astype(jnp.bfloat16)
        else:
            dk_ref[behind] = jnp.zeros(dk_ref.shape[1:], dk_ref.dtype)
            dv_ref[behind] = jnp.zeros(dv_ref.shape[1:], dv_ref.dtype)


def by_offset(body, causal, offset_ref, *refs):
    reaches = refs[1].shape[0]
    if reaches == 1:
        body(1, causal, *refs)
        return
    offset = offset_ref[pl.program_id(0)]
    for earlier_bands in range(reaches):
        @pl.when(offset == earlier_bands)
        def _():
            body(earlier_bands + 1, causal, *refs)


def attention_specs(queries, keys):
    rows, reaches, key_rows = queries.shape[1], keys.shape[1], keys.shape[2]
    row_spec = pl.BlockSpec((None, rows, LANES), lambda stream, pair: (stream, 0, pair))
    key_spec = pl.BlockSpec((None, reaches, key_rows, LANES), lambda stream, pair: (stream, 0, 0, pair))
    total_spec = pl.BlockSpec((None, None, 8, rows), lambda stream, pair: (stream, pair, 0, 0))
    return row_spec, key_spec, total_spec


def attention(queries, keys, values, offsets, causal):
    streams, rows, width = queries.shape
    row_spec, key_spec, total_spec = attention_specs(queries, keys)
    return pl.pallas_call(
        partial(by_offset, attend_body, causal),
        grid=(streams, width // LANES),
        in_specs=[pl.BlockSpec(memory_space=pltpu.SMEM), row_spec, key_spec, key_spec],
        out_specs=[row_spec, total_spec],
        out_shape=[
            jax.ShapeDtypeStruct(queries.shape, jnp.bfloat16),
            jax.ShapeDtypeStruct((streams, width // LANES, 8, rows), jnp.float32),
        ],
        name="attend",
    )(offsets, queries, keys, values)


def attention_back(queries, keys, values, offsets, totals, grad_out, causal):
    streams, rows, width = queries.shape
    row_spec, key_spec, total_spec = attention_specs(queries, keys)
    return pl.pallas_call(
        partial(by_offset, attend_back_body, causal),
        grid=(streams, width // LANES),
        in_specs=[pl.BlockSpec(memory_space=pltpu.SMEM), row_spec, key_spec, key_spec, total_spec, row_spec],
        out_specs=[row_spec, key_spec, key_spec],
        out_shape=[
            jax.ShapeDtypeStruct(queries.shape, jnp.bfloat16),
            jax.ShapeDtypeStruct(keys.shape, jnp.bfloat16),
            jax.ShapeDtypeStruct(keys.shape, jnp.bfloat16),
        ],
        name="attend_back",
    )(offsets, queries, keys, values, totals, grad_out)


def swap_kernel(count, *refs):
    sources, targets = refs[:count], refs[count : 2 * count]
    send_sem, recv_sem = refs[2 * count :]
    band, head = lax.axis_index("band"), lax.axis_index("head")
    barrier = pltpu.get_barrier_semaphore()
    pl.semaphore_signal(barrier, inc=1, device_id=(band, 1 - head), device_id_type=MESH)
    pl.semaphore_wait(barrier, 1)
    copies = [
        pltpu.make_async_remote_copy(
            sources[one], targets[one], send_sem.at[one], recv_sem.at[one],
            device_id=(band, 1 - head), device_id_type=MESH,
        )
        for one in range(count)
    ]
    for copy in copies:
        copy.start()
    for copy in copies:
        copy.wait()


def swapped(collective_id, *arrays):
    vmem = pl.BlockSpec(memory_space=pltpu.VMEM)
    return pl.pallas_call(
        partial(swap_kernel, len(arrays)),
        out_shape=[jax.ShapeDtypeStruct(array.shape, array.dtype) for array in arrays],
        in_specs=[vmem] * len(arrays),
        out_specs=[vmem] * len(arrays),
        scratch_shapes=[pltpu.SemaphoreType.DMA((len(arrays),)), pltpu.SemaphoreType.DMA((len(arrays),))],
        compiler_params=pltpu.CompilerParams(collective_id=collective_id, has_side_effects=True),
        name="swap_heads",
    )(*arrays)


def total_kernel(dims, in_ref, out_ref, *scratch):
    slots, (send_sem, recv_sem) = scratch[:4], scratch[4:]
    band, place = place_of(dims)
    head = lax.axis_index("head")
    strides = strides_of(dims)
    lines = [
        (dims[axis], place[axis], lambda at, axis=axis: (band + (at - place[axis]) * strides[axis], head))
        for axis in (2, 1, 0)
    ]
    lines.append((2, head, lambda at: (band, at)))
    barrier = pltpu.get_barrier_semaphore()
    for size, mine, device in lines:
        for shift in range(1, size):
            pl.semaphore_signal(barrier, inc=1, device_id=device((mine + shift) % size), device_id_type=MESH)
    pl.semaphore_wait(barrier, sum(size - 1 for size, _, _ in lines))
    out_ref[...] = in_ref[...]
    rows = in_ref.shape[0]
    for line, (size, mine, device) in enumerate(lines):
        part = pl.ds(0, rows) if line < 3 else pl.ds(rows - 8, 8)
        slots[line][mine] = out_ref[part, :]

        def copy(shift):
            return pltpu.make_async_remote_copy(
                slots[line].at[mine], slots[line].at[mine], send_sem.at[line, shift - 1], recv_sem.at[line, shift - 1],
                device_id=device((mine + shift) % size), device_id_type=MESH,
            )

        def incoming(shift):
            there = (mine + size - shift) % size
            return pltpu.make_async_remote_copy(
                slots[line].at[there], slots[line].at[there], send_sem.at[line, shift - 1], recv_sem.at[line, shift - 1],
                device_id=device(there), device_id_type=MESH,
            )

        for shift in range(1, size):
            copy(shift).start()
        for shift in range(1, size):
            incoming(shift).wait_recv()
        total = slots[line][0]
        for at in range(1, size):
            total = total + slots[line][at]
        out_ref[part, :] = total
        for shift in range(1, size):
            copy(shift).wait_send()


def mesh_total(bands, tile, collective_id):
    dims = band_dims(bands)
    longest = max(*dims, 2)
    vmem = pl.BlockSpec(memory_space=pltpu.VMEM)
    rows = tile.shape[0]
    return pl.pallas_call(
        partial(total_kernel, dims),
        out_shape=jax.ShapeDtypeStruct(tile.shape, tile.dtype),
        in_specs=[vmem],
        out_specs=vmem,
        scratch_shapes=[
            *(pltpu.VMEM((dims[axis], rows, LANES), tile.dtype) for axis in (2, 1, 0)),
            pltpu.VMEM((2, 8, LANES), tile.dtype),
            pltpu.SemaphoreType.DMA((4, longest - 1)),
            pltpu.SemaphoreType.DMA((4, longest - 1)),
        ],
        compiler_params=pltpu.CompilerParams(collective_id=collective_id, has_side_effects=True),
        name="mesh_total",
    )(tile)


def head_total(partials, collective_id):
    low = partials.astype(jnp.bfloat16)
    (there,) = swapped(collective_id, low)
    return low.astype(jnp.float32) + there.astype(jnp.float32)


def adamw_update(weight, moment_one, moment_two, gradient, step_rate, decay_rate):
    moment_one_new = BETA_ONE * moment_one + (1.0 - BETA_ONE) * gradient
    moment_two_new = BETA_TWO * moment_two + (1.0 - BETA_TWO) * gradient * gradient
    unbiased_one = moment_one_new / (1.0 - BETA_ONE**STEP)
    unbiased_two = moment_two_new / (1.0 - BETA_TWO**STEP)
    weight_new = weight - step_rate * (
        unbiased_one / (jnp.sqrt(unbiased_two) + ADAM_EPS) + decay_rate * weight
    )
    return (weight_new, moment_one_new, moment_two_new)


def local(
    tokens,
    text_states,
    cotangent,
    earlier,
    proj_master,
    out_master,
    mlp_master,
    gain_master,
    proj_first,
    proj_second,
    out_first,
    out_second,
    mlp_first,
    mlp_second,
    gain_first,
    gain_second,
):
    streams, band_rows, model_width = tokens.shape
    row_count = streams * band_rows
    text_rows = text_states.shape[1]
    bands, head = lax.axis_size("band"), lax.axis_index("head")
    shard_rows, width = proj_master.shape[1:]
    chunks = mlp_master.shape[2] // width
    mlp_cut = mlp_master.reshape(2, shard_rows, chunks, width).transpose(0, 2, 1, 3)
    shard = jnp.concatenate(
        [proj_master, out_master, mlp_cut.reshape(2 * chunks, shard_rows, width)]
    ).astype(jnp.bfloat16)
    gain_low = gain_master.astype(jnp.bfloat16).astype(jnp.float32)
    gain_tile = jnp.pad(gain_low, ((0, 5), (0, LANES - shard_rows)))
    both = jnp.concatenate([tokens, text_states], axis=1)
    context = lax.dynamic_index_in_dim(both, head, 0, keepdims=False)
    gathered, gain_tiles, passed = gather_weights(bands, shard, gain_tile, context, 1)
    weights = gathered.reshape(shard.shape[0], model_width, width)
    w_query, w_key, w_value, w_cross, w_text_key, w_text_value, w_self_out, w_cross_out = (
        weights[at] for at in range(8)
    )
    w_up = [weights[8 + at] for at in range(chunks)]
    w_down = [weights[8 + chunks + at] for at in range(chunks)]
    gains = gain_tiles.reshape(bands, 8, LANES)[:, :3, :shard_rows].transpose(1, 0, 2).reshape(3, model_width)

    offsets = earlier[:, 0]
    reach_ids = jnp.arange(SEQ_BANDS)
    within = reach_ids[None, :] <= offsets[:, None]
    inputs = tokens.astype(jnp.float32).reshape(row_count, model_width)
    reached = jnp.concatenate([tokens[:, None], passed[:, :, :band_rows]], axis=1)
    normed_all = jnp.where(
        within[:, :, None, None], norm_rows(reached.astype(jnp.float32), gains[0]), 0.0
    ).astype(jnp.bfloat16)
    normed_one = normed_all[:, 0].reshape(row_count, model_width)
    normed_all = normed_all.reshape(SEQ_BANDS * row_count, model_width)
    row_shape = (streams, band_rows, width)
    reach_shape = (streams, SEQ_BANDS, band_rows, width)
    text_shape = (streams, 1, text_rows, width)
    queries = matmul(normed_one, w_query).astype(jnp.bfloat16).reshape(row_shape)
    keys = matmul(normed_all, w_key).astype(jnp.bfloat16).reshape(reach_shape)
    values = matmul(normed_all, w_value).astype(jnp.bfloat16).reshape(reach_shape)
    attended, self_totals = attention(queries, keys, values, offsets, True)
    attended = attended.reshape(row_count, width)
    hidden_one = inputs + head_total(matmul_t(attended, w_self_out), 3)
    normed_two = norm_rows(hidden_one, gains[1]).astype(jnp.bfloat16)
    cross_queries = matmul(normed_two, w_cross).astype(jnp.bfloat16).reshape(row_shape)
    caption = text_states
    for behind in range(1, SEQ_BANDS):
        caption = jnp.where((offsets == behind)[:, None, None], passed[:, behind - 1, band_rows:], caption)
    caption = caption.reshape(streams * text_rows, model_width)
    cross_keys = matmul(caption, w_text_key).astype(jnp.bfloat16).reshape(text_shape)
    cross_values = matmul(caption, w_text_value).astype(jnp.bfloat16).reshape(text_shape)
    crossed, cross_totals = attention(cross_queries, cross_keys, cross_values, offsets, False)
    crossed = crossed.reshape(row_count, width)
    hidden_two = hidden_one + head_total(matmul_t(crossed, w_cross_out), 4)
    normed_three = norm_rows(hidden_two, gains[2]).astype(jnp.bfloat16)
    before = [matmul(normed_three, part) for part in w_up]
    gelu = partial(jax.nn.gelu, approximate=False)
    activated = [gelu(part).astype(jnp.bfloat16) for part in before]
    mlp_out = sum(matmul_t(part, weight) for part, weight in zip(activated, w_down))
    block_out = (hidden_two + head_total(mlp_out, 5)).astype(jnp.bfloat16).reshape(tokens.shape)

    incoming_low = cotangent.reshape(row_count, model_width)
    incoming = incoming_low.astype(jnp.float32)
    grad_down = [inner_t(incoming_low, part) for part in activated]
    grad_before = []
    for part, weight in zip(before, w_down):
        _, gelu_pull = jax.vjp(gelu, part)
        grad_before.append(gelu_pull(matmul(incoming_low, weight))[0].astype(jnp.bfloat16))
    grad_up = [inner_t(normed_three, part) for part in grad_before]
    grad_normed_three = head_total(sum(matmul_t(part, weight) for part, weight in zip(grad_before, w_up)), 6)
    _, pull_three = jax.vjp(norm_rows, hidden_two, gains[2])
    back_two, gain_grad_three = pull_three(grad_normed_three)
    grad_two = incoming + back_two
    grad_two_low = grad_two.astype(jnp.bfloat16)
    grad_cross_out = inner_t(grad_two_low, crossed)
    grad_crossed = matmul(grad_two_low, w_cross_out).astype(jnp.bfloat16).reshape(row_shape)
    grad_cq, grad_ck, grad_cv = attention_back(
        cross_queries, cross_keys, cross_values, offsets, cross_totals, grad_crossed, False
    )
    grad_cq = grad_cq.reshape(row_count, width)
    grad_ck = grad_ck.reshape(streams * text_rows, width)
    grad_cv = grad_cv.reshape(streams * text_rows, width)
    text_part = (matmul_t(grad_ck, w_text_key) + matmul_t(grad_cv, w_text_value)).astype(jnp.bfloat16)
    text_part = text_part.reshape(text_states.shape)
    grad_normed_two = head_total(matmul_t(grad_cq, w_cross), 7)
    _, pull_two = jax.vjp(norm_rows, hidden_one, gains[1])
    back_one, gain_grad_two = pull_two(grad_normed_two)
    grad_one = grad_two + back_one
    grad_one_low = grad_one.astype(jnp.bfloat16)
    grad_self_out = inner_t(grad_one_low, attended)
    grad_attended = matmul(grad_one_low, w_self_out).astype(jnp.bfloat16).reshape(row_shape)
    grad_queries, grad_keys, grad_values = attention_back(
        queries, keys, values, offsets, self_totals, grad_attended, True
    )
    grad_queries = grad_queries.reshape(row_count, width)
    reach_part = matmul_t(grad_keys.reshape(-1, width), w_key) + matmul_t(grad_values.reshape(-1, width), w_value)
    reach_part = reach_part.reshape(streams, SEQ_BANDS, band_rows, model_width)
    own_part = matmul_t(grad_queries, w_query).reshape(tokens.shape) + reach_part[:, 0]
    own_text = jnp.where((offsets == 0)[:, None, None], text_part, 0).astype(jnp.bfloat16)
    sent_text = jnp.where(
        (offsets[:, None] == reach_ids[None, 1:])[:, :, None, None], text_part[:, None], 0
    ).astype(jnp.bfloat16)
    own_back = jnp.concatenate([own_part.astype(jnp.bfloat16), own_text], axis=1)
    sent_back = jnp.concatenate([reach_part[:, 1:].astype(jnp.bfloat16), sent_text], axis=2)
    mine = lax.dynamic_index_in_dim(sent_back, head, 0, keepdims=False)
    other = lax.dynamic_index_in_dim(sent_back, 1 - head, 0, keepdims=False)
    own_there, mine_there = swapped(8, own_back, other)
    own_back = own_back.astype(jnp.float32) + own_there.astype(jnp.float32)
    returned = (mine.astype(jnp.float32) + mine_there.astype(jnp.float32)).astype(jnp.bfloat16)

    flat = lambda part: part.reshape(-1, width)
    grads = jnp.stack(
        [
            part.astype(jnp.bfloat16)
            for part in (
                inner_t(normed_one, grad_queries),
                inner_t(normed_all, flat(grad_keys)),
                inner_t(normed_all, flat(grad_values)),
                inner_t(normed_two, grad_cq),
                inner_t(caption, grad_ck),
                inner_t(caption, grad_cv),
                grad_self_out,
                grad_cross_out,
                *grad_up,
                *grad_down,
            )
        ]
    )
    summed, came_back = reduce_grads(bands, grads, returned, 2)
    came_low = came_back.astype(jnp.bfloat16)
    (came_there,) = swapped(9, came_low)
    came_both = jnp.stack([jnp.where(head == 0, came_low, came_there), jnp.where(head == 0, came_there, came_low)])
    back_all = own_back + came_both.astype(jnp.float32)
    grad_normed_one = back_all[:, :band_rows].reshape(row_count, model_width)
    grad_text = back_all[:, band_rows:]
    _, pull_one = jax.vjp(norm_rows, inputs, gains[0])
    back_zero, gain_grad_one = pull_one(grad_normed_one)
    grad_tokens = (grad_one + back_zero).reshape(tokens.shape)

    squares = jnp.sum(summed * summed)
    gain_rows = jnp.stack([gain_grad_one, gain_grad_two, gain_grad_three]).reshape(-1, LANES)
    tile = jnp.concatenate([gain_rows, jnp.full((8, LANES), squares)])
    tile = mesh_total(bands, tile, 10)
    gain_total = tile[:-8].reshape(3, model_width)
    grad_norm = jnp.sqrt(tile[-1, 0] + jnp.sum(gain_total * gain_total))
    gain_grad = lax.dynamic_slice_in_dim(gain_total, lax.axis_index("band") * shard_rows, shard_rows, 1)
    proj_grad, out_grad = summed[:6], summed[6:8]
    mlp_grad = summed[8:].reshape(2, chunks, shard_rows, width).transpose(0, 2, 1, 3).reshape(mlp_master.shape)
    factor = jnp.minimum(1.0, CLIP / grad_norm)
    matrix_rate = 2.0 * D ** (-0.5)
    new_proj = adamw_update(
        proj_master, proj_first, proj_second, proj_grad * factor, matrix_rate, DECAY
    )
    new_out = adamw_update(out_master, out_first, out_second, out_grad * factor, matrix_rate, DECAY)
    new_mlp = adamw_update(mlp_master, mlp_first, mlp_second, mlp_grad * factor, matrix_rate, DECAY)
    new_gain = adamw_update(
        gain_master, gain_first, gain_second, gain_grad * factor, GAIN_RATE, 0.0
    )
    return (
        block_out,
        grad_tokens,
        grad_text,
        grad_norm,
        new_proj[0],
        new_proj[1],
        new_proj[2],
        new_out[0],
        new_out[1],
        new_out[2],
        new_mlp[0],
        new_mlp[1],
        new_mlp[2],
        new_gain[0],
        new_gain[1],
        new_gain[2],
    )


def solution(mesh):
    return jax.shard_map(
        local,
        mesh=mesh,
        in_specs=(
            P(None, "band", None),
            P(None, "band", None),
            P(None, "band", None),
            P(None, "band"),
            P(None, "band", "head"),
            P(None, "band", "head"),
            P(None, "band", "head"),
            P(None, "band"),
            P(None, "band", "head"),
            P(None, "band", "head"),
            P(None, "band", "head"),
            P(None, "band", "head"),
            P(None, "band", "head"),
            P(None, "band", "head"),
            P(None, "band"),
            P(None, "band"),
        ),
        out_specs=(
            P(None, "band", None),
            P(None, "band", None),
            P(None, "band", None),
            P(),
            P(None, "band", "head"),
            P(None, "band", "head"),
            P(None, "band", "head"),
            P(None, "band", "head"),
            P(None, "band", "head"),
            P(None, "band", "head"),
            P(None, "band", "head"),
            P(None, "band", "head"),
            P(None, "band", "head"),
            P(None, "band"),
            P(None, "band"),
            P(None, "band"),
        ),
        check_vma=False,
    )
```

```python
from functools import partial

import jax
import jax.numpy as jnp
from jax import lax
from jax.experimental import pallas as pl
from jax.experimental.pallas import tpu as pltpu
from jax.sharding import PartitionSpec as P

D = 1024
HEAD_DIM = 64
SEQ_BANDS = 4
STEP = 10


EPS = 1e-05
NEG = -1e30
CLIP = 1.0
BETA_ONE = 0.9
BETA_TWO = 0.95
ADAM_EPS = 1e-08
DECAY = 0.1
GAIN_RATE = 0.5
LANES = 128


MESH = pl.DeviceIdType.MESH
ORDERS = ((2, 0, 1), (1, 0, 2))
GROUP = 4
GAP = 2


def band_dims(bands):
    inner = 4 if bands >= 64 else 2
    return (bands // (inner * inner), inner, inner)


def strides_of(dims):
    return (dims[1] * dims[2], dims[2], 1)


def place_of(dims):
    band = lax.axis_index("band")
    return band, (
        band // (dims[1] * dims[2]),
        (band // dims[2]) % dims[1],
        band % dims[2],
    )


def stage_list(dims, order):
    return [(phase, step) for phase in range(3) for step in range(dims[order[phase]] - 1)]


def block_of(ref, lead, place, order, phase, index, columns):
    at = list(place)
    for done in range(phase):
        at[order[done]] = slice(None)
    at[order[phase]] = index
    return ref.at[(*lead, *at, slice(None), columns)]


def greet(dims, place, band, head, extra):
    barrier = pltpu.get_barrier_semaphore()
    strides = strides_of(dims)
    total = jnp.int32(0)
    peers = []
    for axis in range(3):
        for sign in (1, -1):
            there = place[axis] + sign
            peers.append(((there >= 0) & (there < dims[axis]), band + sign * strides[axis], head))
    peers += extra
    for present, peer_band, peer_head in peers:
        @pl.when(present)
        def _():
            pl.semaphore_signal(barrier, inc=1, device_id=(peer_band, peer_head), device_id_type=MESH)
        total = total + present.astype(jnp.int32)
    pl.semaphore_wait(barrier, total)


def gather_kernel(dims, has_context, *refs):
    if has_context:
        (w_ref, gain_ref, ctx_ref, out_ref, gains_ref, ctx_out,
         own_sem, send_sem, recv_sem, gsend, grecv, prev_ref, up_sem, csend, crecv, psend, precv) = refs
    else:
        (w_ref, gain_ref, out_ref, gains_ref, own_sem, send_sem, recv_sem, gsend, grecv) = refs
    band, place = place_of(dims)
    head = lax.axis_index("head")
    strides = strides_of(dims)
    count = w_ref.shape[0]
    half = w_ref.shape[2] // 2
    bands = dims[0] * dims[1] * dims[2]
    true = band >= 0
    extra = []
    if has_context:
        base = (band // GROUP) * GROUP
        mine = band % GROUP
        for shift in range(1, GROUP):
            extra.append((true, base + (mine + shift) % GROUP, head))
        extra.append((band + GROUP < bands, band + GROUP, head))
        extra.append((band >= GROUP, band - GROUP, head))
        extra.append((true, band, 1 - head))
    greet(dims, place, band, head, extra)

    own = [
        pltpu.make_async_copy(w_ref, out_ref.at[:, place[0], place[1], place[2]], own_sem.at[0]),
        pltpu.make_async_copy(gain_ref, gains_ref.at[place[0], place[1], place[2]], own_sem.at[1]),
    ]
    for copy in own:
        copy.start()

    def up_copy():
        return pltpu.make_async_remote_copy(
            ctx_ref, prev_ref, up_sem.at[0], up_sem.at[1], device_id=(band + GROUP, head), device_id_type=MESH
        )

    def peer_copy(back, source):
        return pltpu.make_async_remote_copy(
            source, ctx_out.at[head, back - 1], csend.at[back - 1], crecv.at[back - 1],
            device_id=(base + (mine + back) % GROUP, head), device_id_type=MESH,
        )

    def pair_copy(back):
        return pltpu.make_async_remote_copy(
            ctx_out.at[head, back - 1], ctx_out.at[head, back - 1], psend.at[back - 1], precv.at[back - 1],
            device_id=(band, 1 - head), device_id_type=MESH,
        )

    if has_context:
        @pl.when(band + GROUP < bands)
        def _():
            up_copy().start()

    def piece(color, m, phase, step, way, incoming):
        order = ORDERS[color]
        axis = order[phase]
        size, at = dims[axis], place[axis]
        toward = 1 if way == 0 else -1
        stage = stage_list(dims, order).index((phase, step))
        if incoming:
            index = at - toward * (step + 1)
            present = (index >= 0) & (index < size)
        else:
            index = at - toward * step
            present = (index >= 0) & (index < size) & (at + toward >= 0) & (at + toward < size)
        columns = pl.ds(color * half, half)
        target = (band + toward * strides[axis], head)
        land = block_of(out_ref, (m,), place, order, phase, index, columns)
        source = w_ref.at[m, :, columns] if stage == 0 else land
        copy = pltpu.make_async_remote_copy(
            source, land, send_sem.at[color, stage, way, m], recv_sem.at[color, stage, way, m],
            device_id=target, device_id_type=MESH,
        )
        return present, copy

    def gain_piece(phase, step, way, incoming):
        order = ORDERS[0]
        axis = order[phase]
        size, at = dims[axis], place[axis]
        toward = 1 if way == 0 else -1
        stage = stage_list(dims, order).index((phase, step))
        if incoming:
            index = at - toward * (step + 1)
            present = (index >= 0) & (index < size)
        else:
            index = at - toward * step
            present = (index >= 0) & (index < size) & (at + toward >= 0) & (at + toward < size)
        land = block_of(gains_ref, (), place, order, phase, index, slice(None))
        source = gain_ref if stage == 0 else land
        copy = pltpu.make_async_remote_copy(
            source, land, gsend.at[stage, way], grecv.at[stage, way],
            device_id=(band + toward * strides[axis], head), device_id_type=MESH,
        )
        return present, copy

    stages = [stage_list(dims, order) for order in ORDERS]
    depth = len(stages[0])

    def context_step(t):
        for back in range(1, GROUP):
            @pl.when((t == back - 1) & (mine + back < GROUP))
            def _():
                peer_copy(back, ctx_ref).start()
        @pl.when((t == 2) & (band >= GROUP))
        def _():
            pltpu.make_async_remote_copy(
                ctx_ref, prev_ref, up_sem.at[0], up_sem.at[1], device_id=(band - GROUP, head), device_id_type=MESH
            ).wait_recv()
        for back in range(1, GROUP):
            @pl.when((t == GROUP - back + 1) & (mine + back >= GROUP) & (band >= GROUP))
            def _():
                peer_copy(back, prev_ref).start()
        for back in range(1, GROUP):
            @pl.when((t == 7) & ((mine >= back) | (band >= GROUP)))
            def _():
                peer_copy(back, ctx_ref).wait_recv()
                pair_copy(back).start()

    def gains_step(t):
        for stage in range(depth + 1):
            @pl.when(t == stage)
            def _():
                if stage == 1:
                    for copy in own:
                        copy.wait()
                if stage > 0:
                    for way in range(2):
                        present, copy = gain_piece(*stages[0][stage - 1], way, True)
                        @pl.when(present)
                        def _():
                            copy.wait_recv()
                if stage < depth:
                    for way in range(2):
                        present, copy = gain_piece(*stages[0][stage], way, False)
                        @pl.when(present)
                        def _():
                            copy.start()

    def body(t, carry):
        gains_step(t)
        if has_context:
            context_step(t)
        for stage in range(depth, -1, -1):
            m = t - GAP * stage
            @pl.when((m >= 0) & (m < count))
            def _():
                for color in range(2):
                    if stage > 0:
                        for way in range(2):
                            present, copy = piece(color, m, *stages[color][stage - 1], way, True)
                            @pl.when(present)
                            def _():
                                copy.wait_recv()
                    if stage < depth:
                        for way in range(2):
                            present, copy = piece(color, m, *stages[color][stage], way, False)
                            @pl.when(present)
                            def _():
                                copy.start()
        return carry

    lax.fori_loop(0, count + GAP * depth, body, 0)

    if has_context:
        for back in range(1, GROUP):
            @pl.when((mine >= back) | (band >= GROUP))
            def _():
                pltpu.make_async_remote_copy(
                    ctx_out.at[1 - head, back - 1], ctx_out.at[1 - head, back - 1], psend.at[back - 1],
                    precv.at[back - 1], device_id=(band, 1 - head), device_id_type=MESH,
                ).wait_recv()
                pair_copy(back).wait_send()
            @pl.when((mine + back < GROUP) | (band >= GROUP))
            def _():
                peer_copy(back, ctx_ref).wait_send()
        @pl.when(band + GROUP < bands)
        def _():
            up_copy().wait_send()

    for stage in range(depth):
        for way in range(2):
            present, copy = gain_piece(*stages[0][stage], way, False)
            @pl.when(present)
            def _():
                copy.wait_send()

    def drain(m, carry):
        for stage in range(depth):
            for color in range(2):
                for way in range(2):
                    present, copy = piece(color, m, *stages[color][stage], way, False)
                    @pl.when(present)
                    def _():
                        copy.wait_send()
        return carry

    lax.fori_loop(0, count, drain, 0)


def gather_weights(bands, shard, gain_tile, context, collective_id):
    dims = band_dims(bands)
    count, rows, width = shard.shape
    depth = len(stage_list(dims, ORDERS[0]))
    vmem = pl.BlockSpec(memory_space=pltpu.VMEM)
    anyspace = pl.BlockSpec(memory_space=pl.ANY)
    has_context = context is not None
    out_shape = [
        jax.ShapeDtypeStruct((count, *dims, rows, width), shard.dtype),
        jax.ShapeDtypeStruct((*dims, *gain_tile.shape), gain_tile.dtype),
    ]
    scratch = [
        pltpu.SemaphoreType.DMA((2,)),
        pltpu.SemaphoreType.DMA((2, depth, 2, count)),
        pltpu.SemaphoreType.DMA((2, depth, 2, count)),
        pltpu.SemaphoreType.DMA((depth, 2)),
        pltpu.SemaphoreType.DMA((depth, 2)),
    ]
    args = [shard, gain_tile]
    if has_context:
        args.append(context)
        out_shape.append(jax.ShapeDtypeStruct((2, GROUP - 1, *context.shape), context.dtype))
        scratch += [
            pltpu.VMEM(context.shape, context.dtype),
            pltpu.SemaphoreType.DMA((2,)),
            pltpu.SemaphoreType.DMA((GROUP - 1,)),
            pltpu.SemaphoreType.DMA((GROUP - 1,)),
            pltpu.SemaphoreType.DMA((GROUP - 1,)),
            pltpu.SemaphoreType.DMA((GROUP - 1,)),
        ]
    return pl.pallas_call(
        partial(gather_kernel, dims, has_context),
        out_shape=out_shape,
        in_specs=[vmem] * len(args),
        out_specs=[anyspace] * len(out_shape),
        scratch_shapes=scratch,
        compiler_params=pltpu.CompilerParams(collective_id=collective_id, has_side_effects=True),
        name="gather_weights",
    )(*args)


def reduce_kernel(dims, count, has_context, *refs):
    g_refs, refs = refs[:count], refs[count:]
    if has_context:
        (back_ref, out_ref, back_out, gv, load_sem, last_ref, mid_ref, first_ref, send_sem, recv_sem,
         landed, relay, from_up, csend, crecv, up_sem) = refs
    else:
        (out_ref, gv, load_sem, last_ref, mid_ref, first_ref, send_sem, recv_sem) = refs
    band, place = place_of(dims)
    head = lax.axis_index("head")
    strides = strides_of(dims)
    half = g_refs[0].shape[-1] // 2
    bands = dims[0] * dims[1] * dims[2]
    true = band >= 0
    orders = tuple(order[::-1] for order in ORDERS)
    lands = (last_ref, mid_ref, first_ref)

    def load(m, source):
        return pltpu.make_async_copy(source, gv.at[m], load_sem.at[m])

    for m in range(count):
        load(m, g_refs[m]).start()

    extra = []
    if has_context:
        base = (band // GROUP) * GROUP
        mine = band % GROUP
        for shift in range(1, GROUP):
            extra.append((true, base + (mine + shift) % GROUP, head))
        extra.append((band + GROUP < bands, band + GROUP, head))
        extra.append((band >= GROUP, band - GROUP, head))
    greet(dims, place, band, head, extra)

    def peer_copy(back):
        return pltpu.make_async_remote_copy(
            back_ref.at[back - 1], landed.at[back - 1], csend.at[back - 1], crecv.at[back - 1],
            device_id=(base + (mine + GROUP - back) % GROUP, head), device_id_type=MESH,
        )

    def down_copy(target):
        return pltpu.make_async_remote_copy(
            relay, from_up, up_sem.at[0], up_sem.at[1], device_id=(target, head), device_id_type=MESH
        )

    def slot(size, step, way):
        return 0 if size == 2 else step * 2 + way

    def own_block(m, color, phase, index):
        order = orders[color]
        at = list(place)
        for later in range(phase + 1, 3):
            at[order[later]] = slice(None)
        at[order[phase]] = index
        return gv.at[(m, *at, slice(None), pl.ds(color * half, half))]

    def landing(m, color, phase, step, way):
        size = dims[orders[color][phase]]
        return lands[phase].at[m, color, slot(size, step, way)]

    def outgoing(m, color, phase, step, way):
        axis = orders[color][phase]
        size, at = dims[axis], place[axis]
        toward = 1 if way == 0 else -1
        rank = at if way == 0 else size - 1 - at
        index = size - 1 - step + at if way == 0 else step + at - (size - 1)
        present = (rank <= step) & (at + toward >= 0) & (at + toward < size)
        stage = stage_list(dims, orders[color]).index((phase, step))
        target = (band + toward * strides[axis], head)

        def copy(source):
            return pltpu.make_async_remote_copy(
                source, landing(m, color, phase, step, way),
                send_sem.at[color, stage, way, m], recv_sem.at[color, stage, way, m],
                device_id=target, device_id_type=MESH,
            )

        return present, rank, index, copy

    def arrived(m, color, phase, step, way):
        axis = orders[color][phase]
        size, at = dims[axis], place[axis]
        before = at - 1 if way == 0 else at + 1
        rank = before if way == 0 else size - 1 - before
        present = (before >= 0) & (before < size) & (rank <= step)
        _, _, _, copy = outgoing(m, color, phase, step, way)
        return present, copy(landing(m, color, phase, step, way))

    def add_into(target, source):
        lead = target.shape[:-2]
        if len(lead) == 0:
            target[...] = target[...] + source[...]
        elif len(lead) == 1:
            for i in range(lead[0]):
                target[i] = target[i] + source[i]
        else:
            for i in range(lead[0]):
                for j in range(lead[1]):
                    target[i, j] = target[i, j] + source[i, j]

    stages = [stage_list(dims, order) for order in orders]
    depth = len(stages[0])

    def send(m, color, phase, step):
        axis = orders[color][phase]
        size = dims[axis]
        for way in range(2):
            present, rank, index, copy = outgoing(m, color, phase, step, way)
            @pl.when(present & (rank == 0))
            def _():
                copy(own_block(m, color, phase, index)).start()
            if step > 0:
                @pl.when(present & (rank > 0))
                def _():
                    from_before = landing(m, color, phase, step - 1, way)
                    add_into(from_before, own_block(m, color, phase, index))
                    copy(from_before).start()

    def settle(m, color, phase, step):
        axis = orders[color][phase]
        size = dims[axis]
        for way in range(2):
            present, copy = arrived(m, color, phase, step, way)
            @pl.when(present)
            def _():
                copy.wait_recv()
                if step == size - 2:
                    landed_here = landing(m, color, phase, step, way)
                    if phase < 2:
                        add_into(own_block(m, color, phase, place[axis]), landed_here)
                    else:
                        columns = pl.ds(color * half, half)
                        if size == 2:
                            own = own_block(m, color, phase, place[axis])
                            out_ref[m, :, columns] = own[...].astype(jnp.float32) + landed_here[...].astype(jnp.float32)
                        else:
                            add_into(own_block(m, color, phase, place[axis]), landed_here)
        if phase == 2 and step == size - 2 and size > 2:
            columns = pl.ds(color * half, half)
            out_ref[m, :, columns] = own_block(m, color, phase, place[axis])[...].astype(jnp.float32)

    def body(t, carry):
        for stage in range(depth, -1, -1):
            m = t - stage
            @pl.when((m >= 0) & (m < count))
            def _():
                if stage == 0:
                    load(m, g_refs[0]).wait()
                for color in range(2):
                    if stage > 0:
                        settle(m, color, *stages[color][stage - 1])
                    if stage < depth:
                        send(m, color, *stages[color][stage])
        if has_context:
            for back in range(1, GROUP):
                @pl.when((t == back - 1) & ((mine >= back) | (band >= GROUP)))
                def _():
                    peer_copy(back).start()
            @pl.when(t == 4)
            def _():
                for back in range(1, GROUP):
                    @pl.when((mine + back < GROUP) | (band >= GROUP))
                    def _():
                        peer_copy(back).wait_recv()
                @pl.when((mine > 0) & (band >= GROUP))
                def _():
                    for cut in range(0, relay.shape[0], 64):
                        rows = pl.ds(cut, 64)
                        total = landed[GROUP - 2, rows, :].astype(jnp.float32)
                        for back in range(1, GROUP - 1):
                            total = total + jnp.where(mine + back >= GROUP, landed[back - 1, rows, :].astype(jnp.float32), 0.0)
                        relay[rows, :] = total.astype(relay.dtype)
                    down_copy(band - GROUP).start()
            @pl.when(t == 8)
            def _():
                @pl.when((mine > 0) & (band + GROUP < bands))
                def _():
                    down_copy(band + GROUP).wait_recv()
                for cut in range(0, relay.shape[0], 64):
                    rows = pl.ds(cut, 64)
                    total = jnp.where((mine > 0) & (band + GROUP < bands), from_up[rows, :].astype(jnp.float32), 0.0)
                    for back in range(1, GROUP):
                        total = total + jnp.where(mine + back < GROUP, landed[back - 1, rows, :].astype(jnp.float32), 0.0)
                    back_out[rows, :] = total
        return carry

    lax.fori_loop(0, count + depth, body, 0)

    if has_context:
        for back in range(1, GROUP):
            @pl.when((mine >= back) | (band >= GROUP))
            def _():
                peer_copy(back).wait_send()
        @pl.when((mine > 0) & (band >= GROUP))
        def _():
            down_copy(band - GROUP).wait_send()

    def drain(m, carry):
        for stage in range(depth):
            for color in range(2):
                phase, step = stages[color][stage]
                for way in range(2):
                    present, rank, index, copy = outgoing(m, color, phase, step, way)
                    @pl.when(present)
                    def _():
                        copy(own_block(m, color, phase, index)).wait_send()
        return carry

    lax.fori_loop(0, count, drain, 0)


def reduce_grads(bands, grads, returned, collective_id):
    dims = band_dims(bands)
    count = len(grads)
    depth_rows, width = grads[0].shape
    rows = depth_rows // bands
    half = width // 2
    depth = len(stage_list(dims, ORDERS[0]))
    vmem = pl.BlockSpec(memory_space=pltpu.VMEM)
    anyspace = pl.BlockSpec(memory_space=pl.ANY)
    slots = lambda size: 1 if size == 2 else 2 * (size - 1)
    inner = dims[1]
    has_context = returned is not None
    grads = [part.reshape(*dims, rows, width) for part in grads]
    scratch = [
        pltpu.VMEM((count, *grads[0].shape), jnp.bfloat16),
        pltpu.SemaphoreType.DMA((count,)),
        pltpu.VMEM((count, 2, slots(inner), dims[0], inner, rows, half), jnp.bfloat16),
        pltpu.VMEM((count, 2, slots(dims[0]), inner, rows, half), jnp.bfloat16),
        pltpu.VMEM((count, 2, slots(inner), rows, half), jnp.bfloat16),
        pltpu.SemaphoreType.DMA((2, depth, 2, count)),
        pltpu.SemaphoreType.DMA((2, depth, 2, count)),
    ]
    args = list(grads)
    in_specs = [anyspace] * count
    out_shape = [jax.ShapeDtypeStruct((count, rows, width), jnp.float32)]
    if has_context:
        args.append(returned)
        in_specs.append(vmem)
        ctx_shape = returned.shape[1:]
        out_shape.append(jax.ShapeDtypeStruct(ctx_shape, jnp.float32))
        scratch += [
            pltpu.VMEM(returned.shape, returned.dtype),
            pltpu.VMEM(ctx_shape, returned.dtype),
            pltpu.VMEM(ctx_shape, returned.dtype),
            pltpu.SemaphoreType.DMA((GROUP - 1,)),
            pltpu.SemaphoreType.DMA((GROUP - 1,)),
            pltpu.SemaphoreType.DMA((2,)),
        ]
    return pl.pallas_call(
        partial(reduce_kernel, dims, count, has_context),
        out_shape=out_shape,
        in_specs=in_specs,
        out_specs=[vmem] * len(out_shape),
        scratch_shapes=scratch,
        compiler_params=pltpu.CompilerParams(
            collective_id=collective_id, has_side_effects=True, vmem_limit_bytes=67043328
        ),
        name="reduce_grads",
    )(*args)


def norm_rows(values, gain_row):
    centre = values - jnp.mean(values, axis=-1, keepdims=True)
    spread = jnp.mean(centre * centre, axis=-1, keepdims=True)
    return centre * lax.rsqrt(spread + EPS) * gain_row


def matmul(former, latter):
    return jnp.dot(former, latter, preferred_element_type=jnp.float32)


def matmul_t(former, latter):
    return lax.dot_general(
        former, latter, (((1,), (1,)), ((), ())), preferred_element_type=jnp.float32
    )


def inner_t(former, latter):
    return lax.dot_general(
        former, latter, (((0,), (0,)), ((), ())), preferred_element_type=jnp.float32
    )


def heads_of(block):
    lane = lax.broadcasted_iota(jnp.int32, block.shape, 1) // HEAD_DIM
    return [
        block * (lane == one).astype(jnp.float32).astype(block.dtype) for one in range(LANES // HEAD_DIM)
    ]


def shifted(scores, causal, behind):
    if not causal or behind > 0:
        return scores
    key_ids = lax.broadcasted_iota(jnp.int32, scores.shape, 0)
    query_ids = lax.broadcasted_iota(jnp.int32, scores.shape, 1)
    return jnp.where(key_ids <= query_ids, scores, NEG)


def attend_body(reach, causal, q_ref, k_ref, v_ref, out_ref, total_ref):
    scale = HEAD_DIM**-0.5
    values_t = [v_ref[behind].T for behind in range(reach)]
    outs = []
    for one, q_one in enumerate(heads_of(q_ref[...])):
        scores = [shifted(matmul_t(k_ref[behind], q_one) * scale, causal, behind) for behind in range(reach)]
        top = jnp.max(scores[0], axis=0, keepdims=True)
        for block in scores[1:]:
            top = jnp.maximum(top, jnp.max(block, axis=0, keepdims=True))
        raised = [jnp.exp(block - top) for block in scores]
        total = jnp.sum(raised[0], axis=0, keepdims=True)
        for block in raised[1:]:
            total = total + jnp.sum(block, axis=0, keepdims=True)
        share = 1.0 / total
        mixed = None
        for behind in range(reach):
            part = matmul(values_t[behind], (raised[behind] * share).astype(jnp.bfloat16))
            mixed = part if mixed is None else mixed + part
        outs.append(mixed[one * HEAD_DIM : (one + 1) * HEAD_DIM])
        total_ref[one : one + 1, :] = top + jnp.log(total)
    out_ref[...] = jnp.concatenate(outs, axis=0).T.astype(jnp.bfloat16)


def attend_back_body(reach, causal, q_ref, k_ref, v_ref, total_ref, g_ref, dq_ref, dk_ref, dv_ref):
    scale = HEAD_DIM**-0.5
    keys_t = [k_ref[behind].T for behind in range(reach)]
    q_heads, g_heads = heads_of(q_ref[...]), heads_of(g_ref[...])
    query_grads = []
    key_grads, value_grads = [None] * reach, [None] * reach
    for one in range(len(q_heads)):
        q_one, g_one = q_heads[one], g_heads[one]
        log_total = total_ref[one : one + 1, :]
        probs, grads, centre = [], [], None
        for behind in range(reach):
            scores = shifted(matmul_t(k_ref[behind], q_one) * scale, causal, behind)
            probs.append(jnp.exp(scores - log_total))
            grads.append(matmul_t(v_ref[behind], g_one))
            part = jnp.sum(grads[-1] * probs[-1], axis=0, keepdims=True)
            centre = part if centre is None else centre + part
        query_grad = None
        for behind in range(reach):
            grad_scores = (probs[behind] * (grads[behind] - centre)).astype(jnp.bfloat16)
            part = matmul(keys_t[behind], grad_scores)
            query_grad = part if query_grad is None else query_grad + part
            key_part = matmul(grad_scores, q_one)
            value_part = matmul(probs[behind].astype(jnp.bfloat16), g_one)
            key_grads[behind] = key_part if one == 0 else key_grads[behind] + key_part
            value_grads[behind] = value_part if one == 0 else value_grads[behind] + value_part
        query_grads.append(query_grad[one * HEAD_DIM : (one + 1) * HEAD_DIM])
    dq_ref[...] = (jnp.concatenate(query_grads, axis=0).T * scale).astype(jnp.bfloat16)
    for behind in range(dk_ref.shape[0]):
        if behind < reach:
            dk_ref[behind] = (key_grads[behind] * scale).astype(jnp.bfloat16)
            dv_ref[behind] = value_grads[behind].astype(jnp.bfloat16)
        else:
            dk_ref[behind] = jnp.zeros(dk_ref.shape[1:], dk_ref.dtype)
            dv_ref[behind] = jnp.zeros(dv_ref.shape[1:], dv_ref.dtype)


def by_offset(body, causal, offset_ref, *refs):
    reaches = refs[1].shape[0]
    if reaches == 1:
        body(1, causal, *refs)
        return
    offset = offset_ref[pl.program_id(0)]
    for earlier_bands in range(reaches):
        @pl.when(offset == earlier_bands)
        def _():
            body(earlier_bands + 1, causal, *refs)


def attention_specs(queries, keys):
    rows, reaches, key_rows = queries.shape[1], keys.shape[1], keys.shape[2]
    row_spec = pl.BlockSpec((None, rows, LANES), lambda stream, pair: (stream, 0, pair))
    key_spec = pl.BlockSpec((None, reaches, key_rows, LANES), lambda stream, pair: (stream, 0, 0, pair))
    total_spec = pl.BlockSpec((None, None, 8, rows), lambda stream, pair: (stream, pair, 0, 0))
    return row_spec, key_spec, total_spec


def attention(queries, keys, values, offsets, causal):
    streams, rows, width = queries.shape
    row_spec, key_spec, total_spec = attention_specs(queries, keys)
    return pl.pallas_call(
        partial(by_offset, attend_body, causal),
        grid=(streams, width // LANES),
        in_specs=[pl.BlockSpec(memory_space=pltpu.SMEM), row_spec, key_spec, key_spec],
        out_specs=[row_spec, total_spec],
        out_shape=[
            jax.ShapeDtypeStruct(queries.shape, jnp.bfloat16),
            jax.ShapeDtypeStruct((streams, width // LANES, 8, rows), jnp.float32),
        ],
        name="attend",
    )(offsets, queries, keys, values)


def attention_back(queries, keys, values, offsets, totals, grad_out, causal):
    streams, rows, width = queries.shape
    row_spec, key_spec, total_spec = attention_specs(queries, keys)
    return pl.pallas_call(
        partial(by_offset, attend_back_body, causal),
        grid=(streams, width // LANES),
        in_specs=[pl.BlockSpec(memory_space=pltpu.SMEM), row_spec, key_spec, key_spec, total_spec, row_spec],
        out_specs=[row_spec, key_spec, key_spec],
        out_shape=[
            jax.ShapeDtypeStruct(queries.shape, jnp.bfloat16),
            jax.ShapeDtypeStruct(keys.shape, jnp.bfloat16),
            jax.ShapeDtypeStruct(keys.shape, jnp.bfloat16),
        ],
        name="attend_back",
    )(offsets, queries, keys, values, totals, grad_out)


def swap_kernel(count, *refs):
    sources, targets = refs[:count], refs[count : 2 * count]
    send_sem, recv_sem = refs[2 * count :]
    band, head = lax.axis_index("band"), lax.axis_index("head")
    barrier = pltpu.get_barrier_semaphore()
    pl.semaphore_signal(barrier, inc=1, device_id=(band, 1 - head), device_id_type=MESH)
    pl.semaphore_wait(barrier, 1)
    copies = [
        pltpu.make_async_remote_copy(
            sources[one], targets[one], send_sem.at[one], recv_sem.at[one],
            device_id=(band, 1 - head), device_id_type=MESH,
        )
        for one in range(count)
    ]
    for copy in copies:
        copy.start()
    for copy in copies:
        copy.wait()


def swapped(collective_id, *arrays):
    vmem = pl.BlockSpec(memory_space=pltpu.VMEM)
    return pl.pallas_call(
        partial(swap_kernel, len(arrays)),
        out_shape=[jax.ShapeDtypeStruct(array.shape, array.dtype) for array in arrays],
        in_specs=[vmem] * len(arrays),
        out_specs=[vmem] * len(arrays),
        scratch_shapes=[pltpu.SemaphoreType.DMA((len(arrays),)), pltpu.SemaphoreType.DMA((len(arrays),))],
        compiler_params=pltpu.CompilerParams(collective_id=collective_id, has_side_effects=True),
        name="swap_heads",
    )(*arrays)


def total_kernel(dims, in_ref, out_ref, *scratch):
    slots, (send_sem, recv_sem) = scratch[:4], scratch[4:]
    band, place = place_of(dims)
    head = lax.axis_index("head")
    strides = strides_of(dims)
    lines = [
        (dims[axis], place[axis], lambda at, axis=axis: (band + (at - place[axis]) * strides[axis], head))
        for axis in (2, 1, 0)
    ]
    lines.append((2, head, lambda at: (band, at)))
    barrier = pltpu.get_barrier_semaphore()
    for size, mine, device in lines:
        for shift in range(1, size):
            pl.semaphore_signal(barrier, inc=1, device_id=device((mine + shift) % size), device_id_type=MESH)
    pl.semaphore_wait(barrier, sum(size - 1 for size, _, _ in lines))
    out_ref[...] = in_ref[...]
    rows = in_ref.shape[0]
    for line, (size, mine, device) in enumerate(lines):
        part = pl.ds(0, rows) if line < 3 else pl.ds(rows - 8, 8)
        slots[line][mine] = out_ref[part, :]

        def copy(shift):
            return pltpu.make_async_remote_copy(
                slots[line].at[mine], slots[line].at[mine], send_sem.at[line, shift - 1], recv_sem.at[line, shift - 1],
                device_id=device((mine + shift) % size), device_id_type=MESH,
            )

        def incoming(shift):
            there = (mine + size - shift) % size
            return pltpu.make_async_remote_copy(
                slots[line].at[there], slots[line].at[there], send_sem.at[line, shift - 1], recv_sem.at[line, shift - 1],
                device_id=device(there), device_id_type=MESH,
            )

        for shift in range(1, size):
            copy(shift).start()
        for shift in range(1, size):
            incoming(shift).wait_recv()
        total = slots[line][0]
        for at in range(1, size):
            total = total + slots[line][at]
        out_ref[part, :] = total
        for shift in range(1, size):
            copy(shift).wait_send()


def mesh_total(bands, tile, collective_id):
    dims = band_dims(bands)
    longest = max(*dims, 2)
    vmem = pl.BlockSpec(memory_space=pltpu.VMEM)
    rows = tile.shape[0]
    return pl.pallas_call(
        partial(total_kernel, dims),
        out_shape=jax.ShapeDtypeStruct(tile.shape, tile.dtype),
        in_specs=[vmem],
        out_specs=vmem,
        scratch_shapes=[
            *(pltpu.VMEM((dims[axis], rows, LANES), tile.dtype) for axis in (2, 1, 0)),
            pltpu.VMEM((2, 8, LANES), tile.dtype),
            pltpu.SemaphoreType.DMA((4, longest - 1)),
            pltpu.SemaphoreType.DMA((4, longest - 1)),
        ],
        compiler_params=pltpu.CompilerParams(collective_id=collective_id, has_side_effects=True),
        name="mesh_total",
    )(tile)


def head_total(partials, collective_id):
    low = partials.astype(jnp.bfloat16)
    (there,) = swapped(collective_id, low)
    return low.astype(jnp.float32) + there.astype(jnp.float32)


def adamw_update(weight, moment_one, moment_two, gradient, step_rate, decay_rate):
    moment_one_new = BETA_ONE * moment_one + (1.0 - BETA_ONE) * gradient
    moment_two_new = BETA_TWO * moment_two + (1.0 - BETA_TWO) * gradient * gradient
    unbiased_one = moment_one_new / (1.0 - BETA_ONE**STEP)
    unbiased_two = moment_two_new / (1.0 - BETA_TWO**STEP)
    weight_new = weight - step_rate * (
        unbiased_one / (jnp.sqrt(unbiased_two) + ADAM_EPS) + decay_rate * weight
    )
    return (weight_new, moment_one_new, moment_two_new)


def local(
    tokens,
    text_states,
    cotangent,
    earlier,
    proj_master,
    out_master,
    mlp_master,
    gain_master,
    proj_first,
    proj_second,
    out_first,
    out_second,
    mlp_first,
    mlp_second,
    gain_first,
    gain_second,
):
    streams, band_rows, model_width = tokens.shape
    row_count = streams * band_rows
    text_rows = text_states.shape[1]
    bands, head = lax.axis_size("band"), lax.axis_index("head")
    shard_rows, width = proj_master.shape[1:]
    shard = jnp.concatenate([proj_master, out_master]).astype(jnp.bfloat16)
    gain_low = gain_master.astype(jnp.bfloat16).astype(jnp.float32)
    gain_tile = jnp.pad(gain_low, ((0, 5), (0, LANES - shard_rows)))
    both = jnp.concatenate([tokens, text_states], axis=1)
    context = lax.dynamic_index_in_dim(both, head, 0, keepdims=False)
    gathered, gain_tiles, passed = gather_weights(bands, shard, gain_tile, context, 1)
    w_up = lax.all_gather(mlp_master[0].astype(jnp.bfloat16), "band", axis=0, tiled=True)
    down_low, gain_tiles = lax.optimization_barrier((mlp_master[1].astype(jnp.bfloat16), gain_tiles))
    w_down = lax.all_gather(down_low, "band", axis=0, tiled=True)
    weights = gathered.reshape(shard.shape[0], model_width, width)
    w_query, w_key, w_value, w_cross, w_text_key, w_text_value, w_self_out, w_cross_out = (
        weights[at] for at in range(8)
    )
    gains = gain_tiles.reshape(bands, 8, LANES)[:, :3, :shard_rows].transpose(1, 0, 2).reshape(3, model_width)

    offsets = earlier[:, 0]
    reach_ids = jnp.arange(SEQ_BANDS)
    within = reach_ids[None, :] <= offsets[:, None]
    inputs = tokens.astype(jnp.float32).reshape(row_count, model_width)
    reached = jnp.concatenate([tokens[:, None], passed[:, :, :band_rows]], axis=1)
    normed_all = jnp.where(
        within[:, :, None, None], norm_rows(reached.astype(jnp.float32), gains[0]), 0.0
    ).astype(jnp.bfloat16)
    normed_one = normed_all[:, 0].reshape(row_count, model_width)
    normed_all = normed_all.reshape(SEQ_BANDS * row_count, model_width)
    row_shape = (streams, band_rows, width)
    reach_shape = (streams, SEQ_BANDS, band_rows, width)
    text_shape = (streams, 1, text_rows, width)
    queries = matmul(normed_one, w_query).astype(jnp.bfloat16).reshape(row_shape)
    keys = matmul(normed_all, w_key).astype(jnp.bfloat16).reshape(reach_shape)
    values = matmul(normed_all, w_value).astype(jnp.bfloat16).reshape(reach_shape)
    attended, self_totals = attention(queries, keys, values, offsets, True)
    attended = attended.reshape(row_count, width)
    hidden_one = inputs + head_total(matmul_t(attended, w_self_out), 3)
    normed_two = norm_rows(hidden_one, gains[1]).astype(jnp.bfloat16)
    cross_queries = matmul(normed_two, w_cross).astype(jnp.bfloat16).reshape(row_shape)
    caption = text_states
    for behind in range(1, SEQ_BANDS):
        caption = jnp.where((offsets == behind)[:, None, None], passed[:, behind - 1, band_rows:], caption)
    caption = caption.reshape(streams * text_rows, model_width)
    cross_keys = matmul(caption, w_text_key).astype(jnp.bfloat16).reshape(text_shape)
    cross_values = matmul(caption, w_text_value).astype(jnp.bfloat16).reshape(text_shape)
    crossed, cross_totals = attention(cross_queries, cross_keys, cross_values, offsets, False)
    crossed = crossed.reshape(row_count, width)
    hidden_two = hidden_one + head_total(matmul_t(crossed, w_cross_out), 4)
    normed_three = norm_rows(hidden_two, gains[2]).astype(jnp.bfloat16)
    before = matmul(normed_three, w_up)
    gelu = partial(jax.nn.gelu, approximate=False)
    activated = gelu(before).astype(jnp.bfloat16)
    mlp_out = matmul_t(activated, w_down)
    block_out = (hidden_two + head_total(mlp_out, 5)).astype(jnp.bfloat16).reshape(tokens.shape)

    incoming_low = cotangent.reshape(row_count, model_width)
    incoming = incoming_low.astype(jnp.float32)
    grad_down = inner_t(incoming_low, activated).astype(jnp.bfloat16)
    _, gelu_pull = jax.vjp(gelu, before)
    grad_before = gelu_pull(matmul(incoming_low, w_down))[0].astype(jnp.bfloat16)
    grad_up = inner_t(normed_three, grad_before).astype(jnp.bfloat16)
    grad_before, grad_up, grad_down = lax.optimization_barrier((grad_before, grad_up, grad_down))
    mlp_grad = jnp.stack(
        [lax.psum_scatter(part, "band", scatter_dimension=0, tiled=True) for part in (grad_up, grad_down)]
    ).astype(jnp.float32)
    grad_normed_three = head_total(matmul_t(grad_before, w_up), 6)
    _, pull_three = jax.vjp(norm_rows, hidden_two, gains[2])
    back_two, gain_grad_three = pull_three(grad_normed_three)
    grad_two = incoming + back_two
    grad_two_low = grad_two.astype(jnp.bfloat16)
    grad_cross_out = inner_t(grad_two_low, crossed)
    grad_crossed = matmul(grad_two_low, w_cross_out).astype(jnp.bfloat16).reshape(row_shape)
    grad_cq, grad_ck, grad_cv = attention_back(
        cross_queries, cross_keys, cross_values, offsets, cross_totals, grad_crossed, False
    )
    grad_cq = grad_cq.reshape(row_count, width)
    grad_ck = grad_ck.reshape(streams * text_rows, width)
    grad_cv = grad_cv.reshape(streams * text_rows, width)
    text_part = (matmul_t(grad_ck, w_text_key) + matmul_t(grad_cv, w_text_value)).astype(jnp.bfloat16)
    text_part = text_part.reshape(text_states.shape)
    grad_normed_two = head_total(matmul_t(grad_cq, w_cross), 7)
    _, pull_two = jax.vjp(norm_rows, hidden_one, gains[1])
    back_one, gain_grad_two = pull_two(grad_normed_two)
    grad_one = grad_two + back_one
    grad_one_low = grad_one.astype(jnp.bfloat16)
    grad_self_out = inner_t(grad_one_low, attended)
    grad_attended = matmul(grad_one_low, w_self_out).astype(jnp.bfloat16).reshape(row_shape)
    grad_queries, grad_keys, grad_values = attention_back(
        queries, keys, values, offsets, self_totals, grad_attended, True
    )
    grad_queries = grad_queries.reshape(row_count, width)
    reach_part = matmul_t(grad_keys.reshape(-1, width), w_key) + matmul_t(grad_values.reshape(-1, width), w_value)
    reach_part = reach_part.reshape(streams, SEQ_BANDS, band_rows, model_width)
    own_part = matmul_t(grad_queries, w_query).reshape(tokens.shape) + reach_part[:, 0]
    own_text = jnp.where((offsets == 0)[:, None, None], text_part, 0).astype(jnp.bfloat16)
    sent_text = jnp.where(
        (offsets[:, None] == reach_ids[None, 1:])[:, :, None, None], text_part[:, None], 0
    ).astype(jnp.bfloat16)
    own_back = jnp.concatenate([own_part.astype(jnp.bfloat16), own_text], axis=1)
    sent_back = jnp.concatenate([reach_part[:, 1:].astype(jnp.bfloat16), sent_text], axis=2)
    mine = lax.dynamic_index_in_dim(sent_back, head, 0, keepdims=False)
    other = lax.dynamic_index_in_dim(sent_back, 1 - head, 0, keepdims=False)
    own_there, mine_there = swapped(8, own_back, other)
    own_back = own_back.astype(jnp.float32) + own_there.astype(jnp.float32)
    returned = (mine.astype(jnp.float32) + mine_there.astype(jnp.float32)).astype(jnp.bfloat16)

    flat = lambda part: part.reshape(-1, width)
    grads = [
        part.astype(jnp.bfloat16)
        for part in (
            inner_t(normed_one, grad_queries),
            inner_t(normed_all, flat(grad_keys)),
            inner_t(normed_all, flat(grad_values)),
            inner_t(normed_two, grad_cq),
            inner_t(caption, grad_ck),
            inner_t(caption, grad_cv),
            grad_self_out,
            grad_cross_out,
        )
    ]
    summed, came_back = reduce_grads(bands, grads, returned, 2)
    came_low = came_back.astype(jnp.bfloat16)
    (came_there,) = swapped(9, came_low)
    came_both = jnp.stack([jnp.where(head == 0, came_low, came_there), jnp.where(head == 0, came_there, came_low)])
    back_all = own_back + came_both.astype(jnp.float32)
    grad_normed_one = back_all[:, :band_rows].reshape(row_count, model_width)
    grad_text = back_all[:, band_rows:]
    _, pull_one = jax.vjp(norm_rows, inputs, gains[0])
    back_zero, gain_grad_one = pull_one(grad_normed_one)
    grad_tokens = (grad_one + back_zero).reshape(tokens.shape)

    squares = jnp.sum(summed * summed) + jnp.sum(mlp_grad * mlp_grad)
    gain_rows = jnp.stack([gain_grad_one, gain_grad_two, gain_grad_three]).reshape(-1, LANES)
    tile = jnp.concatenate([gain_rows, jnp.full((8, LANES), squares)])
    tile = mesh_total(bands, tile, 10)
    gain_total = tile[:-8].reshape(3, model_width)
    grad_norm = jnp.sqrt(tile[-1, 0] + jnp.sum(gain_total * gain_total))
    gain_grad = lax.dynamic_slice_in_dim(gain_total, lax.axis_index("band") * shard_rows, shard_rows, 1)
    proj_grad, out_grad = summed[:6], summed[6:8]
    factor = jnp.minimum(1.0, CLIP / grad_norm)
    matrix_rate = 2.0 * D ** (-0.5)
    new_proj = adamw_update(
        proj_master, proj_first, proj_second, proj_grad * factor, matrix_rate, DECAY
    )
    new_out = adamw_update(out_master, out_first, out_second, out_grad * factor, matrix_rate, DECAY)
    new_mlp = adamw_update(mlp_master, mlp_first, mlp_second, mlp_grad * factor, matrix_rate, DECAY)
    new_gain = adamw_update(
        gain_master, gain_first, gain_second, gain_grad * factor, GAIN_RATE, 0.0
    )
    return (
        block_out,
        grad_tokens,
        grad_text,
        grad_norm,
        new_proj[0],
        new_proj[1],
        new_proj[2],
        new_out[0],
        new_out[1],
        new_out[2],
        new_mlp[0],
        new_mlp[1],
        new_mlp[2],
        new_gain[0],
        new_gain[1],
        new_gain[2],
    )


def solution(mesh):
    return jax.shard_map(
        local,
        mesh=mesh,
        in_specs=(
            P(None, "band", None),
            P(None, "band", None),
            P(None, "band", None),
            P(None, "band"),
            P(None, "band", "head"),
            P(None, "band", "head"),
            P(None, "band", "head"),
            P(None, "band"),
            P(None, "band", "head"),
            P(None, "band", "head"),
            P(None, "band", "head"),
            P(None, "band", "head"),
            P(None, "band", "head"),
            P(None, "band", "head"),
            P(None, "band"),
            P(None, "band"),
        ),
        out_specs=(
            P(None, "band", None),
            P(None, "band", None),
            P(None, "band", None),
            P(),
            P(None, "band", "head"),
            P(None, "band", "head"),
            P(None, "band", "head"),
            P(None, "band", "head"),
            P(None, "band", "head"),
            P(None, "band", "head"),
            P(None, "band", "head"),
            P(None, "band", "head"),
            P(None, "band", "head"),
            P(None, "band"),
            P(None, "band"),
            P(None, "band"),
        ),
        check_vma=False,
    )
```

```python
import math
from functools import partial

import jax
import jax.numpy as jnp
from jax import lax
from jax.experimental import pallas as pl
from jax.experimental.pallas import tpu as pltpu
from jax.sharding import PartitionSpec as P

D = 1024
HEAD_DIM = 64
SEQ_BANDS = 4
STEP = 10


EPS = 1e-05
NEG = -1e30
CLIP = 1.0
BETA_ONE = 0.9
BETA_TWO = 0.95
ADAM_EPS = 1e-08
DECAY = 0.1
GAIN_RATE = 0.5
LANES = 128


MESH = pl.DeviceIdType.MESH
ORDERS = ((2, 0, 1), (1, 0, 2))
GROUP = 4
GAP = 2


def band_dims(bands):
    inner = 4 if bands >= 64 else 2
    return (bands // (inner * inner), inner, inner)


def strides_of(dims):
    return (dims[1] * dims[2], dims[2], 1)


def place_of(dims):
    band = lax.axis_index("band")
    return band, (
        band // (dims[1] * dims[2]),
        (band // dims[2]) % dims[1],
        band % dims[2],
    )


def stage_list(dims, order):
    return [(phase, step) for phase in range(3) for step in range(dims[order[phase]] - 1)]


def block_of(ref, lead, place, order, phase, index, columns):
    at = list(place)
    for done in range(phase):
        at[order[done]] = slice(None)
    at[order[phase]] = index
    return ref.at[(*lead, *at, slice(None), columns)]


def greet(dims, place, band, head, extra):
    barrier = pltpu.get_barrier_semaphore()
    strides = strides_of(dims)
    total = jnp.int32(0)
    peers = []
    for axis in range(3):
        for sign in (1, -1):
            there = place[axis] + sign
            peers.append(((there >= 0) & (there < dims[axis]), band + sign * strides[axis], head))
    peers += extra
    for present, peer_band, peer_head in peers:
        @pl.when(present)
        def _():
            pl.semaphore_signal(barrier, inc=1, device_id=(peer_band, peer_head), device_id_type=MESH)
        total = total + present.astype(jnp.int32)
    pl.semaphore_wait(barrier, total)


def gather_kernel(dims, has_context, *refs):
    if has_context:
        (w_ref, gain_ref, ctx_ref, out_ref, gains_ref, ctx_out,
         own_sem, send_sem, recv_sem, gsend, grecv, prev_ref, up_sem, csend, crecv, psend, precv) = refs
    else:
        (w_ref, gain_ref, out_ref, gains_ref, own_sem, send_sem, recv_sem, gsend, grecv) = refs
    band, place = place_of(dims)
    head = lax.axis_index("head")
    strides = strides_of(dims)
    count = w_ref.shape[0]
    half = w_ref.shape[2] // 2
    bands = dims[0] * dims[1] * dims[2]
    true = band >= 0
    extra = []
    if has_context:
        base = (band // GROUP) * GROUP
        mine = band % GROUP
        for shift in range(1, GROUP):
            extra.append((true, base + (mine + shift) % GROUP, head))
        extra.append((band + GROUP < bands, band + GROUP, head))
        extra.append((band >= GROUP, band - GROUP, head))
        extra.append((true, band, 1 - head))
    greet(dims, place, band, head, extra)

    own = [
        pltpu.make_async_copy(w_ref, out_ref.at[:, place[0], place[1], place[2]], own_sem.at[0]),
        pltpu.make_async_copy(gain_ref, gains_ref.at[place[0], place[1], place[2]], own_sem.at[1]),
    ]
    for copy in own:
        copy.start()

    def up_copy():
        return pltpu.make_async_remote_copy(
            ctx_ref, prev_ref, up_sem.at[0], up_sem.at[1], device_id=(band + GROUP, head), device_id_type=MESH
        )

    def peer_copy(back, source):
        return pltpu.make_async_remote_copy(
            source, ctx_out.at[head, back - 1], csend.at[back - 1], crecv.at[back - 1],
            device_id=(base + (mine + back) % GROUP, head), device_id_type=MESH,
        )

    def pair_copy(back):
        return pltpu.make_async_remote_copy(
            ctx_out.at[head, back - 1], ctx_out.at[head, back - 1], psend.at[back - 1], precv.at[back - 1],
            device_id=(band, 1 - head), device_id_type=MESH,
        )

    if has_context:
        @pl.when(band + GROUP < bands)
        def _():
            up_copy().start()

    def piece(color, m, phase, step, way, incoming):
        order = ORDERS[color]
        axis = order[phase]
        size, at = dims[axis], place[axis]
        toward = 1 if way == 0 else -1
        stage = stage_list(dims, order).index((phase, step))
        if incoming:
            index = at - toward * (step + 1)
            present = (index >= 0) & (index < size)
        else:
            index = at - toward * step
            present = (index >= 0) & (index < size) & (at + toward >= 0) & (at + toward < size)
        columns = pl.ds(color * half, half)
        target = (band + toward * strides[axis], head)
        land = block_of(out_ref, (m,), place, order, phase, index, columns)
        source = w_ref.at[m, :, columns] if stage == 0 else land
        copy = pltpu.make_async_remote_copy(
            source, land, send_sem.at[color, stage, way, m], recv_sem.at[color, stage, way, m],
            device_id=target, device_id_type=MESH,
        )
        return present, copy

    def gain_piece(phase, step, way, incoming):
        order = ORDERS[0]
        axis = order[phase]
        size, at = dims[axis], place[axis]
        toward = 1 if way == 0 else -1
        stage = stage_list(dims, order).index((phase, step))
        if incoming:
            index = at - toward * (step + 1)
            present = (index >= 0) & (index < size)
        else:
            index = at - toward * step
            present = (index >= 0) & (index < size) & (at + toward >= 0) & (at + toward < size)
        land = block_of(gains_ref, (), place, order, phase, index, slice(None))
        source = gain_ref if stage == 0 else land
        copy = pltpu.make_async_remote_copy(
            source, land, gsend.at[stage, way], grecv.at[stage, way],
            device_id=(band + toward * strides[axis], head), device_id_type=MESH,
        )
        return present, copy

    stages = [stage_list(dims, order) for order in ORDERS]
    depth = len(stages[0])

    def context_step(t):
        for back in range(1, GROUP):
            @pl.when((t == back - 1) & (mine + back < GROUP))
            def _():
                peer_copy(back, ctx_ref).start()
        @pl.when((t == 2) & (band >= GROUP))
        def _():
            pltpu.make_async_remote_copy(
                ctx_ref, prev_ref, up_sem.at[0], up_sem.at[1], device_id=(band - GROUP, head), device_id_type=MESH
            ).wait_recv()
        for back in range(1, GROUP):
            @pl.when((t == GROUP - back + 1) & (mine + back >= GROUP) & (band >= GROUP))
            def _():
                peer_copy(back, prev_ref).start()
        for back in range(1, GROUP):
            @pl.when((t == 7) & ((mine >= back) | (band >= GROUP)))
            def _():
                peer_copy(back, ctx_ref).wait_recv()
                pair_copy(back).start()

    def gains_step(t):
        for stage in range(depth + 1):
            @pl.when(t == stage)
            def _():
                if stage == 1:
                    for copy in own:
                        copy.wait()
                if stage > 0:
                    for way in range(2):
                        present, copy = gain_piece(*stages[0][stage - 1], way, True)
                        @pl.when(present)
                        def _():
                            copy.wait_recv()
                if stage < depth:
                    for way in range(2):
                        present, copy = gain_piece(*stages[0][stage], way, False)
                        @pl.when(present)
                        def _():
                            copy.start()

    def body(t, carry):
        gains_step(t)
        if has_context:
            context_step(t)
        for stage in range(depth, -1, -1):
            m = t - GAP * stage
            @pl.when((m >= 0) & (m < count))
            def _():
                for color in range(2):
                    if stage > 0:
                        for way in range(2):
                            present, copy = piece(color, m, *stages[color][stage - 1], way, True)
                            @pl.when(present)
                            def _():
                                copy.wait_recv()
                    if stage < depth:
                        for way in range(2):
                            present, copy = piece(color, m, *stages[color][stage], way, False)
                            @pl.when(present)
                            def _():
                                copy.start()
        return carry

    lax.fori_loop(0, count + GAP * depth, body, 0)

    if has_context:
        for back in range(1, GROUP):
            @pl.when((mine >= back) | (band >= GROUP))
            def _():
                pltpu.make_async_remote_copy(
                    ctx_out.at[1 - head, back - 1], ctx_out.at[1 - head, back - 1], psend.at[back - 1],
                    precv.at[back - 1], device_id=(band, 1 - head), device_id_type=MESH,
                ).wait_recv()
                pair_copy(back).wait_send()
            @pl.when((mine + back < GROUP) | (band >= GROUP))
            def _():
                peer_copy(back, ctx_ref).wait_send()
        @pl.when(band + GROUP < bands)
        def _():
            up_copy().wait_send()

    for stage in range(depth):
        for way in range(2):
            present, copy = gain_piece(*stages[0][stage], way, False)
            @pl.when(present)
            def _():
                copy.wait_send()

    def drain(m, carry):
        for stage in range(depth):
            for color in range(2):
                for way in range(2):
                    present, copy = piece(color, m, *stages[color][stage], way, False)
                    @pl.when(present)
                    def _():
                        copy.wait_send()
        return carry

    lax.fori_loop(0, count, drain, 0)


def gather_weights(bands, shard, gain_tile, context, collective_id):
    dims = band_dims(bands)
    count, rows, width = shard.shape
    depth = len(stage_list(dims, ORDERS[0]))
    vmem = pl.BlockSpec(memory_space=pltpu.VMEM)
    anyspace = pl.BlockSpec(memory_space=pl.ANY)
    has_context = context is not None
    out_shape = [
        jax.ShapeDtypeStruct((count, *dims, rows, width), shard.dtype),
        jax.ShapeDtypeStruct((*dims, *gain_tile.shape), gain_tile.dtype),
    ]
    scratch = [
        pltpu.SemaphoreType.DMA((2,)),
        pltpu.SemaphoreType.DMA((2, depth, 2, count)),
        pltpu.SemaphoreType.DMA((2, depth, 2, count)),
        pltpu.SemaphoreType.DMA((depth, 2)),
        pltpu.SemaphoreType.DMA((depth, 2)),
    ]
    args = [shard, gain_tile]
    if has_context:
        args.append(context)
        out_shape.append(jax.ShapeDtypeStruct((2, GROUP - 1, *context.shape), context.dtype))
        scratch += [
            pltpu.VMEM(context.shape, context.dtype),
            pltpu.SemaphoreType.DMA((2,)),
            pltpu.SemaphoreType.DMA((GROUP - 1,)),
            pltpu.SemaphoreType.DMA((GROUP - 1,)),
            pltpu.SemaphoreType.DMA((GROUP - 1,)),
            pltpu.SemaphoreType.DMA((GROUP - 1,)),
        ]
    return pl.pallas_call(
        partial(gather_kernel, dims, has_context),
        out_shape=out_shape,
        in_specs=[vmem] * len(args),
        out_specs=[anyspace] * len(out_shape),
        scratch_shapes=scratch,
        compiler_params=pltpu.CompilerParams(collective_id=collective_id, has_side_effects=True),
        cost_estimate=worth(200),
        name="gather_weights",
    )(*args)


def reduce_kernel(dims, arrays, has_context, *refs):
    sources = [ref.at[one] for ref in refs[:arrays] for one in range(ref.shape[0])]
    count, refs = len(sources), refs[arrays:]
    if has_context:
        (back_ref, out_ref, back_out, gv, load_sem, last_ref, mid_ref, first_ref, send_sem, recv_sem,
         landed, relay, from_up, csend, crecv, up_sem) = refs
    else:
        (out_ref, gv, load_sem, last_ref, mid_ref, first_ref, send_sem, recv_sem) = refs
    band, place = place_of(dims)
    head = lax.axis_index("head")
    strides = strides_of(dims)
    half = sources[0].shape[-1] // 2
    bands = dims[0] * dims[1] * dims[2]
    true = band >= 0
    orders = tuple(order[::-1] for order in ORDERS)
    lands = (last_ref, mid_ref, first_ref)

    def load(m, source):
        return pltpu.make_async_copy(source, gv.at[m], load_sem.at[m])

    for m in range(count):
        load(m, sources[m]).start()

    extra = []
    if has_context:
        base = (band // GROUP) * GROUP
        mine = band % GROUP
        for shift in range(1, GROUP):
            extra.append((true, base + (mine + shift) % GROUP, head))
        extra.append((band + GROUP < bands, band + GROUP, head))
        extra.append((band >= GROUP, band - GROUP, head))
    greet(dims, place, band, head, extra)

    def peer_copy(back):
        return pltpu.make_async_remote_copy(
            back_ref.at[back - 1], landed.at[back - 1], csend.at[back - 1], crecv.at[back - 1],
            device_id=(base + (mine + GROUP - back) % GROUP, head), device_id_type=MESH,
        )

    def down_copy(target):
        return pltpu.make_async_remote_copy(
            relay, from_up, up_sem.at[0], up_sem.at[1], device_id=(target, head), device_id_type=MESH
        )

    def slot(size, step, way):
        return 0 if size == 2 else step * 2 + way

    def own_block(m, color, phase, index):
        order = orders[color]
        at = list(place)
        for later in range(phase + 1, 3):
            at[order[later]] = slice(None)
        at[order[phase]] = index
        return gv.at[(m, *at, slice(None), pl.ds(color * half, half))]

    def landing(m, color, phase, step, way):
        size = dims[orders[color][phase]]
        return lands[phase].at[m, color, slot(size, step, way)]

    def outgoing(m, color, phase, step, way):
        axis = orders[color][phase]
        size, at = dims[axis], place[axis]
        toward = 1 if way == 0 else -1
        rank = at if way == 0 else size - 1 - at
        index = size - 1 - step + at if way == 0 else step + at - (size - 1)
        present = (rank <= step) & (at + toward >= 0) & (at + toward < size)
        stage = stage_list(dims, orders[color]).index((phase, step))
        target = (band + toward * strides[axis], head)

        def copy(source):
            return pltpu.make_async_remote_copy(
                source, landing(m, color, phase, step, way),
                send_sem.at[color, stage, way, m], recv_sem.at[color, stage, way, m],
                device_id=target, device_id_type=MESH,
            )

        return present, rank, index, copy

    def arrived(m, color, phase, step, way):
        axis = orders[color][phase]
        size, at = dims[axis], place[axis]
        before = at - 1 if way == 0 else at + 1
        rank = before if way == 0 else size - 1 - before
        present = (before >= 0) & (before < size) & (rank <= step)
        _, _, _, copy = outgoing(m, color, phase, step, way)
        return present, copy(landing(m, color, phase, step, way))

    def add_into(target, source):
        lead = target.shape[:-2]
        if len(lead) == 0:
            target[...] = target[...] + source[...]
        elif len(lead) == 1:
            for i in range(lead[0]):
                target[i] = target[i] + source[i]
        else:
            for i in range(lead[0]):
                for j in range(lead[1]):
                    target[i, j] = target[i, j] + source[i, j]

    stages = [stage_list(dims, order) for order in orders]
    depth = len(stages[0])

    def send(m, color, phase, step):
        axis = orders[color][phase]
        size = dims[axis]
        for way in range(2):
            present, rank, index, copy = outgoing(m, color, phase, step, way)
            @pl.when(present & (rank == 0))
            def _():
                copy(own_block(m, color, phase, index)).start()
            if step > 0:
                @pl.when(present & (rank > 0))
                def _():
                    from_before = landing(m, color, phase, step - 1, way)
                    add_into(from_before, own_block(m, color, phase, index))
                    copy(from_before).start()

    def settle(m, color, phase, step):
        axis = orders[color][phase]
        size = dims[axis]
        for way in range(2):
            present, copy = arrived(m, color, phase, step, way)
            @pl.when(present)
            def _():
                copy.wait_recv()
                if step == size - 2:
                    landed_here = landing(m, color, phase, step, way)
                    if phase < 2:
                        add_into(own_block(m, color, phase, place[axis]), landed_here)
                    else:
                        columns = pl.ds(color * half, half)
                        if size == 2:
                            own = own_block(m, color, phase, place[axis])
                            out_ref[m, :, columns] = own[...].astype(jnp.float32) + landed_here[...].astype(jnp.float32)
                        else:
                            add_into(own_block(m, color, phase, place[axis]), landed_here)
        if phase == 2 and step == size - 2 and size > 2:
            columns = pl.ds(color * half, half)
            out_ref[m, :, columns] = own_block(m, color, phase, place[axis])[...].astype(jnp.float32)

    def body(t, carry):
        for stage in range(depth, -1, -1):
            m = t - stage
            @pl.when((m >= 0) & (m < count))
            def _():
                if stage == 0:
                    load(m, sources[0]).wait()
                for color in range(2):
                    if stage > 0:
                        settle(m, color, *stages[color][stage - 1])
                    if stage < depth:
                        send(m, color, *stages[color][stage])
        if has_context:
            for back in range(1, GROUP):
                @pl.when((t == back - 1) & ((mine >= back) | (band >= GROUP)))
                def _():
                    peer_copy(back).start()
            @pl.when(t == 4)
            def _():
                for back in range(1, GROUP):
                    @pl.when((mine + back < GROUP) | (band >= GROUP))
                    def _():
                        peer_copy(back).wait_recv()
                @pl.when((mine > 0) & (band >= GROUP))
                def _():
                    for cut in range(0, relay.shape[0], 64):
                        rows = pl.ds(cut, 64)
                        total = landed[GROUP - 2, rows, :].astype(jnp.float32)
                        for back in range(1, GROUP - 1):
                            total = total + jnp.where(mine + back >= GROUP, landed[back - 1, rows, :].astype(jnp.float32), 0.0)
                        relay[rows, :] = total.astype(relay.dtype)
                    down_copy(band - GROUP).start()
            @pl.when(t == 8)
            def _():
                @pl.when((mine > 0) & (band + GROUP < bands))
                def _():
                    down_copy(band + GROUP).wait_recv()
                for cut in range(0, relay.shape[0], 64):
                    rows = pl.ds(cut, 64)
                    total = jnp.where((mine > 0) & (band + GROUP < bands), from_up[rows, :].astype(jnp.float32), 0.0)
                    for back in range(1, GROUP):
                        total = total + jnp.where(mine + back < GROUP, landed[back - 1, rows, :].astype(jnp.float32), 0.0)
                    back_out[rows, :] = total
        return carry

    lax.fori_loop(0, count + depth, body, 0)

    if has_context:
        for back in range(1, GROUP):
            @pl.when((mine >= back) | (band >= GROUP))
            def _():
                peer_copy(back).wait_send()
        @pl.when((mine > 0) & (band >= GROUP))
        def _():
            down_copy(band - GROUP).wait_send()

    def drain(m, carry):
        for stage in range(depth):
            for color in range(2):
                phase, step = stages[color][stage]
                for way in range(2):
                    present, rank, index, copy = outgoing(m, color, phase, step, way)
                    @pl.when(present)
                    def _():
                        copy(own_block(m, color, phase, index)).wait_send()
        return carry

    lax.fori_loop(0, count, drain, 0)


def reduce_grads(bands, grads, returned, collective_id):
    dims = band_dims(bands)
    count = sum(part.shape[0] for part in grads)
    depth_rows, width = grads[0].shape[1:]
    rows = depth_rows // bands
    half = width // 2
    depth = len(stage_list(dims, ORDERS[0]))
    vmem = pl.BlockSpec(memory_space=pltpu.VMEM)
    anyspace = pl.BlockSpec(memory_space=pl.ANY)
    slots = lambda size: 1 if size == 2 else 2 * (size - 1)
    inner = dims[1]
    has_context = returned is not None
    grads = [part.reshape(-1, *dims, rows, width) for part in grads]
    scratch = [
        pltpu.VMEM((count, *grads[0].shape[1:]), jnp.bfloat16),
        pltpu.SemaphoreType.DMA((count,)),
        pltpu.VMEM((count, 2, slots(inner), dims[0], inner, rows, half), jnp.bfloat16),
        pltpu.VMEM((count, 2, slots(dims[0]), inner, rows, half), jnp.bfloat16),
        pltpu.VMEM((count, 2, slots(inner), rows, half), jnp.bfloat16),
        pltpu.SemaphoreType.DMA((2, depth, 2, count)),
        pltpu.SemaphoreType.DMA((2, depth, 2, count)),
    ]
    args = list(grads)
    in_specs = [anyspace] * len(grads)
    out_shape = [jax.ShapeDtypeStruct((count, rows, width), jnp.float32)]
    if has_context:
        args.append(returned)
        in_specs.append(vmem)
        ctx_shape = returned.shape[1:]
        out_shape.append(jax.ShapeDtypeStruct(ctx_shape, jnp.float32))
        scratch += [
            pltpu.VMEM(returned.shape, returned.dtype),
            pltpu.VMEM(ctx_shape, returned.dtype),
            pltpu.VMEM(ctx_shape, returned.dtype),
            pltpu.SemaphoreType.DMA((GROUP - 1,)),
            pltpu.SemaphoreType.DMA((GROUP - 1,)),
            pltpu.SemaphoreType.DMA((2,)),
        ]
    return pl.pallas_call(
        partial(reduce_kernel, dims, len(grads), has_context),
        out_shape=out_shape,
        in_specs=in_specs,
        out_specs=[vmem] * len(out_shape),
        scratch_shapes=scratch,
        compiler_params=pltpu.CompilerParams(
            collective_id=collective_id, has_side_effects=True, vmem_limit_bytes=67043328
        ),
        cost_estimate=worth(1),
        name="reduce_grads",
    )(*args)


def norm_rows(values, gain_row):
    centre = values - jnp.mean(values, axis=-1, keepdims=True)
    spread = jnp.mean(centre * centre, axis=-1, keepdims=True)
    return centre * lax.rsqrt(spread + EPS) * gain_row


def matmul(former, latter):
    return jnp.dot(former, latter, preferred_element_type=jnp.float32)


def matmul_t(former, latter):
    return lax.dot_general(
        former, latter, (((1,), (1,)), ((), ())), preferred_element_type=jnp.float32
    )


def inner_t(former, latter):
    return lax.dot_general(
        former, latter, (((0,), (0,)), ((), ())), preferred_element_type=jnp.float32
    )


def worth(microseconds):
    return pl.CostEstimate(flops=microseconds * 10**9, bytes_accessed=0, transcendentals=0)


def norm_stats(rows):
    centre = rows - jnp.mean(rows, axis=-1, keepdims=True)
    inverse = lax.rsqrt(jnp.mean(centre * centre, axis=-1, keepdims=True) + EPS)
    return centre * inverse, inverse


def norm_pull(rows, gain_row, grad):
    unit, inverse = norm_stats(rows)
    scaled = grad * gain_row
    inner = jnp.mean(scaled * unit, axis=-1, keepdims=True)
    pulled = inverse * (scaled - jnp.mean(scaled, axis=-1, keepdims=True) - unit * inner)
    return pulled, jnp.sum(grad * unit, axis=0, keepdims=True)


def greet_pair():
    pl.semaphore_signal(
        pltpu.get_barrier_semaphore(), inc=1,
        device_id=(lax.axis_index("band"), 1 - lax.axis_index("head")), device_id_type=MESH,
    )


def pair_send(source, target, send_sem, recv_sem):
    return pltpu.make_async_remote_copy(
        source, target, send_sem, recv_sem,
        device_id=(lax.axis_index("band"), 1 - lax.axis_index("head")), device_id_type=MESH,
    )


def mlp_kernel(
    hidden_ref, incoming_ref, gain_ref, up_ref, down_ref,
    block_ref, grad_ref, gain_grad_ref, grad_up_ref, grad_down_ref,
    normed, normed_t, incoming_t, out_sum, back_sum, low, there, send_sem, recv_sem,
):
    step, last = pl.program_id(0), pl.num_programs(0) - 1
    rows = hidden_ref.shape[0]
    tile = 64

    @pl.when(step == 0)
    def _():
        greet_pair()

        def one(at, carry):
            part = pl.ds(pl.multiple_of(at * tile, tile), tile)
            unit, _ = norm_stats(hidden_ref[part, :])
            normed[part, :] = (unit * gain_ref[...]).astype(jnp.bfloat16)
            return carry

        lax.fori_loop(0, rows // tile, one, 0)
        normed_t[...] = normed[...].T
        incoming_t[...] = incoming_ref[...].T
        out_sum[...] = jnp.zeros_like(out_sum)
        back_sum[...] = jnp.zeros_like(back_sum)

    copies = [pair_send(low.at[one], there.at[one], send_sem.at[one], recv_sem.at[one]) for one in range(2)]
    before = matmul(normed[...], up_ref[...])
    share = 0.5 * (1.0 + lax.erf(before * 2.0**-0.5))
    activated = (before * share).astype(jnp.bfloat16)
    out_sum[...] += matmul_t(activated, down_ref[...])

    @pl.when(step == last)
    def _():
        pl.semaphore_wait(pltpu.get_barrier_semaphore(), 1)
        low[0] = out_sum[...].astype(jnp.bfloat16)
        copies[0].start()

    slope = share + before * jnp.exp(before * before * -0.5) * (2.0 * math.pi) ** -0.5
    grad_before = (matmul(incoming_ref[...], down_ref[...]) * slope).astype(jnp.bfloat16)
    back_sum[...] += matmul_t(grad_before, up_ref[...])

    @pl.when(step == last)
    def _():
        low[1] = back_sum[...].astype(jnp.bfloat16)
        copies[1].start()

    grad_down_ref[...] = matmul(incoming_t[...], activated).astype(jnp.bfloat16)
    grad_up_ref[...] = matmul(normed_t[...], grad_before).astype(jnp.bfloat16)

    @pl.when(step == last)
    def _():
        for copy in copies:
            copy.wait()
        gain_grad_ref[...] = jnp.zeros_like(gain_grad_ref)

        def one(at, carry):
            part = pl.ds(pl.multiple_of(at * tile, tile), tile)
            total = lambda which: low[which, part, :].astype(jnp.float32) + there[which, part, :].astype(jnp.float32)
            hidden = hidden_ref[part, :]
            block_ref[part, :] = (hidden + total(0)).astype(jnp.bfloat16)
            pulled, gain_part = norm_pull(hidden, gain_ref[...], total(1))
            grad_ref[part, :] = incoming_ref[part, :].astype(jnp.float32) + pulled
            gain_grad_ref[...] += gain_part
            return carry

        lax.fori_loop(0, rows // tile, one, 0)


def mlp_both_ways(hidden, incoming, gain_row, weights, first, w_down, collective_id):
    rows, width = hidden.shape
    units, cut = w_down.shape[1], weights.shape[2]
    whole = pl.BlockSpec((rows, width), lambda step: (0, 0))
    line = pl.BlockSpec((1, width), lambda step: (0, 0))
    columns = pl.BlockSpec((width, cut), lambda step: (0, step))
    up_matrix = pl.BlockSpec((None, width, cut), lambda step: (first + step, 0, 0))
    grad_matrix = pl.BlockSpec((None, width, cut), lambda step: (step, 0, 0))
    return pl.pallas_call(
        mlp_kernel,
        grid=(units // cut,),
        in_specs=[whole, whole, line, up_matrix, columns],
        out_specs=[whole, whole, line, grad_matrix, columns],
        out_shape=[
            jax.ShapeDtypeStruct((rows, width), jnp.bfloat16),
            jax.ShapeDtypeStruct((rows, width), jnp.float32),
            jax.ShapeDtypeStruct((1, width), jnp.float32),
            jax.ShapeDtypeStruct((units // cut, width, cut), jnp.bfloat16),
            jax.ShapeDtypeStruct((width, units), jnp.bfloat16),
        ],
        scratch_shapes=[
            pltpu.VMEM((rows, width), jnp.bfloat16),
            pltpu.VMEM((width, rows), jnp.bfloat16),
            pltpu.VMEM((width, rows), jnp.bfloat16),
            pltpu.VMEM((rows, width), jnp.float32),
            pltpu.VMEM((rows, width), jnp.float32),
            pltpu.VMEM((2, rows, width), jnp.bfloat16),
            pltpu.VMEM((2, rows, width), jnp.bfloat16),
            pltpu.SemaphoreType.DMA((2,)),
            pltpu.SemaphoreType.DMA((2,)),
        ],
        compiler_params=pltpu.CompilerParams(
            collective_id=collective_id, has_side_effects=True, vmem_limit_bytes=63 * 1024 * 1024
        ),
        cost_estimate=worth(1),
        name="mlp_both_ways",
    )(hidden, incoming, gain_row, weights, w_down)


def row_kernel(backward, follows, *refs):
    refs = list(refs)
    x_ref, w_ref, base_ref, gain_ref = refs[:4]
    rest = refs[4:]
    hidden_ref = rest.pop(0) if backward else None
    next_ref = rest.pop(0) if follows else None
    sum_ref = rest.pop(0)
    low_ref, next_out_ref = (rest.pop(0), rest.pop(0)) if follows else (None, None)
    gain_grad_ref = rest.pop(0) if backward else None
    low, there, send_sem, recv_sem = rest
    rows = x_ref.shape[0]
    cut = rows // send_sem.shape[0]
    greet_pair()

    def part_of(at):
        return pl.ds(pl.multiple_of(at * cut, cut), cut)

    def copy_of(at):
        return pair_send(low.at[part_of(at)], there.at[part_of(at)], send_sem.at[at], recv_sem.at[at])

    for at in range(rows // cut):
        low[part_of(at), :] = matmul_t(x_ref[part_of(at), :], w_ref[...]).astype(jnp.bfloat16)
        if at == 0:
            pl.semaphore_wait(pltpu.get_barrier_semaphore(), 1)
        copy_of(at).start()
    if backward:
        gain_grad_ref[...] = jnp.zeros_like(gain_grad_ref)

    def finish(at, carry):
        part = part_of(at)
        copy_of(at).wait()
        total = low[part, :].astype(jnp.float32) + there[part, :].astype(jnp.float32)
        base = base_ref[part, :].astype(jnp.float32)
        if backward:
            pulled, gain_part = norm_pull(hidden_ref[part, :], gain_ref[...], total)
            gain_grad_ref[...] += gain_part
            result = base + pulled
            passed_on = result.astype(jnp.bfloat16)
        else:
            result = base + total
            if follows:
                passed_on = (norm_stats(result)[0] * gain_ref[...]).astype(jnp.bfloat16)
        sum_ref[part, :] = result
        if follows:
            low_ref[part, :] = passed_on
            next_out_ref[part, :] = matmul(passed_on, next_ref[...]).astype(jnp.bfloat16)
        return carry

    lax.fori_loop(0, rows // cut, finish, 0)


def row_step(x, weights, at, base, gain_row, collective_id, hidden=None, follow=None):
    rows, width = base.shape
    units = x.shape[1]
    backward, follows = hidden is not None, follow is not None
    whole = pl.BlockSpec((rows, width), lambda step: (0, 0))
    narrow = pl.BlockSpec((rows, units), lambda step: (0, 0))
    line = pl.BlockSpec((1, width), lambda step: (0, 0))
    matrix = lambda which: pl.BlockSpec((None, width, units), lambda step: (which, 0, 0))
    args, in_specs = [x, weights, base, gain_row], [narrow, matrix(at), whole, line]
    out_specs, out_shape = [whole], [jax.ShapeDtypeStruct((rows, width), jnp.float32)]
    if backward:
        args.append(hidden)
        in_specs.append(whole)
    if follows:
        args.append(weights)
        in_specs.append(matrix(follow))
        out_specs += [whole, narrow]
        out_shape += [
            jax.ShapeDtypeStruct((rows, width), jnp.bfloat16), jax.ShapeDtypeStruct((rows, units), jnp.bfloat16)
        ]
    if backward:
        out_specs.append(line)
        out_shape.append(jax.ShapeDtypeStruct((1, width), jnp.float32))
    cuts = 4
    return pl.pallas_call(
        partial(row_kernel, backward, follows),
        grid=(1,),
        in_specs=in_specs,
        out_specs=out_specs,
        out_shape=out_shape,
        scratch_shapes=[
            pltpu.VMEM((rows, width), jnp.bfloat16),
            pltpu.VMEM((rows, width), jnp.bfloat16),
            pltpu.SemaphoreType.DMA((cuts,)),
            pltpu.SemaphoreType.DMA((cuts,)),
        ],
        compiler_params=pltpu.CompilerParams(
            collective_id=collective_id, has_side_effects=True, vmem_limit_bytes=63 * 1024 * 1024
        ),
        cost_estimate=worth(1),
        name="row_step",
    )(*args)


def heads_of(block):
    lane = lax.broadcasted_iota(jnp.int32, block.shape, 1) // HEAD_DIM
    return [
        block * (lane == one).astype(jnp.float32).astype(block.dtype) for one in range(LANES // HEAD_DIM)
    ]


def shifted(scores, causal, behind):
    if not causal or behind > 0:
        return scores
    key_ids = lax.broadcasted_iota(jnp.int32, scores.shape, 0)
    query_ids = lax.broadcasted_iota(jnp.int32, scores.shape, 1)
    return jnp.where(key_ids <= query_ids, scores, NEG)


def attend_body(reach, causal, q_ref, k_ref, v_ref, out_ref, total_ref):
    scale = HEAD_DIM**-0.5
    values_t = [v_ref[behind].T for behind in range(reach)]
    outs = []
    for one, q_one in enumerate(heads_of(q_ref[...])):
        scores = [shifted(matmul_t(k_ref[behind], q_one) * scale, causal, behind) for behind in range(reach)]
        top = jnp.max(scores[0], axis=0, keepdims=True)
        for block in scores[1:]:
            top = jnp.maximum(top, jnp.max(block, axis=0, keepdims=True))
        raised = [jnp.exp(block - top) for block in scores]
        total = jnp.sum(raised[0], axis=0, keepdims=True)
        for block in raised[1:]:
            total = total + jnp.sum(block, axis=0, keepdims=True)
        share = 1.0 / total
        mixed = None
        for behind in range(reach):
            part = matmul(values_t[behind], (raised[behind] * share).astype(jnp.bfloat16))
            mixed = part if mixed is None else mixed + part
        outs.append(mixed[one * HEAD_DIM : (one + 1) * HEAD_DIM])
        total_ref[one : one + 1, :] = top + jnp.log(total)
    out_ref[...] = jnp.concatenate(outs, axis=0).T.astype(jnp.bfloat16)


def attend_back_body(reach, causal, q_ref, k_ref, v_ref, total_ref, g_ref, dq_ref, dk_ref, dv_ref):
    scale = HEAD_DIM**-0.5
    keys_t = [k_ref[behind].T for behind in range(reach)]
    q_heads, g_heads = heads_of(q_ref[...]), heads_of(g_ref[...])
    query_grads = []
    key_grads, value_grads = [None] * reach, [None] * reach
    for one in range(len(q_heads)):
        q_one, g_one = q_heads[one], g_heads[one]
        log_total = total_ref[one : one + 1, :]
        probs, grads, centre = [], [], None
        for behind in range(reach):
            scores = shifted(matmul_t(k_ref[behind], q_one) * scale, causal, behind)
            probs.append(jnp.exp(scores - log_total))
            grads.append(matmul_t(v_ref[behind], g_one))
            part = jnp.sum(grads[-1] * probs[-1], axis=0, keepdims=True)
            centre = part if centre is None else centre + part
        query_grad = None
        for behind in range(reach):
            grad_scores = (probs[behind] * (grads[behind] - centre)).astype(jnp.bfloat16)
            part = matmul(keys_t[behind], grad_scores)
            query_grad = part if query_grad is None else query_grad + part
            key_part = matmul(grad_scores, q_one)
            value_part = matmul(probs[behind].astype(jnp.bfloat16), g_one)
            key_grads[behind] = key_part if one == 0 else key_grads[behind] + key_part
            value_grads[behind] = value_part if one == 0 else value_grads[behind] + value_part
        query_grads.append(query_grad[one * HEAD_DIM : (one + 1) * HEAD_DIM])
    dq_ref[...] = (jnp.concatenate(query_grads, axis=0).T * scale).astype(jnp.bfloat16)
    for behind in range(dk_ref.shape[0]):
        if behind < reach:
            dk_ref[behind] = (key_grads[behind] * scale).astype(jnp.bfloat16)
            dv_ref[behind] = value_grads[behind].astype(jnp.bfloat16)
        else:
            dk_ref[behind] = jnp.zeros(dk_ref.shape[1:], dk_ref.dtype)
            dv_ref[behind] = jnp.zeros(dv_ref.shape[1:], dv_ref.dtype)


def by_offset(body, causal, offset_ref, *refs):
    reaches = refs[1].shape[0]
    if reaches == 1:
        body(1, causal, *refs)
        return
    offset = offset_ref[pl.program_id(0)]
    for earlier_bands in range(reaches):
        @pl.when(offset == earlier_bands)
        def _():
            body(earlier_bands + 1, causal, *refs)


def attention_specs(queries, keys):
    rows, reaches, key_rows = queries.shape[1], keys.shape[1], keys.shape[2]
    row_spec = pl.BlockSpec((None, rows, LANES), lambda stream, pair: (stream, 0, pair))
    key_spec = pl.BlockSpec((None, reaches, key_rows, LANES), lambda stream, pair: (stream, 0, 0, pair))
    total_spec = pl.BlockSpec((None, None, 8, rows), lambda stream, pair: (stream, pair, 0, 0))
    return row_spec, key_spec, total_spec


def attention(queries, keys, values, offsets, causal):
    streams, rows, width = queries.shape
    row_spec, key_spec, total_spec = attention_specs(queries, keys)
    return pl.pallas_call(
        partial(by_offset, attend_body, causal),
        grid=(streams, width // LANES),
        in_specs=[pl.BlockSpec(memory_space=pltpu.SMEM), row_spec, key_spec, key_spec],
        out_specs=[row_spec, total_spec],
        out_shape=[
            jax.ShapeDtypeStruct(queries.shape, jnp.bfloat16),
            jax.ShapeDtypeStruct((streams, width // LANES, 8, rows), jnp.float32),
        ],
        cost_estimate=worth(1),
        name="attend",
    )(offsets, queries, keys, values)


def attention_back(queries, keys, values, offsets, totals, grad_out, causal):
    streams, rows, width = queries.shape
    row_spec, key_spec, total_spec = attention_specs(queries, keys)
    return pl.pallas_call(
        partial(by_offset, attend_back_body, causal),
        grid=(streams, width // LANES),
        in_specs=[pl.BlockSpec(memory_space=pltpu.SMEM), row_spec, key_spec, key_spec, total_spec, row_spec],
        out_specs=[row_spec, key_spec, key_spec],
        out_shape=[
            jax.ShapeDtypeStruct(queries.shape, jnp.bfloat16),
            jax.ShapeDtypeStruct(keys.shape, jnp.bfloat16),
            jax.ShapeDtypeStruct(keys.shape, jnp.bfloat16),
        ],
        cost_estimate=worth(1),
        name="attend_back",
    )(offsets, queries, keys, values, totals, grad_out)


def swap_kernel(count, *refs):
    sources, targets = refs[:count], refs[count : 2 * count]
    send_sem, recv_sem = refs[2 * count :]
    band, head = lax.axis_index("band"), lax.axis_index("head")
    barrier = pltpu.get_barrier_semaphore()
    pl.semaphore_signal(barrier, inc=1, device_id=(band, 1 - head), device_id_type=MESH)
    pl.semaphore_wait(barrier, 1)
    copies = [
        pltpu.make_async_remote_copy(
            sources[one], targets[one], send_sem.at[one], recv_sem.at[one],
            device_id=(band, 1 - head), device_id_type=MESH,
        )
        for one in range(count)
    ]
    for copy in copies:
        copy.start()
    for copy in copies:
        copy.wait()


def swapped(collective_id, *arrays):
    vmem = pl.BlockSpec(memory_space=pltpu.VMEM)
    return pl.pallas_call(
        partial(swap_kernel, len(arrays)),
        out_shape=[jax.ShapeDtypeStruct(array.shape, array.dtype) for array in arrays],
        in_specs=[vmem] * len(arrays),
        out_specs=[vmem] * len(arrays),
        scratch_shapes=[pltpu.SemaphoreType.DMA((len(arrays),)), pltpu.SemaphoreType.DMA((len(arrays),))],
        compiler_params=pltpu.CompilerParams(collective_id=collective_id, has_side_effects=True),
        cost_estimate=worth(1),
        name="swap_heads",
    )(*arrays)


def total_kernel(dims, in_ref, out_ref, *scratch):
    slots, (send_sem, recv_sem) = scratch[:4], scratch[4:]
    band, place = place_of(dims)
    head = lax.axis_index("head")
    strides = strides_of(dims)
    lines = [
        (dims[axis], place[axis], lambda at, axis=axis: (band + (at - place[axis]) * strides[axis], head))
        for axis in (2, 1, 0)
    ]
    lines.append((2, head, lambda at: (band, at)))
    barrier = pltpu.get_barrier_semaphore()
    for size, mine, device in lines:
        for shift in range(1, size):
            pl.semaphore_signal(barrier, inc=1, device_id=device((mine + shift) % size), device_id_type=MESH)
    pl.semaphore_wait(barrier, sum(size - 1 for size, _, _ in lines))
    out_ref[...] = in_ref[...]
    rows = in_ref.shape[0]
    for line, (size, mine, device) in enumerate(lines):
        part = pl.ds(0, rows) if line < 3 else pl.ds(rows - 8, 8)
        slots[line][mine] = out_ref[part, :]

        def copy(shift):
            return pltpu.make_async_remote_copy(
                slots[line].at[mine], slots[line].at[mine], send_sem.at[line, shift - 1], recv_sem.at[line, shift - 1],
                device_id=device((mine + shift) % size), device_id_type=MESH,
            )

        def incoming(shift):
            there = (mine + size - shift) % size
            return pltpu.make_async_remote_copy(
                slots[line].at[there], slots[line].at[there], send_sem.at[line, shift - 1], recv_sem.at[line, shift - 1],
                device_id=device(there), device_id_type=MESH,
            )

        for shift in range(1, size):
            copy(shift).start()
        for shift in range(1, size):
            incoming(shift).wait_recv()
        total = slots[line][0]
        for at in range(1, size):
            total = total + slots[line][at]
        out_ref[part, :] = total
        for shift in range(1, size):
            copy(shift).wait_send()


def mesh_total(bands, tile, collective_id):
    dims = band_dims(bands)
    longest = max(*dims, 2)
    vmem = pl.BlockSpec(memory_space=pltpu.VMEM)
    rows = tile.shape[0]
    return pl.pallas_call(
        partial(total_kernel, dims),
        out_shape=jax.ShapeDtypeStruct(tile.shape, tile.dtype),
        in_specs=[vmem],
        out_specs=vmem,
        scratch_shapes=[
            *(pltpu.VMEM((dims[axis], rows, LANES), tile.dtype) for axis in (2, 1, 0)),
            pltpu.VMEM((2, 8, LANES), tile.dtype),
            pltpu.SemaphoreType.DMA((4, longest - 1)),
            pltpu.SemaphoreType.DMA((4, longest - 1)),
        ],
        compiler_params=pltpu.CompilerParams(collective_id=collective_id, has_side_effects=True),
        cost_estimate=worth(1),
        name="mesh_total",
    )(tile)


def adamw_update(weight, moment_one, moment_two, gradient, step_rate, decay_rate):
    moment_one_new = BETA_ONE * moment_one + (1.0 - BETA_ONE) * gradient
    moment_two_new = BETA_TWO * moment_two + (1.0 - BETA_TWO) * gradient * gradient
    unbiased_one = moment_one_new / (1.0 - BETA_ONE**STEP)
    unbiased_two = moment_two_new / (1.0 - BETA_TWO**STEP)
    weight_new = weight - step_rate * (
        unbiased_one / (jnp.sqrt(unbiased_two) + ADAM_EPS) + decay_rate * weight
    )
    return (weight_new, moment_one_new, moment_two_new)


def local(
    tokens,
    text_states,
    cotangent,
    earlier,
    proj_master,
    out_master,
    mlp_master,
    gain_master,
    proj_first,
    proj_second,
    out_first,
    out_second,
    mlp_first,
    mlp_second,
    gain_first,
    gain_second,
):
    streams, band_rows, model_width = tokens.shape
    row_count = streams * band_rows
    text_rows = text_states.shape[1]
    bands, head = lax.axis_size("band"), lax.axis_index("head")
    shard_rows, width = proj_master.shape[1:]
    chunks = mlp_master.shape[2] // width
    up_cut = mlp_master[0].reshape(shard_rows, chunks, width).transpose(1, 0, 2)
    shard = jnp.concatenate([proj_master, out_master, up_cut]).astype(jnp.bfloat16)
    gain_low = gain_master.astype(jnp.bfloat16).astype(jnp.float32)
    gain_tile = jnp.pad(gain_low, ((0, 5), (0, LANES - shard_rows)))
    both = jnp.concatenate([tokens, text_states], axis=1)
    context = lax.dynamic_index_in_dim(both, head, 0, keepdims=False)
    gathered, gain_tiles, passed = gather_weights(bands, shard, gain_tile, context, 1)
    down_low, gain_tiles = lax.optimization_barrier((mlp_master[1].astype(jnp.bfloat16), gain_tiles))
    w_down = lax.all_gather(down_low, "band", axis=0, tiled=True)
    weights = gathered.reshape(shard.shape[0], model_width, width)
    w_query, w_key, w_value, _, w_text_key, w_text_value, _, w_cross_out = (weights[at] for at in range(8))
    gains = gain_tiles.reshape(bands, 8, LANES)[:, :3, :shard_rows].transpose(1, 0, 2).reshape(3, model_width)

    offsets = earlier[:, 0]
    reach_ids = jnp.arange(SEQ_BANDS)
    within = reach_ids[None, :] <= offsets[:, None]
    inputs = tokens.astype(jnp.float32).reshape(row_count, model_width)
    reached = jnp.concatenate([tokens[:, None], passed[:, :, :band_rows]], axis=1)
    normed_all = jnp.where(
        within[:, :, None, None], norm_rows(reached.astype(jnp.float32), gains[0]), 0.0
    ).astype(jnp.bfloat16)
    normed_one = normed_all[:, 0].reshape(row_count, model_width)
    normed_all = normed_all.reshape(SEQ_BANDS * row_count, model_width)
    row_shape = (streams, band_rows, width)
    reach_shape = (streams, SEQ_BANDS, band_rows, width)
    text_shape = (streams, 1, text_rows, width)
    queries = matmul(normed_one, w_query).astype(jnp.bfloat16).reshape(row_shape)
    keys = matmul(normed_all, w_key).astype(jnp.bfloat16).reshape(reach_shape)
    values = matmul(normed_all, w_value).astype(jnp.bfloat16).reshape(reach_shape)
    attended, self_totals = attention(queries, keys, values, offsets, True)
    attended = attended.reshape(row_count, width)
    hidden_one, normed_two, cross_queries = row_step(
        attended, weights, 6, tokens.reshape(row_count, model_width), gains[1:2], 3, follow=3
    )
    cross_queries = cross_queries.reshape(row_shape)
    caption = text_states
    for behind in range(1, SEQ_BANDS):
        caption = jnp.where((offsets == behind)[:, None, None], passed[:, behind - 1, band_rows:], caption)
    caption = caption.reshape(streams * text_rows, model_width)
    cross_keys = matmul(caption, w_text_key).astype(jnp.bfloat16).reshape(text_shape)
    cross_values = matmul(caption, w_text_value).astype(jnp.bfloat16).reshape(text_shape)
    crossed, cross_totals = attention(cross_queries, cross_keys, cross_values, offsets, False)
    crossed = crossed.reshape(row_count, width)
    (hidden_two,) = row_step(crossed, weights, 7, hidden_one, gains[2:3], 4)
    incoming = cotangent.reshape(row_count, model_width)
    block_out, grad_two, gain_grad_three, grad_up, grad_down = mlp_both_ways(
        hidden_two, incoming, gains[2:3], weights, 8, w_down, 5
    )
    block_out = block_out.reshape(tokens.shape)
    gain_grad_three = gain_grad_three[0]
    down_sum = lax.psum_scatter(grad_down, "band", scatter_dimension=0, tiled=True).astype(jnp.float32)
    grad_two_low = grad_two.astype(jnp.bfloat16)
    grad_cross_out = inner_t(grad_two_low, crossed)
    grad_crossed = matmul(grad_two_low, w_cross_out).astype(jnp.bfloat16).reshape(row_shape)
    grad_cq, grad_ck, grad_cv = attention_back(
        cross_queries, cross_keys, cross_values, offsets, cross_totals, grad_crossed, False
    )
    grad_cq = grad_cq.reshape(row_count, width)
    grad_ck = grad_ck.reshape(streams * text_rows, width)
    grad_cv = grad_cv.reshape(streams * text_rows, width)
    text_part = (matmul_t(grad_ck, w_text_key) + matmul_t(grad_cv, w_text_value)).astype(jnp.bfloat16)
    text_part = text_part.reshape(text_states.shape)
    grad_one, grad_one_low, grad_attended, gain_grad_two = row_step(
        grad_cq, weights, 3, grad_two, gains[1:2], 7, hidden=hidden_one, follow=6
    )
    gain_grad_two = gain_grad_two[0]
    grad_self_out = inner_t(grad_one_low, attended)
    grad_attended = grad_attended.reshape(row_shape)
    grad_queries, grad_keys, grad_values = attention_back(
        queries, keys, values, offsets, self_totals, grad_attended, True
    )
    grad_queries = grad_queries.reshape(row_count, width)
    reach_part = matmul_t(grad_keys.reshape(-1, width), w_key) + matmul_t(grad_values.reshape(-1, width), w_value)
    reach_part = reach_part.reshape(streams, SEQ_BANDS, band_rows, model_width)
    own_part = matmul_t(grad_queries, w_query).reshape(tokens.shape) + reach_part[:, 0]
    own_text = jnp.where((offsets == 0)[:, None, None], text_part, 0).astype(jnp.bfloat16)
    sent_text = jnp.where(
        (offsets[:, None] == reach_ids[None, 1:])[:, :, None, None], text_part[:, None], 0
    ).astype(jnp.bfloat16)
    own_back = jnp.concatenate([own_part.astype(jnp.bfloat16), own_text], axis=1)
    sent_back = jnp.concatenate([reach_part[:, 1:].astype(jnp.bfloat16), sent_text], axis=2)
    mine = lax.dynamic_index_in_dim(sent_back, head, 0, keepdims=False)
    other = lax.dynamic_index_in_dim(sent_back, 1 - head, 0, keepdims=False)
    own_there, mine_there = swapped(8, own_back, other)
    own_back = own_back.astype(jnp.float32) + own_there.astype(jnp.float32)
    returned = (mine.astype(jnp.float32) + mine_there.astype(jnp.float32)).astype(jnp.bfloat16)

    flat = lambda part: part.reshape(-1, width)
    grads = [
        part.astype(jnp.bfloat16)[None]
        for part in (
            inner_t(normed_one, grad_queries),
            inner_t(normed_all, flat(grad_keys)),
            inner_t(normed_all, flat(grad_values)),
            inner_t(normed_two, grad_cq),
            inner_t(caption, grad_ck),
            inner_t(caption, grad_cv),
            grad_self_out,
            grad_cross_out,
        )
    ]
    grads.append(grad_up)
    returned, down_sum = lax.optimization_barrier((returned, down_sum))
    summed, came_back = reduce_grads(bands, grads, returned, 2)
    came_low = came_back.astype(jnp.bfloat16)
    (came_there,) = swapped(9, came_low)
    came_both = jnp.stack([jnp.where(head == 0, came_low, came_there), jnp.where(head == 0, came_there, came_low)])
    back_all = own_back + came_both.astype(jnp.float32)
    grad_normed_one = back_all[:, :band_rows].reshape(row_count, model_width)
    grad_text = back_all[:, band_rows:]
    _, pull_one = jax.vjp(norm_rows, inputs, gains[0])
    back_zero, gain_grad_one = pull_one(grad_normed_one)
    grad_tokens = (grad_one + back_zero).reshape(tokens.shape)

    squares = jnp.sum(summed * summed) + jnp.sum(down_sum * down_sum)
    gain_rows = jnp.stack([gain_grad_one, gain_grad_two, gain_grad_three]).reshape(-1, LANES)
    tile = jnp.concatenate([gain_rows, jnp.full((8, LANES), squares)])
    tile = mesh_total(bands, tile, 10)
    gain_total = tile[:-8].reshape(3, model_width)
    grad_norm = jnp.sqrt(tile[-1, 0] + jnp.sum(gain_total * gain_total))
    gain_grad = lax.dynamic_slice_in_dim(gain_total, lax.axis_index("band") * shard_rows, shard_rows, 1)
    proj_grad, out_grad = summed[:6], summed[6:8]
    up_sum = summed[8:].transpose(1, 0, 2).reshape(down_sum.shape)
    mlp_grad = jnp.stack([up_sum, down_sum])
    factor = jnp.minimum(1.0, CLIP / grad_norm)
    matrix_rate = 2.0 * D ** (-0.5)
    new_proj = adamw_update(
        proj_master, proj_first, proj_second, proj_grad * factor, matrix_rate, DECAY
    )
    new_out = adamw_update(out_master, out_first, out_second, out_grad * factor, matrix_rate, DECAY)
    new_mlp = adamw_update(mlp_master, mlp_first, mlp_second, mlp_grad * factor, matrix_rate, DECAY)
    new_gain = adamw_update(
        gain_master, gain_first, gain_second, gain_grad * factor, GAIN_RATE, 0.0
    )
    return (
        block_out,
        grad_tokens,
        grad_text,
        grad_norm,
        new_proj[0],
        new_proj[1],
        new_proj[2],
        new_out[0],
        new_out[1],
        new_out[2],
        new_mlp[0],
        new_mlp[1],
        new_mlp[2],
        new_gain[0],
        new_gain[1],
        new_gain[2],
    )


def solution(mesh):
    return jax.shard_map(
        local,
        mesh=mesh,
        in_specs=(
            P(None, "band", None),
            P(None, "band", None),
            P(None, "band", None),
            P(None, "band"),
            P(None, "band", "head"),
            P(None, "band", "head"),
            P(None, "band", "head"),
            P(None, "band"),
            P(None, "band", "head"),
            P(None, "band", "head"),
            P(None, "band", "head"),
            P(None, "band", "head"),
            P(None, "band", "head"),
            P(None, "band", "head"),
            P(None, "band"),
            P(None, "band"),
        ),
        out_specs=(
            P(None, "band", None),
            P(None, "band", None),
            P(None, "band", None),
            P(),
            P(None, "band", "head"),
            P(None, "band", "head"),
            P(None, "band", "head"),
            P(None, "band", "head"),
            P(None, "band", "head"),
            P(None, "band", "head"),
            P(None, "band", "head"),
            P(None, "band", "head"),
            P(None, "band", "head"),
            P(None, "band"),
            P(None, "band"),
            P(None, "band"),
        ),
        check_vma=False,
    )
```

```python
import math
from functools import partial

import jax
import jax.numpy as jnp
from jax import lax
from jax.experimental import pallas as pl
from jax.experimental.pallas import tpu as pltpu
from jax.sharding import PartitionSpec as P

D = 1024
HEAD_DIM = 64
SEQ_BANDS = 4
STEP = 10


EPS = 1e-05
NEG = -1e30
CLIP = 1.0
BETA_ONE = 0.9
BETA_TWO = 0.95
ADAM_EPS = 1e-08
DECAY = 0.1
GAIN_RATE = 0.5
LANES = 128


MESH = pl.DeviceIdType.MESH
ORDERS = ((2, 0, 1), (1, 0, 2))
GROUP = 4
PIECES = 6
GAP = 2


def band_dims(bands):
    inner = 4 if bands >= 64 else 2
    return (bands // (inner * inner), inner, inner)


def strides_of(dims):
    return (dims[1] * dims[2], dims[2], 1)


def place_of(dims):
    band = lax.axis_index("band")
    return band, (
        band // (dims[1] * dims[2]),
        (band // dims[2]) % dims[1],
        band % dims[2],
    )


def stage_list(dims, order):
    return [(phase, step) for phase in range(3) for step in range(dims[order[phase]] - 1)]


def block_of(ref, lead, place, order, phase, index, columns):
    at = list(place)
    for done in range(phase):
        at[order[done]] = slice(None)
    at[order[phase]] = index
    return ref.at[(*lead, *at, slice(None), columns)]


def greet(dims, place, band, head, extra):
    barrier = pltpu.get_barrier_semaphore()
    strides = strides_of(dims)
    total = jnp.int32(0)
    peers = []
    for axis in range(3):
        for sign in (1, -1):
            there = place[axis] + sign
            peers.append(((there >= 0) & (there < dims[axis]), band + sign * strides[axis], head))
    peers += extra
    for present, peer_band, peer_head in peers:
        @pl.when(present)
        def _():
            pl.semaphore_signal(barrier, inc=1, device_id=(peer_band, peer_head), device_id_type=MESH)
        total = total + present.astype(jnp.int32)
    pl.semaphore_wait(barrier, total)


def gather_kernel(dims, has_context, *refs):
    if has_context:
        (w_ref, gain_ref, ctx_ref, out_ref, gains_ref, ctx_out,
         own_sem, send_sem, recv_sem, gsend, grecv, prev_ref, up_sem, csend, crecv, psend, precv) = refs
    else:
        (w_ref, gain_ref, out_ref, gains_ref, own_sem, send_sem, recv_sem, gsend, grecv) = refs
    band, place = place_of(dims)
    head = lax.axis_index("head")
    strides = strides_of(dims)
    count = w_ref.shape[0]
    half = w_ref.shape[2] // 2
    bands = dims[0] * dims[1] * dims[2]
    true = band >= 0
    extra = []
    if has_context:
        base = (band // GROUP) * GROUP
        mine = band % GROUP
        for shift in range(1, GROUP):
            extra.append((true, base + (mine + shift) % GROUP, head))
        extra.append((band + GROUP < bands, band + GROUP, head))
        extra.append((band >= GROUP, band - GROUP, head))
        extra.append((true, band, 1 - head))
    greet(dims, place, band, head, extra)

    own = [
        pltpu.make_async_copy(w_ref, out_ref.at[:, place[0], place[1], place[2]], own_sem.at[0]),
        pltpu.make_async_copy(gain_ref, gains_ref.at[place[0], place[1], place[2]], own_sem.at[1]),
    ]
    for copy in own:
        copy.start()

    def up_copy():
        return pltpu.make_async_remote_copy(
            ctx_ref, prev_ref, up_sem.at[0], up_sem.at[1], device_id=(band + GROUP, head), device_id_type=MESH
        )

    def peer_copy(back, piece_at, source):
        cut = ctx_ref.shape[0] // PIECES
        rows = pl.ds(piece_at * cut, cut)
        return pltpu.make_async_remote_copy(
            source.at[rows], ctx_out.at[head, back - 1, rows], csend.at[back - 1, piece_at], crecv.at[back - 1, piece_at],
            device_id=(base + (mine + back) % GROUP, head), device_id_type=MESH,
        )

    def pair_copy(back):
        return pltpu.make_async_remote_copy(
            ctx_out.at[head, back - 1], ctx_out.at[head, back - 1], psend.at[back - 1], precv.at[back - 1],
            device_id=(band, 1 - head), device_id_type=MESH,
        )

    if has_context:
        @pl.when(band + GROUP < bands)
        def _():
            up_copy().start()

    def piece(color, m, phase, step, way, incoming):
        order = ORDERS[color]
        axis = order[phase]
        size, at = dims[axis], place[axis]
        toward = 1 if way == 0 else -1
        stage = stage_list(dims, order).index((phase, step))
        if incoming:
            index = at - toward * (step + 1)
            present = (index >= 0) & (index < size)
        else:
            index = at - toward * step
            present = (index >= 0) & (index < size) & (at + toward >= 0) & (at + toward < size)
        columns = pl.ds(color * half, half)
        target = (band + toward * strides[axis], head)
        land = block_of(out_ref, (m,), place, order, phase, index, columns)
        source = w_ref.at[m, :, columns] if stage == 0 else land
        copy = pltpu.make_async_remote_copy(
            source, land, send_sem.at[color, stage, way, m], recv_sem.at[color, stage, way, m],
            device_id=target, device_id_type=MESH,
        )
        return present, copy

    def gain_piece(phase, step, way, incoming):
        order = ORDERS[0]
        axis = order[phase]
        size, at = dims[axis], place[axis]
        toward = 1 if way == 0 else -1
        stage = stage_list(dims, order).index((phase, step))
        if incoming:
            index = at - toward * (step + 1)
            present = (index >= 0) & (index < size)
        else:
            index = at - toward * step
            present = (index >= 0) & (index < size) & (at + toward >= 0) & (at + toward < size)
        land = block_of(gains_ref, (), place, order, phase, index, slice(None))
        source = gain_ref if stage == 0 else land
        copy = pltpu.make_async_remote_copy(
            source, land, gsend.at[stage, way], grecv.at[stage, way],
            device_id=(band + toward * strides[axis], head), device_id_type=MESH,
        )
        return present, copy

    stages = [stage_list(dims, order) for order in ORDERS]
    depth = len(stages[0])

    def context_step(t):
        for one in range(PIECES):
            @pl.when(t == one)
            def _():
                for back in range(1, GROUP):
                    @pl.when(mine + back < GROUP)
                    def _():
                        peer_copy(back, one, ctx_ref).start()
        @pl.when((t == 4) & (band >= GROUP))
        def _():
            pltpu.make_async_remote_copy(
                ctx_ref, prev_ref, up_sem.at[0], up_sem.at[1], device_id=(band - GROUP, head), device_id_type=MESH
            ).wait_recv()
        for one in range(PIECES):
            @pl.when((t == 4 + one) & (band >= GROUP))
            def _():
                for back in range(1, GROUP):
                    @pl.when(mine + back >= GROUP)
                    def _():
                        peer_copy(back, one, prev_ref).start()
        @pl.when(t == 13)
        def _():
            for back in range(1, GROUP):
                @pl.when((mine >= back) | (band >= GROUP))
                def _():
                    for one in range(PIECES):
                        peer_copy(back, one, ctx_ref).wait_recv()
                    pair_copy(back).start()

    def gains_step(t):
        for stage in range(depth + 1):
            @pl.when(t == stage)
            def _():
                if stage == 1:
                    for copy in own:
                        copy.wait()
                if stage > 0:
                    for way in range(2):
                        present, copy = gain_piece(*stages[0][stage - 1], way, True)
                        @pl.when(present)
                        def _():
                            copy.wait_recv()
                if stage < depth:
                    for way in range(2):
                        present, copy = gain_piece(*stages[0][stage], way, False)
                        @pl.when(present)
                        def _():
                            copy.start()

    def body(t, carry):
        gains_step(t)
        if has_context:
            context_step(t)
        for stage in range(depth, -1, -1):
            m = t - GAP * stage
            @pl.when((m >= 0) & (m < count))
            def _():
                for color in range(2):
                    if stage > 0:
                        for way in range(2):
                            present, copy = piece(color, m, *stages[color][stage - 1], way, True)
                            @pl.when(present)
                            def _():
                                copy.wait_recv()
                    if stage < depth:
                        for way in range(2):
                            present, copy = piece(color, m, *stages[color][stage], way, False)
                            @pl.when(present)
                            def _():
                                copy.start()
        return carry

    lax.fori_loop(0, count + GAP * depth, body, 0)

    if has_context:
        for back in range(1, GROUP):
            @pl.when((mine >= back) | (band >= GROUP))
            def _():
                pltpu.make_async_remote_copy(
                    ctx_out.at[1 - head, back - 1], ctx_out.at[1 - head, back - 1], psend.at[back - 1],
                    precv.at[back - 1], device_id=(band, 1 - head), device_id_type=MESH,
                ).wait_recv()
                pair_copy(back).wait_send()
            @pl.when((mine + back < GROUP) | (band >= GROUP))
            def _():
                for one in range(PIECES):
                    peer_copy(back, one, ctx_ref).wait_send()
        @pl.when(band + GROUP < bands)
        def _():
            up_copy().wait_send()

    for stage in range(depth):
        for way in range(2):
            present, copy = gain_piece(*stages[0][stage], way, False)
            @pl.when(present)
            def _():
                copy.wait_send()

    def drain(m, carry):
        for stage in range(depth):
            for color in range(2):
                for way in range(2):
                    present, copy = piece(color, m, *stages[color][stage], way, False)
                    @pl.when(present)
                    def _():
                        copy.wait_send()
        return carry

    lax.fori_loop(0, count, drain, 0)


def gather_weights(bands, shard, gain_tile, context, collective_id):
    dims = band_dims(bands)
    count, rows, width = shard.shape
    depth = len(stage_list(dims, ORDERS[0]))
    vmem = pl.BlockSpec(memory_space=pltpu.VMEM)
    anyspace = pl.BlockSpec(memory_space=pl.ANY)
    has_context = context is not None
    out_shape = [
        jax.ShapeDtypeStruct((count, *dims, rows, width), shard.dtype),
        jax.ShapeDtypeStruct((*dims, *gain_tile.shape), gain_tile.dtype),
    ]
    scratch = [
        pltpu.SemaphoreType.DMA((2,)),
        pltpu.SemaphoreType.DMA((2, depth, 2, count)),
        pltpu.SemaphoreType.DMA((2, depth, 2, count)),
        pltpu.SemaphoreType.DMA((depth, 2)),
        pltpu.SemaphoreType.DMA((depth, 2)),
    ]
    args = [shard, gain_tile]
    if has_context:
        args.append(context)
        out_shape.append(jax.ShapeDtypeStruct((2, GROUP - 1, *context.shape), context.dtype))
        scratch += [
            pltpu.VMEM(context.shape, context.dtype),
            pltpu.SemaphoreType.DMA((2,)),
            pltpu.SemaphoreType.DMA((GROUP - 1, PIECES)),
            pltpu.SemaphoreType.DMA((GROUP - 1, PIECES)),
            pltpu.SemaphoreType.DMA((GROUP - 1,)),
            pltpu.SemaphoreType.DMA((GROUP - 1,)),
        ]
    return pl.pallas_call(
        partial(gather_kernel, dims, has_context),
        out_shape=out_shape,
        in_specs=[vmem] * len(args),
        out_specs=[anyspace] * len(out_shape),
        scratch_shapes=scratch,
        compiler_params=pltpu.CompilerParams(collective_id=collective_id, has_side_effects=True),
        cost_estimate=worth(200),
        name="gather_weights",
    )(*args)


def reduce_kernel(dims, arrays, has_context, *refs):
    sources = [ref.at[one] for ref in refs[:arrays] for one in range(ref.shape[0])]
    count, refs = len(sources), refs[arrays:]
    if has_context:
        (back_ref, out_ref, back_out, gv, load_sem, last_ref, mid_ref, first_ref, send_sem, recv_sem,
         landed, relay, from_up, csend, crecv, up_sem, pair_sem) = refs
    else:
        (out_ref, gv, load_sem, last_ref, mid_ref, first_ref, send_sem, recv_sem) = refs
    band, place = place_of(dims)
    head = lax.axis_index("head")
    strides = strides_of(dims)
    half = sources[0].shape[-1] // 2
    bands = dims[0] * dims[1] * dims[2]
    true = band >= 0
    orders = tuple(order[::-1] for order in ORDERS)
    lands = (last_ref, mid_ref, first_ref)

    def load(m, source):
        return pltpu.make_async_copy(source, gv.at[m], load_sem.at[m])

    for m in range(count):
        load(m, sources[m]).start()

    extra = []
    if has_context:
        base = (band // GROUP) * GROUP
        mine = band % GROUP
        for shift in range(1, GROUP):
            extra.append((true, base + (mine + shift) % GROUP, head))
        extra.append((band + GROUP < bands, band + GROUP, head))
        extra.append((band >= GROUP, band - GROUP, head))
        extra.append((true, band, 1 - head))
    greet(dims, place, band, head, extra)

    def peer_copy(back, piece_at):
        cut = relay.shape[0] // PIECES
        rows = pl.ds(piece_at * cut, cut)
        return pltpu.make_async_remote_copy(
            back_ref.at[back - 1, rows], landed.at[back - 1, rows],
            csend.at[back - 1, piece_at], crecv.at[back - 1, piece_at],
            device_id=(base + (mine + GROUP - back) % GROUP, head), device_id_type=MESH,
        )

    def down_copy(target):
        return pltpu.make_async_remote_copy(
            relay, from_up, up_sem.at[0], up_sem.at[1], device_id=(target, head), device_id_type=MESH
        )

    def pair_copy(stream):
        return pltpu.make_async_remote_copy(
            back_out.at[stream], back_out.at[stream], pair_sem.at[0], pair_sem.at[1],
            device_id=(band, 1 - head), device_id_type=MESH,
        )

    def slot(size, step, way):
        return 0 if size == 2 else step * 2 + way

    def own_block(m, color, phase, index):
        order = orders[color]
        at = list(place)
        for later in range(phase + 1, 3):
            at[order[later]] = slice(None)
        at[order[phase]] = index
        return gv.at[(m, *at, slice(None), pl.ds(color * half, half))]

    def landing(m, color, phase, step, way):
        size = dims[orders[color][phase]]
        return lands[phase].at[m, color, slot(size, step, way)]

    def outgoing(m, color, phase, step, way):
        axis = orders[color][phase]
        size, at = dims[axis], place[axis]
        toward = 1 if way == 0 else -1
        rank = at if way == 0 else size - 1 - at
        index = size - 1 - step + at if way == 0 else step + at - (size - 1)
        present = (rank <= step) & (at + toward >= 0) & (at + toward < size)
        stage = stage_list(dims, orders[color]).index((phase, step))
        target = (band + toward * strides[axis], head)

        def copy(source):
            return pltpu.make_async_remote_copy(
                source, landing(m, color, phase, step, way),
                send_sem.at[color, stage, way, m], recv_sem.at[color, stage, way, m],
                device_id=target, device_id_type=MESH,
            )

        return present, rank, index, copy

    def arrived(m, color, phase, step, way):
        axis = orders[color][phase]
        size, at = dims[axis], place[axis]
        before = at - 1 if way == 0 else at + 1
        rank = before if way == 0 else size - 1 - before
        present = (before >= 0) & (before < size) & (rank <= step)
        _, _, _, copy = outgoing(m, color, phase, step, way)
        return present, copy(landing(m, color, phase, step, way))

    def add_into(target, source):
        lead = target.shape[:-2]
        if len(lead) == 0:
            target[...] = target[...] + source[...]
        elif len(lead) == 1:
            for i in range(lead[0]):
                target[i] = target[i] + source[i]
        else:
            for i in range(lead[0]):
                for j in range(lead[1]):
                    target[i, j] = target[i, j] + source[i, j]

    stages = [stage_list(dims, order) for order in orders]
    depth = len(stages[0])

    def send(m, color, phase, step):
        axis = orders[color][phase]
        size = dims[axis]
        for way in range(2):
            present, rank, index, copy = outgoing(m, color, phase, step, way)
            @pl.when(present & (rank == 0))
            def _():
                copy(own_block(m, color, phase, index)).start()
            if step > 0:
                @pl.when(present & (rank > 0))
                def _():
                    from_before = landing(m, color, phase, step - 1, way)
                    add_into(from_before, own_block(m, color, phase, index))
                    copy(from_before).start()

    def settle(m, color, phase, step):
        axis = orders[color][phase]
        size = dims[axis]
        for way in range(2):
            present, copy = arrived(m, color, phase, step, way)
            @pl.when(present)
            def _():
                copy.wait_recv()
                if step == size - 2:
                    landed_here = landing(m, color, phase, step, way)
                    if phase < 2:
                        add_into(own_block(m, color, phase, place[axis]), landed_here)
                    else:
                        columns = pl.ds(color * half, half)
                        if size == 2:
                            own = own_block(m, color, phase, place[axis])
                            out_ref[m, :, columns] = own[...].astype(jnp.float32) + landed_here[...].astype(jnp.float32)
                        else:
                            add_into(own_block(m, color, phase, place[axis]), landed_here)
        if phase == 2 and step == size - 2 and size > 2:
            columns = pl.ds(color * half, half)
            out_ref[m, :, columns] = own_block(m, color, phase, place[axis])[...].astype(jnp.float32)

    def body(t, carry):
        for stage in range(depth, -1, -1):
            m = t - stage
            @pl.when((m >= 0) & (m < count))
            def _():
                if stage == 0:
                    load(m, sources[0]).wait()
                for color in range(2):
                    if stage > 0:
                        settle(m, color, *stages[color][stage - 1])
                    if stage < depth:
                        send(m, color, *stages[color][stage])
        if has_context:
            for one in range(PIECES):
                @pl.when(t == one)
                def _():
                    for back in range(1, GROUP):
                        @pl.when((mine >= back) | (band >= GROUP))
                        def _():
                            peer_copy(back, one).start()
            @pl.when(t == 8)
            def _():
                for back in range(1, GROUP):
                    @pl.when((mine + back < GROUP) | (band >= GROUP))
                    def _():
                        for one in range(PIECES):
                            peer_copy(back, one).wait_recv()
                @pl.when((mine > 0) & (band >= GROUP))
                def _():
                    def relayed(at, inner):
                        rows = pl.ds(pl.multiple_of(at * 64, 64), 64)
                        total = landed[GROUP - 2, rows, :].astype(jnp.float32)
                        for back in range(1, GROUP - 1):
                            total = total + jnp.where(mine + back >= GROUP, landed[back - 1, rows, :].astype(jnp.float32), 0.0)
                        relay[rows, :] = total.astype(relay.dtype)
                        return inner

                    lax.fori_loop(0, relay.shape[0] // 64, relayed, 0)
                    down_copy(band - GROUP).start()
            @pl.when(t == 13)
            def _():
                @pl.when((mine > 0) & (band + GROUP < bands))
                def _():
                    down_copy(band + GROUP).wait_recv()

                def settled(at, inner):
                    rows = pl.ds(pl.multiple_of(at * 64, 64), 64)
                    total = jnp.where((mine > 0) & (band + GROUP < bands), from_up[rows, :].astype(jnp.float32), 0.0)
                    for back in range(1, GROUP):
                        total = total + jnp.where(mine + back < GROUP, landed[back - 1, rows, :].astype(jnp.float32), 0.0)
                    back_out[head, rows, :] = total.astype(back_out.dtype)
                    return inner

                lax.fori_loop(0, relay.shape[0] // 64, settled, 0)
                pair_copy(head).start()
        return carry

    lax.fori_loop(0, count + depth, body, 0)

    if has_context:
        for back in range(1, GROUP):
            @pl.when((mine >= back) | (band >= GROUP))
            def _():
                for one in range(PIECES):
                    peer_copy(back, one).wait_send()
        @pl.when((mine > 0) & (band >= GROUP))
        def _():
            down_copy(band - GROUP).wait_send()
        pair_copy(head).wait_send()
        pair_copy(1 - head).wait_recv()

    def drain(m, carry):
        for stage in range(depth):
            for color in range(2):
                phase, step = stages[color][stage]
                for way in range(2):
                    present, rank, index, copy = outgoing(m, color, phase, step, way)
                    @pl.when(present)
                    def _():
                        copy(own_block(m, color, phase, index)).wait_send()
        return carry

    lax.fori_loop(0, count, drain, 0)


def reduce_grads(bands, grads, returned, collective_id):
    dims = band_dims(bands)
    count = sum(part.shape[0] for part in grads)
    depth_rows, width = grads[0].shape[1:]
    rows = depth_rows // bands
    half = width // 2
    depth = len(stage_list(dims, ORDERS[0]))
    vmem = pl.BlockSpec(memory_space=pltpu.VMEM)
    anyspace = pl.BlockSpec(memory_space=pl.ANY)
    slots = lambda size: 1 if size == 2 else 2 * (size - 1)
    inner = dims[1]
    has_context = returned is not None
    grads = [part.reshape(-1, *dims, rows, width) for part in grads]
    scratch = [
        pltpu.VMEM((count, *grads[0].shape[1:]), jnp.bfloat16),
        pltpu.SemaphoreType.DMA((count,)),
        pltpu.VMEM((count, 2, slots(inner), dims[0], inner, rows, half), jnp.bfloat16),
        pltpu.VMEM((count, 2, slots(dims[0]), inner, rows, half), jnp.bfloat16),
        pltpu.VMEM((count, 2, slots(inner), rows, half), jnp.bfloat16),
        pltpu.SemaphoreType.DMA((2, depth, 2, count)),
        pltpu.SemaphoreType.DMA((2, depth, 2, count)),
    ]
    args = list(grads)
    in_specs = [anyspace] * len(grads)
    out_shape = [jax.ShapeDtypeStruct((count, rows, width), jnp.float32)]
    if has_context:
        args.append(returned)
        in_specs.append(vmem)
        ctx_shape = returned.shape[1:]
        out_shape.append(jax.ShapeDtypeStruct((2, *ctx_shape), returned.dtype))
        scratch += [
            pltpu.VMEM(returned.shape, returned.dtype),
            pltpu.VMEM(ctx_shape, returned.dtype),
            pltpu.VMEM(ctx_shape, returned.dtype),
            pltpu.SemaphoreType.DMA((GROUP - 1, PIECES)),
            pltpu.SemaphoreType.DMA((GROUP - 1, PIECES)),
            pltpu.SemaphoreType.DMA((2,)),
            pltpu.SemaphoreType.DMA((2,)),
        ]
    return pl.pallas_call(
        partial(reduce_kernel, dims, len(grads), has_context),
        out_shape=out_shape,
        in_specs=in_specs,
        out_specs=[vmem] * len(out_shape),
        scratch_shapes=scratch,
        compiler_params=pltpu.CompilerParams(
            collective_id=collective_id, has_side_effects=True, vmem_limit_bytes=67043328
        ),
        cost_estimate=worth(1),
        name="reduce_grads",
    )(*args)


def norm_rows(values, gain_row):
    centre = values - jnp.mean(values, axis=-1, keepdims=True)
    spread = jnp.mean(centre * centre, axis=-1, keepdims=True)
    return centre * lax.rsqrt(spread + EPS) * gain_row


def matmul(former, latter):
    return jnp.dot(former, latter, preferred_element_type=jnp.float32)


def matmul_t(former, latter):
    return lax.dot_general(
        former, latter, (((1,), (1,)), ((), ())), preferred_element_type=jnp.float32
    )


def inner_t(former, latter):
    return lax.dot_general(
        former, latter, (((0,), (0,)), ((), ())), preferred_element_type=jnp.float32
    )


def worth(microseconds):
    return pl.CostEstimate(flops=microseconds * 10**9, bytes_accessed=0, transcendentals=0)


def norm_stats(rows):
    centre = rows - jnp.mean(rows, axis=-1, keepdims=True)
    inverse = lax.rsqrt(jnp.mean(centre * centre, axis=-1, keepdims=True) + EPS)
    return centre * inverse, inverse


def norm_pull(rows, gain_row, grad):
    unit, inverse = norm_stats(rows)
    scaled = grad * gain_row
    inner = jnp.mean(scaled * unit, axis=-1, keepdims=True)
    pulled = inverse * (scaled - jnp.mean(scaled, axis=-1, keepdims=True) - unit * inner)
    return pulled, jnp.sum(grad * unit, axis=0, keepdims=True)


def greet_pair():
    pl.semaphore_signal(
        pltpu.get_barrier_semaphore(), inc=1,
        device_id=(lax.axis_index("band"), 1 - lax.axis_index("head")), device_id_type=MESH,
    )


def pair_send(source, target, send_sem, recv_sem):
    return pltpu.make_async_remote_copy(
        source, target, send_sem, recv_sem,
        device_id=(lax.axis_index("band"), 1 - lax.axis_index("head")), device_id_type=MESH,
    )


def mlp_kernel(
    hidden_ref, incoming_ref, gain_ref, up_ref, down_ref,
    block_ref, grad_ref, gain_grad_ref, grad_up_ref, grad_down_ref,
    normed, normed_t, incoming_t, out_sum, back_sum, low, there, send_sem, recv_sem,
):
    step, last = pl.program_id(0), pl.num_programs(0) - 1
    rows = hidden_ref.shape[0]
    tile = 64

    @pl.when(step == 0)
    def _():
        greet_pair()

        def one(at, carry):
            part = pl.ds(pl.multiple_of(at * tile, tile), tile)
            unit, _ = norm_stats(hidden_ref[part, :])
            normed[part, :] = (unit * gain_ref[...]).astype(jnp.bfloat16)
            return carry

        lax.fori_loop(0, rows // tile, one, 0)
        normed_t[...] = normed[...].T
        incoming_t[...] = incoming_ref[...].T
        out_sum[...] = jnp.zeros_like(out_sum)
        back_sum[...] = jnp.zeros_like(back_sum)

    copies = [pair_send(low.at[one], there.at[one], send_sem.at[one], recv_sem.at[one]) for one in range(2)]
    before = matmul(normed[...], up_ref[...])
    share = 0.5 * (1.0 + lax.erf(before * 2.0**-0.5))
    activated = (before * share).astype(jnp.bfloat16)
    out_sum[...] += matmul_t(activated, down_ref[...])

    @pl.when(step == last)
    def _():
        pl.semaphore_wait(pltpu.get_barrier_semaphore(), 1)
        low[0] = out_sum[...].astype(jnp.bfloat16)
        copies[0].start()

    slope = share + before * jnp.exp(before * before * -0.5) * (2.0 * math.pi) ** -0.5
    grad_before = (matmul(incoming_ref[...], down_ref[...]) * slope).astype(jnp.bfloat16)
    back_sum[...] += matmul_t(grad_before, up_ref[...])

    @pl.when(step == last)
    def _():
        low[1] = back_sum[...].astype(jnp.bfloat16)
        copies[1].start()

    grad_down_ref[...] = matmul(incoming_t[...], activated).astype(jnp.bfloat16)
    grad_up_ref[...] = matmul(normed_t[...], grad_before).astype(jnp.bfloat16)

    @pl.when(step == last)
    def _():
        for copy in copies:
            copy.wait()
        gain_grad_ref[...] = jnp.zeros_like(gain_grad_ref)

        def one(at, carry):
            part = pl.ds(pl.multiple_of(at * tile, tile), tile)
            total = lambda which: low[which, part, :].astype(jnp.float32) + there[which, part, :].astype(jnp.float32)
            hidden = hidden_ref[part, :]
            block_ref[part, :] = (hidden + total(0)).astype(jnp.bfloat16)
            pulled, gain_part = norm_pull(hidden, gain_ref[...], total(1))
            grad_ref[part, :] = incoming_ref[part, :].astype(jnp.float32) + pulled
            gain_grad_ref[...] += gain_part
            return carry

        lax.fori_loop(0, rows // tile, one, 0)


def mlp_both_ways(hidden, incoming, gain_row, weights, first, w_down, collective_id):
    rows, width = hidden.shape
    units, cut = w_down.shape[1], weights.shape[2]
    whole = pl.BlockSpec((rows, width), lambda step: (0, 0))
    line = pl.BlockSpec((1, width), lambda step: (0, 0))
    columns = pl.BlockSpec((width, cut), lambda step: (0, step))
    up_matrix = pl.BlockSpec((None, width, cut), lambda step: (first + step, 0, 0))
    grad_matrix = pl.BlockSpec((None, width, cut), lambda step: (step, 0, 0))
    return pl.pallas_call(
        mlp_kernel,
        grid=(units // cut,),
        in_specs=[whole, whole, line, up_matrix, columns],
        out_specs=[whole, whole, line, grad_matrix, columns],
        out_shape=[
            jax.ShapeDtypeStruct((rows, width), jnp.bfloat16),
            jax.ShapeDtypeStruct((rows, width), jnp.float32),
            jax.ShapeDtypeStruct((1, width), jnp.float32),
            jax.ShapeDtypeStruct((units // cut, width, cut), jnp.bfloat16),
            jax.ShapeDtypeStruct((width, units), jnp.bfloat16),
        ],
        scratch_shapes=[
            pltpu.VMEM((rows, width), jnp.bfloat16),
            pltpu.VMEM((width, rows), jnp.bfloat16),
            pltpu.VMEM((width, rows), jnp.bfloat16),
            pltpu.VMEM((rows, width), jnp.float32),
            pltpu.VMEM((rows, width), jnp.float32),
            pltpu.VMEM((2, rows, width), jnp.bfloat16),
            pltpu.VMEM((2, rows, width), jnp.bfloat16),
            pltpu.SemaphoreType.DMA((2,)),
            pltpu.SemaphoreType.DMA((2,)),
        ],
        compiler_params=pltpu.CompilerParams(
            collective_id=collective_id, has_side_effects=True, vmem_limit_bytes=63 * 1024 * 1024
        ),
        cost_estimate=worth(1),
        name="mlp_both_ways",
    )(hidden, incoming, gain_row, weights, w_down)


def row_kernel(backward, follows, *refs):
    refs = list(refs)
    x_ref, w_ref, base_ref, gain_ref = refs[:4]
    rest = refs[4:]
    hidden_ref = rest.pop(0) if backward else None
    next_ref = rest.pop(0) if follows else None
    sum_ref = rest.pop(0)
    low_ref, next_out_ref = (rest.pop(0), rest.pop(0)) if follows else (None, None)
    gain_grad_ref = rest.pop(0) if backward else None
    low, there, send_sem, recv_sem = rest
    rows = x_ref.shape[0]
    cut = rows // send_sem.shape[0]
    greet_pair()

    def part_of(at):
        return pl.ds(pl.multiple_of(at * cut, cut), cut)

    def copy_of(at):
        return pair_send(low.at[part_of(at)], there.at[part_of(at)], send_sem.at[at], recv_sem.at[at])

    for at in range(rows // cut):
        low[part_of(at), :] = matmul_t(x_ref[part_of(at), :], w_ref[...]).astype(jnp.bfloat16)
        if at == 0:
            pl.semaphore_wait(pltpu.get_barrier_semaphore(), 1)
        copy_of(at).start()
    if backward:
        gain_grad_ref[...] = jnp.zeros_like(gain_grad_ref)

    def finish(at, carry):
        part = part_of(at)
        copy_of(at).wait()
        total = low[part, :].astype(jnp.float32) + there[part, :].astype(jnp.float32)
        base = base_ref[part, :].astype(jnp.float32)
        if backward:
            pulled, gain_part = norm_pull(hidden_ref[part, :], gain_ref[...], total)
            gain_grad_ref[...] += gain_part
            result = base + pulled
            passed_on = result.astype(jnp.bfloat16)
        else:
            result = base + total
            if follows:
                passed_on = (norm_stats(result)[0] * gain_ref[...]).astype(jnp.bfloat16)
        sum_ref[part, :] = result
        if follows:
            low_ref[part, :] = passed_on
            next_out_ref[part, :] = matmul(passed_on, next_ref[...]).astype(jnp.bfloat16)
        return carry

    lax.fori_loop(0, rows // cut, finish, 0)


def row_step(x, weights, at, base, gain_row, collective_id, hidden=None, follow=None):
    rows, width = base.shape
    units = x.shape[1]
    backward, follows = hidden is not None, follow is not None
    whole = pl.BlockSpec((rows, width), lambda step: (0, 0))
    narrow = pl.BlockSpec((rows, units), lambda step: (0, 0))
    line = pl.BlockSpec((1, width), lambda step: (0, 0))
    matrix = lambda which: pl.BlockSpec((None, width, units), lambda step: (which, 0, 0))
    args, in_specs = [x, weights, base, gain_row], [narrow, matrix(at), whole, line]
    out_specs, out_shape = [whole], [jax.ShapeDtypeStruct((rows, width), jnp.float32)]
    if backward:
        args.append(hidden)
        in_specs.append(whole)
    if follows:
        args.append(weights)
        in_specs.append(matrix(follow))
        out_specs += [whole, narrow]
        out_shape += [
            jax.ShapeDtypeStruct((rows, width), jnp.bfloat16), jax.ShapeDtypeStruct((rows, units), jnp.bfloat16)
        ]
    if backward:
        out_specs.append(line)
        out_shape.append(jax.ShapeDtypeStruct((1, width), jnp.float32))
    cuts = 4
    return pl.pallas_call(
        partial(row_kernel, backward, follows),
        grid=(1,),
        in_specs=in_specs,
        out_specs=out_specs,
        out_shape=out_shape,
        scratch_shapes=[
            pltpu.VMEM((rows, width), jnp.bfloat16),
            pltpu.VMEM((rows, width), jnp.bfloat16),
            pltpu.SemaphoreType.DMA((cuts,)),
            pltpu.SemaphoreType.DMA((cuts,)),
        ],
        compiler_params=pltpu.CompilerParams(
            collective_id=collective_id, has_side_effects=True, vmem_limit_bytes=63 * 1024 * 1024
        ),
        cost_estimate=worth(1),
        name="row_step",
    )(*args)


def heads_of(block):
    lane = lax.broadcasted_iota(jnp.int32, block.shape, 1) // HEAD_DIM
    return [
        block * (lane == one).astype(jnp.float32).astype(block.dtype) for one in range(LANES // HEAD_DIM)
    ]


def shifted(scores, causal, behind):
    if not causal or behind > 0:
        return scores
    key_ids = lax.broadcasted_iota(jnp.int32, scores.shape, 0)
    query_ids = lax.broadcasted_iota(jnp.int32, scores.shape, 1)
    return jnp.where(key_ids <= query_ids, scores, NEG)


def attend_body(reach, causal, q_ref, k_ref, v_ref, out_ref, total_ref):
    scale = HEAD_DIM**-0.5
    values_t = [v_ref[behind].T for behind in range(reach)]
    outs = []
    for one, q_one in enumerate(heads_of(q_ref[...])):
        scores = [shifted(matmul_t(k_ref[behind], q_one) * scale, causal, behind) for behind in range(reach)]
        top = jnp.max(scores[0], axis=0, keepdims=True)
        for block in scores[1:]:
            top = jnp.maximum(top, jnp.max(block, axis=0, keepdims=True))
        raised = [jnp.exp(block - top) for block in scores]
        total = jnp.sum(raised[0], axis=0, keepdims=True)
        for block in raised[1:]:
            total = total + jnp.sum(block, axis=0, keepdims=True)
        share = 1.0 / total
        mixed = None
        for behind in range(reach):
            part = matmul(values_t[behind], (raised[behind] * share).astype(jnp.bfloat16))
            mixed = part if mixed is None else mixed + part
        outs.append(mixed[one * HEAD_DIM : (one + 1) * HEAD_DIM])
        total_ref[one : one + 1, :] = top + jnp.log(total)
    out_ref[...] = jnp.concatenate(outs, axis=0).T.astype(jnp.bfloat16)


def attend_back_body(reach, causal, q_ref, k_ref, v_ref, total_ref, g_ref, dq_ref, dk_ref, dv_ref):
    scale = HEAD_DIM**-0.5
    keys_t = [k_ref[behind].T for behind in range(reach)]
    q_heads, g_heads = heads_of(q_ref[...]), heads_of(g_ref[...])
    query_grads = []
    key_grads, value_grads = [None] * reach, [None] * reach
    for one in range(len(q_heads)):
        q_one, g_one = q_heads[one], g_heads[one]
        log_total = total_ref[one : one + 1, :]
        probs, grads, centre = [], [], None
        for behind in range(reach):
            scores = shifted(matmul_t(k_ref[behind], q_one) * scale, causal, behind)
            probs.append(jnp.exp(scores - log_total))
            grads.append(matmul_t(v_ref[behind], g_one))
            part = jnp.sum(grads[-1] * probs[-1], axis=0, keepdims=True)
            centre = part if centre is None else centre + part
        query_grad = None
        for behind in range(reach):
            grad_scores = (probs[behind] * (grads[behind] - centre)).astype(jnp.bfloat16)
            part = matmul(keys_t[behind], grad_scores)
            query_grad = part if query_grad is None else query_grad + part
            key_part = matmul(grad_scores, q_one)
            value_part = matmul(probs[behind].astype(jnp.bfloat16), g_one)
            key_grads[behind] = key_part if one == 0 else key_grads[behind] + key_part
            value_grads[behind] = value_part if one == 0 else value_grads[behind] + value_part
        query_grads.append(query_grad[one * HEAD_DIM : (one + 1) * HEAD_DIM])
    dq_ref[...] = (jnp.concatenate(query_grads, axis=0).T * scale).astype(jnp.bfloat16)
    for behind in range(dk_ref.shape[0]):
        if behind < reach:
            dk_ref[behind] = (key_grads[behind] * scale).astype(jnp.bfloat16)
            dv_ref[behind] = value_grads[behind].astype(jnp.bfloat16)
        else:
            dk_ref[behind] = jnp.zeros(dk_ref.shape[1:], dk_ref.dtype)
            dv_ref[behind] = jnp.zeros(dv_ref.shape[1:], dv_ref.dtype)


def by_offset(body, causal, offset_ref, *refs):
    reaches = refs[1].shape[0]
    if reaches == 1:
        body(1, causal, *refs)
        return
    offset = offset_ref[pl.program_id(0)]
    for earlier_bands in range(reaches):
        @pl.when(offset == earlier_bands)
        def _():
            body(earlier_bands + 1, causal, *refs)


def attention_specs(queries, keys):
    rows, reaches, key_rows = queries.shape[1], keys.shape[1], keys.shape[2]
    row_spec = pl.BlockSpec((None, rows, LANES), lambda stream, pair: (stream, 0, pair))
    key_spec = pl.BlockSpec((None, reaches, key_rows, LANES), lambda stream, pair: (stream, 0, 0, pair))
    total_spec = pl.BlockSpec((None, None, 8, rows), lambda stream, pair: (stream, pair, 0, 0))
    return row_spec, key_spec, total_spec


def attention(queries, keys, values, offsets, causal):
    streams, rows, width = queries.shape
    row_spec, key_spec, total_spec = attention_specs(queries, keys)
    return pl.pallas_call(
        partial(by_offset, attend_body, causal),
        grid=(streams, width // LANES),
        in_specs=[pl.BlockSpec(memory_space=pltpu.SMEM), row_spec, key_spec, key_spec],
        out_specs=[row_spec, total_spec],
        out_shape=[
            jax.ShapeDtypeStruct(queries.shape, jnp.bfloat16),
            jax.ShapeDtypeStruct((streams, width // LANES, 8, rows), jnp.float32),
        ],
        cost_estimate=worth(1),
        name="attend",
    )(offsets, queries, keys, values)


def attention_back(queries, keys, values, offsets, totals, grad_out, causal):
    streams, rows, width = queries.shape
    row_spec, key_spec, total_spec = attention_specs(queries, keys)
    return pl.pallas_call(
        partial(by_offset, attend_back_body, causal),
        grid=(streams, width // LANES),
        in_specs=[pl.BlockSpec(memory_space=pltpu.SMEM), row_spec, key_spec, key_spec, total_spec, row_spec],
        out_specs=[row_spec, key_spec, key_spec],
        out_shape=[
            jax.ShapeDtypeStruct(queries.shape, jnp.bfloat16),
            jax.ShapeDtypeStruct(keys.shape, jnp.bfloat16),
            jax.ShapeDtypeStruct(keys.shape, jnp.bfloat16),
        ],
        cost_estimate=worth(1),
        name="attend_back",
    )(offsets, queries, keys, values, totals, grad_out)


def swap_kernel(count, *refs):
    sources, targets = refs[:count], refs[count : 2 * count]
    send_sem, recv_sem = refs[2 * count :]
    band, head = lax.axis_index("band"), lax.axis_index("head")
    barrier = pltpu.get_barrier_semaphore()
    pl.semaphore_signal(barrier, inc=1, device_id=(band, 1 - head), device_id_type=MESH)
    pl.semaphore_wait(barrier, 1)
    copies = [
        pltpu.make_async_remote_copy(
            sources[one], targets[one], send_sem.at[one], recv_sem.at[one],
            device_id=(band, 1 - head), device_id_type=MESH,
        )
        for one in range(count)
    ]
    for copy in copies:
        copy.start()
    for copy in copies:
        copy.wait()


def swapped(collective_id, *arrays):
    vmem = pl.BlockSpec(memory_space=pltpu.VMEM)
    return pl.pallas_call(
        partial(swap_kernel, len(arrays)),
        out_shape=[jax.ShapeDtypeStruct(array.shape, array.dtype) for array in arrays],
        in_specs=[vmem] * len(arrays),
        out_specs=[vmem] * len(arrays),
        scratch_shapes=[pltpu.SemaphoreType.DMA((len(arrays),)), pltpu.SemaphoreType.DMA((len(arrays),))],
        compiler_params=pltpu.CompilerParams(collective_id=collective_id, has_side_effects=True),
        cost_estimate=worth(1),
        name="swap_heads",
    )(*arrays)


def total_kernel(dims, in_ref, out_ref, near, far, send_sem, recv_sem):
    head = lax.axis_index("head")
    band, place = place_of(dims)
    layer = dims[1] * dims[2]
    inside = (band % layer) * 2 + head
    lines = [
        (near, layer * 2, inside, lambda at: (place[0] * layer + at // 2, at % 2)),
        (far, dims[0], place[0], lambda at: (at * layer + band % layer, head)),
    ]
    barrier = pltpu.get_barrier_semaphore()
    for _, size, mine, device in lines:
        for shift in range(1, size):
            pl.semaphore_signal(barrier, inc=1, device_id=device((mine + shift) % size), device_id_type=MESH)
    pl.semaphore_wait(barrier, sum(size - 1 for _, size, _, _ in lines))
    total = in_ref[...]
    for line, (slots, size, mine, device) in enumerate(lines):
        slots[mine] = total

        def copy(there, shift):
            return pltpu.make_async_remote_copy(
                slots.at[mine], slots.at[mine], send_sem.at[line, shift - 1], recv_sem.at[line, shift - 1],
                device_id=device(there), device_id_type=MESH,
            )

        def incoming(there, shift):
            return pltpu.make_async_remote_copy(
                slots.at[there], slots.at[there], send_sem.at[line, shift - 1], recv_sem.at[line, shift - 1],
                device_id=device(there), device_id_type=MESH,
            )

        for shift in range(1, size):
            copy((mine + shift) % size, shift).start()
        for shift in range(1, size):
            incoming((mine + size - shift) % size, shift).wait_recv()
        total = slots[0]
        for at in range(1, size):
            total = total + slots[at]
        for shift in range(1, size):
            copy((mine + shift) % size, shift).wait_send()
    out_ref[...] = total


def mesh_total(bands, tile, collective_id):
    dims = band_dims(bands)
    near = dims[1] * dims[2] * 2
    longest = max(dims[0], near)
    vmem = pl.BlockSpec(memory_space=pltpu.VMEM)
    return pl.pallas_call(
        partial(total_kernel, dims),
        out_shape=jax.ShapeDtypeStruct(tile.shape, tile.dtype),
        in_specs=[vmem],
        out_specs=vmem,
        scratch_shapes=[
            pltpu.VMEM((near, *tile.shape), tile.dtype),
            pltpu.VMEM((dims[0], *tile.shape), tile.dtype),
            pltpu.SemaphoreType.DMA((2, longest - 1)),
            pltpu.SemaphoreType.DMA((2, longest - 1)),
        ],
        compiler_params=pltpu.CompilerParams(collective_id=collective_id, has_side_effects=True),
        cost_estimate=worth(1),
        name="mesh_total",
    )(tile)


def adamw_update(weight, moment_one, moment_two, gradient, step_rate, decay_rate):
    moment_one_new = BETA_ONE * moment_one + (1.0 - BETA_ONE) * gradient
    moment_two_new = BETA_TWO * moment_two + (1.0 - BETA_TWO) * gradient * gradient
    unbiased_one = moment_one_new / (1.0 - BETA_ONE**STEP)
    unbiased_two = moment_two_new / (1.0 - BETA_TWO**STEP)
    weight_new = weight - step_rate * (
        unbiased_one / (jnp.sqrt(unbiased_two) + ADAM_EPS) + decay_rate * weight
    )
    return (weight_new, moment_one_new, moment_two_new)


def local(
    tokens,
    text_states,
    cotangent,
    earlier,
    proj_master,
    out_master,
    mlp_master,
    gain_master,
    proj_first,
    proj_second,
    out_first,
    out_second,
    mlp_first,
    mlp_second,
    gain_first,
    gain_second,
):
    streams, band_rows, model_width = tokens.shape
    row_count = streams * band_rows
    text_rows = text_states.shape[1]
    bands, head = lax.axis_size("band"), lax.axis_index("head")
    shard_rows, width = proj_master.shape[1:]
    chunks = mlp_master.shape[2] // width
    up_cut = mlp_master[0].reshape(shard_rows, chunks, width).transpose(1, 0, 2)
    shard = jnp.concatenate([proj_master, out_master, up_cut]).astype(jnp.bfloat16)
    gain_low = gain_master.astype(jnp.bfloat16).astype(jnp.float32)
    gain_tile = jnp.pad(gain_low, ((0, 5), (0, LANES - shard_rows)))
    both = jnp.concatenate([tokens, text_states], axis=1)
    context = lax.dynamic_index_in_dim(both, head, 0, keepdims=False)
    gathered, gain_tiles, passed = gather_weights(bands, shard, gain_tile, context, 1)
    down_low, gain_tiles = lax.optimization_barrier((mlp_master[1].astype(jnp.bfloat16), gain_tiles))
    w_down = lax.all_gather(down_low, "band", axis=0, tiled=True)
    weights = gathered.reshape(shard.shape[0], model_width, width)
    w_query, w_key, w_value, _, w_text_key, w_text_value, _, w_cross_out = (weights[at] for at in range(8))
    gains = gain_tiles.reshape(bands, 8, LANES)[:, :3, :shard_rows].transpose(1, 0, 2).reshape(3, model_width)

    offsets = earlier[:, 0]
    reach_ids = jnp.arange(SEQ_BANDS)
    within = reach_ids[None, :] <= offsets[:, None]
    inputs = tokens.astype(jnp.float32).reshape(row_count, model_width)
    reached = jnp.concatenate([tokens[:, None], passed[:, :, :band_rows]], axis=1)
    normed_all = jnp.where(
        within[:, :, None, None], norm_rows(reached.astype(jnp.float32), gains[0]), 0.0
    ).astype(jnp.bfloat16)
    normed_one = normed_all[:, 0].reshape(row_count, model_width)
    normed_all = normed_all.reshape(SEQ_BANDS * row_count, model_width)
    row_shape = (streams, band_rows, width)
    reach_shape = (streams, SEQ_BANDS, band_rows, width)
    text_shape = (streams, 1, text_rows, width)
    queries = matmul(normed_one, w_query).astype(jnp.bfloat16).reshape(row_shape)
    keys = matmul(normed_all, w_key).astype(jnp.bfloat16).reshape(reach_shape)
    values = matmul(normed_all, w_value).astype(jnp.bfloat16).reshape(reach_shape)
    attended, self_totals = attention(queries, keys, values, offsets, True)
    attended = attended.reshape(row_count, width)
    hidden_one, normed_two, cross_queries = row_step(
        attended, weights, 6, tokens.reshape(row_count, model_width), gains[1:2], 3, follow=3
    )
    cross_queries = cross_queries.reshape(row_shape)
    caption = text_states
    for behind in range(1, SEQ_BANDS):
        caption = jnp.where((offsets == behind)[:, None, None], passed[:, behind - 1, band_rows:], caption)
    caption = caption.reshape(streams * text_rows, model_width)
    cross_keys = matmul(caption, w_text_key).astype(jnp.bfloat16).reshape(text_shape)
    cross_values = matmul(caption, w_text_value).astype(jnp.bfloat16).reshape(text_shape)
    crossed, cross_totals = attention(cross_queries, cross_keys, cross_values, offsets, False)
    crossed = crossed.reshape(row_count, width)
    (hidden_two,) = row_step(crossed, weights, 7, hidden_one, gains[2:3], 4)
    incoming = cotangent.reshape(row_count, model_width)
    block_out, grad_two, gain_grad_three, grad_up, grad_down = mlp_both_ways(
        hidden_two, incoming, gains[2:3], weights, 8, w_down, 5
    )
    block_out = block_out.reshape(tokens.shape)
    gain_grad_three = gain_grad_three[0]
    down_sum = lax.psum_scatter(grad_down, "band", scatter_dimension=0, tiled=True).astype(jnp.float32)
    grad_two_low = grad_two.astype(jnp.bfloat16)
    grad_cross_out = inner_t(grad_two_low, crossed)
    grad_crossed = matmul(grad_two_low, w_cross_out).astype(jnp.bfloat16).reshape(row_shape)
    grad_cq, grad_ck, grad_cv = attention_back(
        cross_queries, cross_keys, cross_values, offsets, cross_totals, grad_crossed, False
    )
    grad_cq = grad_cq.reshape(row_count, width)
    grad_ck = grad_ck.reshape(streams * text_rows, width)
    grad_cv = grad_cv.reshape(streams * text_rows, width)
    text_part = (matmul_t(grad_ck, w_text_key) + matmul_t(grad_cv, w_text_value)).astype(jnp.bfloat16)
    text_part = text_part.reshape(text_states.shape)
    grad_one, grad_one_low, grad_attended, gain_grad_two = row_step(
        grad_cq, weights, 3, grad_two, gains[1:2], 7, hidden=hidden_one, follow=6
    )
    gain_grad_two = gain_grad_two[0]
    grad_self_out = inner_t(grad_one_low, attended)
    grad_attended = grad_attended.reshape(row_shape)
    grad_queries, grad_keys, grad_values = attention_back(
        queries, keys, values, offsets, self_totals, grad_attended, True
    )
    grad_queries = grad_queries.reshape(row_count, width)
    reach_part = matmul_t(grad_keys.reshape(-1, width), w_key) + matmul_t(grad_values.reshape(-1, width), w_value)
    reach_part = reach_part.reshape(streams, SEQ_BANDS, band_rows, model_width)
    own_part = matmul_t(grad_queries, w_query).reshape(tokens.shape) + reach_part[:, 0]
    own_text = jnp.where((offsets == 0)[:, None, None], text_part, 0).astype(jnp.bfloat16)
    sent_text = jnp.where(
        (offsets[:, None] == reach_ids[None, 1:])[:, :, None, None], text_part[:, None], 0
    ).astype(jnp.bfloat16)
    own_back = jnp.concatenate([own_part.astype(jnp.bfloat16), own_text], axis=1)
    sent_back = jnp.concatenate([reach_part[:, 1:].astype(jnp.bfloat16), sent_text], axis=2)
    mine = lax.dynamic_index_in_dim(sent_back, head, 0, keepdims=False)
    other = lax.dynamic_index_in_dim(sent_back, 1 - head, 0, keepdims=False)
    own_there, mine_there = swapped(8, own_back, other)
    own_back = own_back.astype(jnp.float32) + own_there.astype(jnp.float32)
    returned = (mine.astype(jnp.float32) + mine_there.astype(jnp.float32)).astype(jnp.bfloat16)

    flat = lambda part: part.reshape(-1, width)
    grads = [
        part.astype(jnp.bfloat16)[None]
        for part in (
            inner_t(normed_one, grad_queries),
            inner_t(normed_all, flat(grad_keys)),
            inner_t(normed_all, flat(grad_values)),
            inner_t(normed_two, grad_cq),
            inner_t(caption, grad_ck),
            inner_t(caption, grad_cv),
            grad_self_out,
            grad_cross_out,
        )
    ]
    grads.append(grad_up)
    returned, down_sum = lax.optimization_barrier((returned, down_sum))
    summed, came_back = reduce_grads(bands, grads, returned, 2)
    back_all = own_back + came_back.astype(jnp.float32)
    grad_normed_one = back_all[:, :band_rows].reshape(row_count, model_width)
    grad_text = back_all[:, band_rows:]
    _, pull_one = jax.vjp(norm_rows, inputs, gains[0])
    back_zero, gain_grad_one = pull_one(grad_normed_one)
    grad_tokens = (grad_one + back_zero).reshape(tokens.shape)

    squares = jnp.sum(summed * summed) + jnp.sum(down_sum * down_sum)
    gain_rows = jnp.stack([gain_grad_one, gain_grad_two, gain_grad_three]).reshape(-1, LANES)
    tile = jnp.concatenate([gain_rows, jnp.full((8, LANES), squares)])
    tile = mesh_total(bands, tile, 10)
    gain_total = 0.5 * tile[:-8].reshape(3, model_width)
    grad_norm = jnp.sqrt(tile[-1, 0] + jnp.sum(gain_total * gain_total))
    gain_grad = lax.dynamic_slice_in_dim(gain_total, lax.axis_index("band") * shard_rows, shard_rows, 1)
    proj_grad, out_grad = summed[:6], summed[6:8]
    up_sum = summed[8:].transpose(1, 0, 2).reshape(down_sum.shape)
    mlp_grad = jnp.stack([up_sum, down_sum])
    factor = jnp.minimum(1.0, CLIP / grad_norm)
    matrix_rate = 2.0 * D ** (-0.5)
    new_proj = adamw_update(
        proj_master, proj_first, proj_second, proj_grad * factor, matrix_rate, DECAY
    )
    new_out = adamw_update(out_master, out_first, out_second, out_grad * factor, matrix_rate, DECAY)
    new_mlp = adamw_update(mlp_master, mlp_first, mlp_second, mlp_grad * factor, matrix_rate, DECAY)
    new_gain = adamw_update(
        gain_master, gain_first, gain_second, gain_grad * factor, GAIN_RATE, 0.0
    )
    return (
        block_out,
        grad_tokens,
        grad_text,
        grad_norm,
        new_proj[0],
        new_proj[1],
        new_proj[2],
        new_out[0],
        new_out[1],
        new_out[2],
        new_mlp[0],
        new_mlp[1],
        new_mlp[2],
        new_gain[0],
        new_gain[1],
        new_gain[2],
    )


def solution(mesh):
    return jax.shard_map(
        local,
        mesh=mesh,
        in_specs=(
            P(None, "band", None),
            P(None, "band", None),
            P(None, "band", None),
            P(None, "band"),
            P(None, "band", "head"),
            P(None, "band", "head"),
            P(None, "band", "head"),
            P(None, "band"),
            P(None, "band", "head"),
            P(None, "band", "head"),
            P(None, "band", "head"),
            P(None, "band", "head"),
            P(None, "band", "head"),
            P(None, "band", "head"),
            P(None, "band"),
            P(None, "band"),
        ),
        out_specs=(
            P(None, "band", None),
            P(None, "band", None),
            P(None, "band", None),
            P(),
            P(None, "band", "head"),
            P(None, "band", "head"),
            P(None, "band", "head"),
            P(None, "band", "head"),
            P(None, "band", "head"),
            P(None, "band", "head"),
            P(None, "band", "head"),
            P(None, "band", "head"),
            P(None, "band", "head"),
            P(None, "band"),
            P(None, "band"),
            P(None, "band"),
        ),
        check_vma=False,
    )
```

```python
import math
from functools import partial

import jax
import jax.numpy as jnp
from jax import lax
from jax.experimental import pallas as pl
from jax.experimental.pallas import tpu as pltpu
from jax.sharding import PartitionSpec as P

D = 1024
HEAD_DIM = 64
SEQ_BANDS = 4
STEP = 10


EPS = 1e-05
NEG = -1e30
CLIP = 1.0
BETA_ONE = 0.9
BETA_TWO = 0.95
ADAM_EPS = 1e-08
DECAY = 0.1
GAIN_RATE = 0.5
LANES = 128


MESH = pl.DeviceIdType.MESH
ORDERS = ((2, 0, 1), (1, 0, 2))
GROUP = 4
PIECES = 6
GAP = 2
REDUCE_GAP = 1


def band_dims(bands):
    inner = 4 if bands >= 64 else 2
    return (bands // (inner * inner), inner, inner)


def strides_of(dims):
    return (dims[1] * dims[2], dims[2], 1)


def place_of(dims):
    band = lax.axis_index("band")
    return band, (
        band // (dims[1] * dims[2]),
        (band // dims[2]) % dims[1],
        band % dims[2],
    )


def stage_list(dims, order):
    return [(phase, step) for phase in range(3) for step in range(dims[order[phase]] - 1)]


def block_of(ref, lead, place, order, phase, index, columns):
    at = list(place)
    for done in range(phase):
        at[order[done]] = slice(None)
    at[order[phase]] = index
    return ref.at[(*lead, *at, slice(None), columns)]


def greet(dims, place, band, head, extra):
    barrier = pltpu.get_barrier_semaphore()
    strides = strides_of(dims)
    total = jnp.int32(0)
    peers = []
    for axis in range(3):
        for sign in (1, -1):
            there = place[axis] + sign
            peers.append(((there >= 0) & (there < dims[axis]), band + sign * strides[axis], head))
    peers += extra
    for present, peer_band, peer_head in peers:
        @pl.when(present)
        def _():
            pl.semaphore_signal(barrier, inc=1, device_id=(peer_band, peer_head), device_id_type=MESH)
        total = total + present.astype(jnp.int32)
    pl.semaphore_wait(barrier, total)


def gather_kernel(dims, has_context, *refs):
    if has_context:
        (w_ref, gain_ref, ctx_ref, out_ref, gains_ref, ctx_out,
         own_sem, send_sem, recv_sem, gsend, grecv, prev_ref, up_sem, csend, crecv, psend, precv) = refs
    else:
        (w_ref, gain_ref, out_ref, gains_ref, own_sem, send_sem, recv_sem, gsend, grecv) = refs
    band, place = place_of(dims)
    head = lax.axis_index("head")
    strides = strides_of(dims)
    count = w_ref.shape[0]
    half = w_ref.shape[2] // 2
    bands = dims[0] * dims[1] * dims[2]
    true = band >= 0
    extra = []
    if has_context:
        base = (band // GROUP) * GROUP
        mine = band % GROUP
        for shift in range(1, GROUP):
            extra.append((true, base + (mine + shift) % GROUP, head))
        extra.append((band + GROUP < bands, band + GROUP, head))
        extra.append((band >= GROUP, band - GROUP, head))
        extra.append((true, band, 1 - head))
    greet(dims, place, band, head, extra)

    own = [
        pltpu.make_async_copy(w_ref, out_ref.at[:, place[0], place[1], place[2]], own_sem.at[0]),
        pltpu.make_async_copy(gain_ref, gains_ref.at[place[0], place[1], place[2]], own_sem.at[1]),
    ]
    for copy in own:
        copy.start()

    def up_copy():
        return pltpu.make_async_remote_copy(
            ctx_ref, prev_ref, up_sem.at[0], up_sem.at[1], device_id=(band + GROUP, head), device_id_type=MESH
        )

    def peer_copy(back, piece_at, source):
        cut = ctx_ref.shape[0] // PIECES
        rows = pl.ds(piece_at * cut, cut)
        return pltpu.make_async_remote_copy(
            source.at[rows], ctx_out.at[head, back - 1, rows], csend.at[back - 1, piece_at], crecv.at[back - 1, piece_at],
            device_id=(base + (mine + back) % GROUP, head), device_id_type=MESH,
        )

    def pair_copy(back):
        return pltpu.make_async_remote_copy(
            ctx_out.at[head, back - 1], ctx_out.at[head, back - 1], psend.at[back - 1], precv.at[back - 1],
            device_id=(band, 1 - head), device_id_type=MESH,
        )

    if has_context:
        @pl.when(band + GROUP < bands)
        def _():
            up_copy().start()

    def piece(color, m, phase, step, way, incoming):
        order = ORDERS[color]
        axis = order[phase]
        size, at = dims[axis], place[axis]
        toward = 1 if way == 0 else -1
        stage = stage_list(dims, order).index((phase, step))
        if incoming:
            index = at - toward * (step + 1)
            present = (index >= 0) & (index < size)
        else:
            index = at - toward * step
            present = (index >= 0) & (index < size) & (at + toward >= 0) & (at + toward < size)
        columns = pl.ds(color * half, half)
        target = (band + toward * strides[axis], head)
        land = block_of(out_ref, (m,), place, order, phase, index, columns)
        source = w_ref.at[m, :, columns] if stage == 0 else land
        copy = pltpu.make_async_remote_copy(
            source, land, send_sem.at[color, stage, way, m], recv_sem.at[color, stage, way, m],
            device_id=target, device_id_type=MESH,
        )
        return present, copy

    def gain_piece(phase, step, way, incoming):
        order = ORDERS[0]
        axis = order[phase]
        size, at = dims[axis], place[axis]
        toward = 1 if way == 0 else -1
        stage = stage_list(dims, order).index((phase, step))
        if incoming:
            index = at - toward * (step + 1)
            present = (index >= 0) & (index < size)
        else:
            index = at - toward * step
            present = (index >= 0) & (index < size) & (at + toward >= 0) & (at + toward < size)
        land = block_of(gains_ref, (), place, order, phase, index, slice(None))
        source = gain_ref if stage == 0 else land
        copy = pltpu.make_async_remote_copy(
            source, land, gsend.at[stage, way], grecv.at[stage, way],
            device_id=(band + toward * strides[axis], head), device_id_type=MESH,
        )
        return present, copy

    stages = [stage_list(dims, order) for order in ORDERS]
    depth = len(stages[0])

    def context_step(t):
        for one in range(PIECES):
            @pl.when(t == one)
            def _():
                for back in range(1, GROUP):
                    @pl.when(mine + back < GROUP)
                    def _():
                        peer_copy(back, one, ctx_ref).start()
        @pl.when((t == 4) & (band >= GROUP))
        def _():
            pltpu.make_async_remote_copy(
                ctx_ref, prev_ref, up_sem.at[0], up_sem.at[1], device_id=(band - GROUP, head), device_id_type=MESH
            ).wait_recv()
        for one in range(PIECES):
            @pl.when((t == 4 + one) & (band >= GROUP))
            def _():
                for back in range(1, GROUP):
                    @pl.when(mine + back >= GROUP)
                    def _():
                        peer_copy(back, one, prev_ref).start()
        @pl.when(t == 13)
        def _():
            for back in range(1, GROUP):
                @pl.when((mine >= back) | (band >= GROUP))
                def _():
                    for one in range(PIECES):
                        peer_copy(back, one, ctx_ref).wait_recv()
                    pair_copy(back).start()

    def gains_step(t):
        for stage in range(depth + 1):
            @pl.when(t == stage)
            def _():
                if stage == 1:
                    for copy in own:
                        copy.wait()
                if stage > 0:
                    for way in range(2):
                        present, copy = gain_piece(*stages[0][stage - 1], way, True)
                        @pl.when(present)
                        def _():
                            copy.wait_recv()
                if stage < depth:
                    for way in range(2):
                        present, copy = gain_piece(*stages[0][stage], way, False)
                        @pl.when(present)
                        def _():
                            copy.start()

    def body(t, carry):
        gains_step(t)
        if has_context:
            context_step(t)
        for stage in range(depth, -1, -1):
            m = t - GAP * stage
            @pl.when((m >= 0) & (m < count))
            def _():
                for color in range(2):
                    if stage > 0:
                        for way in range(2):
                            present, copy = piece(color, m, *stages[color][stage - 1], way, True)
                            @pl.when(present)
                            def _():
                                copy.wait_recv()
                    if stage < depth:
                        for way in range(2):
                            present, copy = piece(color, m, *stages[color][stage], way, False)
                            @pl.when(present)
                            def _():
                                copy.start()
        return carry

    lax.fori_loop(0, count + GAP * depth, body, 0)

    if has_context:
        for back in range(1, GROUP):
            @pl.when((mine >= back) | (band >= GROUP))
            def _():
                pltpu.make_async_remote_copy(
                    ctx_out.at[1 - head, back - 1], ctx_out.at[1 - head, back - 1], psend.at[back - 1],
                    precv.at[back - 1], device_id=(band, 1 - head), device_id_type=MESH,
                ).wait_recv()
                pair_copy(back).wait_send()
            @pl.when((mine + back < GROUP) | (band >= GROUP))
            def _():
                for one in range(PIECES):
                    peer_copy(back, one, ctx_ref).wait_send()
        @pl.when(band + GROUP < bands)
        def _():
            up_copy().wait_send()

    for stage in range(depth):
        for way in range(2):
            present, copy = gain_piece(*stages[0][stage], way, False)
            @pl.when(present)
            def _():
                copy.wait_send()

    def drain(m, carry):
        for stage in range(depth):
            for color in range(2):
                for way in range(2):
                    present, copy = piece(color, m, *stages[color][stage], way, False)
                    @pl.when(present)
                    def _():
                        copy.wait_send()
        return carry

    lax.fori_loop(0, count, drain, 0)


def gather_weights(bands, shard, gain_tile, context, collective_id):
    dims = band_dims(bands)
    count, rows, width = shard.shape
    depth = len(stage_list(dims, ORDERS[0]))
    vmem = pl.BlockSpec(memory_space=pltpu.VMEM)
    anyspace = pl.BlockSpec(memory_space=pl.ANY)
    has_context = context is not None
    out_shape = [
        jax.ShapeDtypeStruct((count, *dims, rows, width), shard.dtype),
        jax.ShapeDtypeStruct((*dims, *gain_tile.shape), gain_tile.dtype),
    ]
    scratch = [
        pltpu.SemaphoreType.DMA((2,)),
        pltpu.SemaphoreType.DMA((2, depth, 2, count)),
        pltpu.SemaphoreType.DMA((2, depth, 2, count)),
        pltpu.SemaphoreType.DMA((depth, 2)),
        pltpu.SemaphoreType.DMA((depth, 2)),
    ]
    args = [shard, gain_tile]
    if has_context:
        args.append(context)
        out_shape.append(jax.ShapeDtypeStruct((2, GROUP - 1, *context.shape), context.dtype))
        scratch += [
            pltpu.VMEM(context.shape, context.dtype),
            pltpu.SemaphoreType.DMA((2,)),
            pltpu.SemaphoreType.DMA((GROUP - 1, PIECES)),
            pltpu.SemaphoreType.DMA((GROUP - 1, PIECES)),
            pltpu.SemaphoreType.DMA((GROUP - 1,)),
            pltpu.SemaphoreType.DMA((GROUP - 1,)),
        ]
    return pl.pallas_call(
        partial(gather_kernel, dims, has_context),
        out_shape=out_shape,
        in_specs=[vmem] * len(args),
        out_specs=[anyspace] * len(out_shape),
        scratch_shapes=scratch,
        compiler_params=pltpu.CompilerParams(collective_id=collective_id, has_side_effects=True),
        cost_estimate=worth(200),
        name="gather_weights",
    )(*args)


def reduce_kernel(dims, arrays, has_context, *refs):
    sources = [ref.at[one] for ref in refs[:arrays] for one in range(ref.shape[0])]
    count, refs = len(sources), refs[arrays:]
    if has_context:
        (back_ref, out_ref, back_out, squares_ref, gv, load_sem, last_ref, mid_ref, first_ref, send_sem, recv_sem,
         landed, relay, from_up, csend, crecv, up_sem, pair_sem) = refs
    else:
        (out_ref, gv, load_sem, last_ref, mid_ref, first_ref, send_sem, recv_sem) = refs
    band, place = place_of(dims)
    head = lax.axis_index("head")
    strides = strides_of(dims)
    half = sources[0].shape[-1] // 2
    bands = dims[0] * dims[1] * dims[2]
    true = band >= 0
    orders = tuple(order[::-1] for order in ORDERS)
    lands = (last_ref, mid_ref, first_ref)

    def load(m, source):
        return pltpu.make_async_copy(source, gv.at[m], load_sem.at[m])

    for m in range(count):
        load(m, sources[m]).start()

    extra = []
    if has_context:
        base = (band // GROUP) * GROUP
        mine = band % GROUP
        for shift in range(1, GROUP):
            extra.append((true, base + (mine + shift) % GROUP, head))
        extra.append((band + GROUP < bands, band + GROUP, head))
        extra.append((band >= GROUP, band - GROUP, head))
        extra.append((true, band, 1 - head))
    greet(dims, place, band, head, extra)

    def peer_copy(back, piece_at):
        cut = relay.shape[0] // PIECES
        rows = pl.ds(piece_at * cut, cut)
        return pltpu.make_async_remote_copy(
            back_ref.at[back - 1, rows], landed.at[back - 1, rows],
            csend.at[back - 1, piece_at], crecv.at[back - 1, piece_at],
            device_id=(base + (mine + GROUP - back) % GROUP, head), device_id_type=MESH,
        )

    def down_copy(target):
        return pltpu.make_async_remote_copy(
            relay, from_up, up_sem.at[0], up_sem.at[1], device_id=(target, head), device_id_type=MESH
        )

    def pair_copy(stream):
        return pltpu.make_async_remote_copy(
            back_out.at[stream], back_out.at[stream], pair_sem.at[0], pair_sem.at[1],
            device_id=(band, 1 - head), device_id_type=MESH,
        )

    def slot(size, step, way):
        return 0 if size == 2 else step * 2 + way

    def own_block(m, color, phase, index):
        order = orders[color]
        at = list(place)
        for later in range(phase + 1, 3):
            at[order[later]] = slice(None)
        at[order[phase]] = index
        return gv.at[(m, *at, slice(None), pl.ds(color * half, half))]

    def landing(m, color, phase, step, way):
        size = dims[orders[color][phase]]
        return lands[phase].at[m, color, slot(size, step, way)]

    def outgoing(m, color, phase, step, way):
        axis = orders[color][phase]
        size, at = dims[axis], place[axis]
        toward = 1 if way == 0 else -1
        rank = at if way == 0 else size - 1 - at
        index = size - 1 - step + at if way == 0 else step + at - (size - 1)
        present = (rank <= step) & (at + toward >= 0) & (at + toward < size)
        stage = stage_list(dims, orders[color]).index((phase, step))
        target = (band + toward * strides[axis], head)

        def copy(source):
            return pltpu.make_async_remote_copy(
                source, landing(m, color, phase, step, way),
                send_sem.at[color, stage, way, m], recv_sem.at[color, stage, way, m],
                device_id=target, device_id_type=MESH,
            )

        return present, rank, index, copy

    def arrived(m, color, phase, step, way):
        axis = orders[color][phase]
        size, at = dims[axis], place[axis]
        before = at - 1 if way == 0 else at + 1
        rank = before if way == 0 else size - 1 - before
        present = (before >= 0) & (before < size) & (rank <= step)
        _, _, _, copy = outgoing(m, color, phase, step, way)
        return present, copy(landing(m, color, phase, step, way))

    def add_into(target, source):
        lead = target.shape[:-2]
        if len(lead) == 0:
            target[...] = target[...] + source[...]
        elif len(lead) == 1:
            for i in range(lead[0]):
                target[i] = target[i] + source[i]
        else:
            for i in range(lead[0]):
                for j in range(lead[1]):
                    target[i, j] = target[i, j] + source[i, j]

    stages = [stage_list(dims, order) for order in orders]
    depth = len(stages[0])

    def send(m, color, phase, step):
        axis = orders[color][phase]
        size = dims[axis]
        for way in range(2):
            present, rank, index, copy = outgoing(m, color, phase, step, way)
            @pl.when(present & (rank == 0))
            def _():
                copy(own_block(m, color, phase, index)).start()
            if step > 0:
                @pl.when(present & (rank > 0))
                def _():
                    from_before = landing(m, color, phase, step - 1, way)
                    add_into(from_before, own_block(m, color, phase, index))
                    copy(from_before).start()

    def settle(m, color, phase, step):
        axis = orders[color][phase]
        size = dims[axis]
        for way in range(2):
            present, copy = arrived(m, color, phase, step, way)
            @pl.when(present)
            def _():
                copy.wait_recv()
                if step == size - 2:
                    landed_here = landing(m, color, phase, step, way)
                    if phase < 2:
                        add_into(own_block(m, color, phase, place[axis]), landed_here)
                    else:
                        columns = pl.ds(color * half, half)
                        if size == 2:
                            own = own_block(m, color, phase, place[axis])
                            out_ref[m, :, columns] = own[...].astype(jnp.float32) + landed_here[...].astype(jnp.float32)
                        else:
                            add_into(own_block(m, color, phase, place[axis]), landed_here)
        if phase == 2 and step == size - 2 and size > 2:
            columns = pl.ds(color * half, half)
            out_ref[m, :, columns] = own_block(m, color, phase, place[axis])[...].astype(jnp.float32)

    def body(t, carry):
        for stage in range(depth, -1, -1):
            m = t - REDUCE_GAP * stage
            @pl.when((m >= 0) & (m < count))
            def _():
                if stage == 0:
                    load(m, sources[0]).wait()
                for color in range(2):
                    if stage > 0:
                        settle(m, color, *stages[color][stage - 1])
                    if stage < depth:
                        send(m, color, *stages[color][stage])
        if has_context:
            for one in range(PIECES):
                @pl.when(t == one)
                def _():
                    for back in range(1, GROUP):
                        @pl.when((mine >= back) | (band >= GROUP))
                        def _():
                            peer_copy(back, one).start()
            @pl.when(t == 8)
            def _():
                for back in range(1, GROUP):
                    @pl.when((mine + back < GROUP) | (band >= GROUP))
                    def _():
                        for one in range(PIECES):
                            peer_copy(back, one).wait_recv()
                @pl.when((mine > 0) & (band >= GROUP))
                def _():
                    def relayed(at, inner):
                        rows = pl.ds(pl.multiple_of(at * 64, 64), 64)
                        total = landed[GROUP - 2, rows, :].astype(jnp.float32)
                        for back in range(1, GROUP - 1):
                            total = total + jnp.where(mine + back >= GROUP, landed[back - 1, rows, :].astype(jnp.float32), 0.0)
                        relay[rows, :] = total.astype(relay.dtype)
                        return inner

                    lax.fori_loop(0, relay.shape[0] // 64, relayed, 0)
                    down_copy(band - GROUP).start()
            @pl.when(t == 13)
            def _():
                @pl.when((mine > 0) & (band + GROUP < bands))
                def _():
                    down_copy(band + GROUP).wait_recv()

                def settled(at, inner):
                    rows = pl.ds(pl.multiple_of(at * 64, 64), 64)
                    total = jnp.where((mine > 0) & (band + GROUP < bands), from_up[rows, :].astype(jnp.float32), 0.0)
                    for back in range(1, GROUP):
                        total = total + jnp.where(mine + back < GROUP, landed[back - 1, rows, :].astype(jnp.float32), 0.0)
                    back_out[head, rows, :] = total.astype(back_out.dtype)
                    return inner

                lax.fori_loop(0, relay.shape[0] // 64, settled, 0)
                pair_copy(head).start()
        return carry

    lax.fori_loop(0, count + REDUCE_GAP * depth, body, 0)

    if has_context:
        def add_squares(m, total):
            block = out_ref[m]
            for top in range(0, block.shape[0], 8):
                for left in range(0, block.shape[1], LANES):
                    part = block[top : top + 8, left : left + LANES]
                    total = total + part * part
            return total

        squares_ref[...] = lax.fori_loop(0, count, add_squares, jnp.zeros(squares_ref.shape, jnp.float32))

    if has_context:
        for back in range(1, GROUP):
            @pl.when((mine >= back) | (band >= GROUP))
            def _():
                for one in range(PIECES):
                    peer_copy(back, one).wait_send()
        @pl.when((mine > 0) & (band >= GROUP))
        def _():
            down_copy(band - GROUP).wait_send()
        pair_copy(head).wait_send()
        pair_copy(1 - head).wait_recv()

    def drain(m, carry):
        for stage in range(depth):
            for color in range(2):
                phase, step = stages[color][stage]
                for way in range(2):
                    present, rank, index, copy = outgoing(m, color, phase, step, way)
                    @pl.when(present)
                    def _():
                        copy(own_block(m, color, phase, index)).wait_send()
        return carry

    lax.fori_loop(0, count, drain, 0)


def reduce_grads(bands, grads, returned, collective_id):
    dims = band_dims(bands)
    count = sum(part.shape[0] for part in grads)
    depth_rows, width = grads[0].shape[1:]
    rows = depth_rows // bands
    half = width // 2
    depth = len(stage_list(dims, ORDERS[0]))
    vmem = pl.BlockSpec(memory_space=pltpu.VMEM)
    anyspace = pl.BlockSpec(memory_space=pl.ANY)
    slots = lambda size: 1 if size == 2 else 2 * (size - 1)
    inner = dims[1]
    has_context = returned is not None
    grads = [part.reshape(-1, *dims, rows, width) for part in grads]
    scratch = [
        pltpu.VMEM((count, *grads[0].shape[1:]), jnp.bfloat16),
        pltpu.SemaphoreType.DMA((count,)),
        pltpu.VMEM((count, 2, slots(inner), dims[0], inner, rows, half), jnp.bfloat16),
        pltpu.VMEM((count, 2, slots(dims[0]), inner, rows, half), jnp.bfloat16),
        pltpu.VMEM((count, 2, slots(inner), rows, half), jnp.bfloat16),
        pltpu.SemaphoreType.DMA((2, depth, 2, count)),
        pltpu.SemaphoreType.DMA((2, depth, 2, count)),
    ]
    args = list(grads)
    in_specs = [anyspace] * len(grads)
    out_shape = [jax.ShapeDtypeStruct((count, rows, width), jnp.float32)]
    if has_context:
        args.append(returned)
        in_specs.append(vmem)
        ctx_shape = returned.shape[1:]
        out_shape += [
            jax.ShapeDtypeStruct((2, *ctx_shape), returned.dtype), jax.ShapeDtypeStruct((8, LANES), jnp.float32)
        ]
        scratch += [
            pltpu.VMEM(returned.shape, returned.dtype),
            pltpu.VMEM(ctx_shape, returned.dtype),
            pltpu.VMEM(ctx_shape, returned.dtype),
            pltpu.SemaphoreType.DMA((GROUP - 1, PIECES)),
            pltpu.SemaphoreType.DMA((GROUP - 1, PIECES)),
            pltpu.SemaphoreType.DMA((2,)),
            pltpu.SemaphoreType.DMA((2,)),
        ]
    return pl.pallas_call(
        partial(reduce_kernel, dims, len(grads), has_context),
        out_shape=out_shape,
        in_specs=in_specs,
        out_specs=[vmem] * len(out_shape),
        scratch_shapes=scratch,
        compiler_params=pltpu.CompilerParams(
            collective_id=collective_id, has_side_effects=True, vmem_limit_bytes=67043328
        ),
        cost_estimate=worth(1),
        name="reduce_grads",
    )(*args)


def norm_rows(values, gain_row):
    centre = values - jnp.mean(values, axis=-1, keepdims=True)
    spread = jnp.mean(centre * centre, axis=-1, keepdims=True)
    return centre * lax.rsqrt(spread + EPS) * gain_row


def matmul(former, latter):
    return jnp.dot(former, latter, preferred_element_type=jnp.float32)


def matmul_t(former, latter):
    return lax.dot_general(
        former, latter, (((1,), (1,)), ((), ())), preferred_element_type=jnp.float32
    )


def inner_t(former, latter):
    return lax.dot_general(
        former, latter, (((0,), (0,)), ((), ())), preferred_element_type=jnp.float32
    )


def worth(microseconds):
    return pl.CostEstimate(flops=microseconds * 10**9, bytes_accessed=0, transcendentals=0)


def norm_stats(rows):
    centre = rows - jnp.mean(rows, axis=-1, keepdims=True)
    inverse = lax.rsqrt(jnp.mean(centre * centre, axis=-1, keepdims=True) + EPS)
    return centre * inverse, inverse


def norm_pull(rows, gain_row, grad):
    unit, inverse = norm_stats(rows)
    scaled = grad * gain_row
    inner = jnp.mean(scaled * unit, axis=-1, keepdims=True)
    pulled = inverse * (scaled - jnp.mean(scaled, axis=-1, keepdims=True) - unit * inner)
    return pulled, jnp.sum(grad * unit, axis=0, keepdims=True)


def greet_pair():
    pl.semaphore_signal(
        pltpu.get_barrier_semaphore(), inc=1,
        device_id=(lax.axis_index("band"), 1 - lax.axis_index("head")), device_id_type=MESH,
    )


def pair_send(source, target, send_sem, recv_sem):
    return pltpu.make_async_remote_copy(
        source, target, send_sem, recv_sem,
        device_id=(lax.axis_index("band"), 1 - lax.axis_index("head")), device_id_type=MESH,
    )


def mlp_kernel(
    hidden_ref, incoming_ref, gain_ref, up_ref, down_ref,
    block_ref, grad_ref, gain_grad_ref, grad_up_ref, grad_down_ref,
    normed, normed_t, incoming_t, out_sum, back_sum, low, there, send_sem, recv_sem,
):
    step, last = pl.program_id(0), pl.num_programs(0) - 1
    rows = hidden_ref.shape[0]
    tile = 64

    @pl.when(step == 0)
    def _():
        greet_pair()

        def one(at, carry):
            part = pl.ds(pl.multiple_of(at * tile, tile), tile)
            unit, _ = norm_stats(hidden_ref[part, :])
            normed[part, :] = (unit * gain_ref[...]).astype(jnp.bfloat16)
            return carry

        lax.fori_loop(0, rows // tile, one, 0)
        normed_t[...] = normed[...].T
        incoming_t[...] = incoming_ref[...].T
        out_sum[...] = jnp.zeros_like(out_sum)
        back_sum[...] = jnp.zeros_like(back_sum)

    copies = [pair_send(low.at[one], there.at[one], send_sem.at[one], recv_sem.at[one]) for one in range(2)]
    before = matmul(normed[...], up_ref[...])
    share = 0.5 * (1.0 + lax.erf(before * 2.0**-0.5))
    activated = (before * share).astype(jnp.bfloat16)
    out_sum[...] += matmul_t(activated, down_ref[...])

    @pl.when(step == last)
    def _():
        pl.semaphore_wait(pltpu.get_barrier_semaphore(), 1)
        low[0] = out_sum[...].astype(jnp.bfloat16)
        copies[0].start()

    slope = share + before * jnp.exp(before * before * -0.5) * (2.0 * math.pi) ** -0.5
    grad_before = (matmul(incoming_ref[...], down_ref[...]) * slope).astype(jnp.bfloat16)
    back_sum[...] += matmul_t(grad_before, up_ref[...])

    @pl.when(step == last)
    def _():
        low[1] = back_sum[...].astype(jnp.bfloat16)
        copies[1].start()

    grad_down_ref[...] = matmul(incoming_t[...], activated).astype(jnp.bfloat16)
    grad_up_ref[...] = matmul(normed_t[...], grad_before).astype(jnp.bfloat16)

    @pl.when(step == last)
    def _():
        for copy in copies:
            copy.wait()
        gain_grad_ref[...] = jnp.zeros_like(gain_grad_ref)

        def one(at, carry):
            part = pl.ds(pl.multiple_of(at * tile, tile), tile)
            total = lambda which: low[which, part, :].astype(jnp.float32) + there[which, part, :].astype(jnp.float32)
            hidden = hidden_ref[part, :]
            block_ref[part, :] = (hidden + total(0)).astype(jnp.bfloat16)
            pulled, gain_part = norm_pull(hidden, gain_ref[...], total(1))
            grad_ref[part, :] = incoming_ref[part, :].astype(jnp.float32) + pulled
            gain_grad_ref[...] += gain_part
            return carry

        lax.fori_loop(0, rows // tile, one, 0)


def mlp_both_ways(hidden, incoming, gain_row, weights, first, w_down, collective_id):
    rows, width = hidden.shape
    units, cut = w_down.shape[1], weights.shape[2]
    whole = pl.BlockSpec((rows, width), lambda step: (0, 0))
    line = pl.BlockSpec((1, width), lambda step: (0, 0))
    columns = pl.BlockSpec((width, cut), lambda step: (0, step))
    up_matrix = pl.BlockSpec((None, width, cut), lambda step: (first + step, 0, 0))
    grad_matrix = pl.BlockSpec((None, width, cut), lambda step: (step, 0, 0))
    return pl.pallas_call(
        mlp_kernel,
        grid=(units // cut,),
        in_specs=[whole, whole, line, up_matrix, columns],
        out_specs=[whole, whole, line, grad_matrix, columns],
        out_shape=[
            jax.ShapeDtypeStruct((rows, width), jnp.bfloat16),
            jax.ShapeDtypeStruct((rows, width), jnp.float32),
            jax.ShapeDtypeStruct((1, width), jnp.float32),
            jax.ShapeDtypeStruct((units // cut, width, cut), jnp.bfloat16),
            jax.ShapeDtypeStruct((width, units), jnp.bfloat16),
        ],
        scratch_shapes=[
            pltpu.VMEM((rows, width), jnp.bfloat16),
            pltpu.VMEM((width, rows), jnp.bfloat16),
            pltpu.VMEM((width, rows), jnp.bfloat16),
            pltpu.VMEM((rows, width), jnp.float32),
            pltpu.VMEM((rows, width), jnp.float32),
            pltpu.VMEM((2, rows, width), jnp.bfloat16),
            pltpu.VMEM((2, rows, width), jnp.bfloat16),
            pltpu.SemaphoreType.DMA((2,)),
            pltpu.SemaphoreType.DMA((2,)),
        ],
        compiler_params=pltpu.CompilerParams(
            collective_id=collective_id, has_side_effects=True, vmem_limit_bytes=63 * 1024 * 1024
        ),
        cost_estimate=worth(1),
        name="mlp_both_ways",
    )(hidden, incoming, gain_row, weights, w_down)


def row_kernel(backward, follows, *refs):
    refs = list(refs)
    x_ref, w_ref, base_ref, gain_ref = refs[:4]
    rest = refs[4:]
    hidden_ref = rest.pop(0) if backward else None
    next_ref = rest.pop(0) if follows else None
    sum_ref = rest.pop(0)
    low_ref, next_out_ref = (rest.pop(0), rest.pop(0)) if follows else (None, None)
    gain_grad_ref = rest.pop(0) if backward else None
    low, there, send_sem, recv_sem = rest
    rows = x_ref.shape[0]
    cut = rows // send_sem.shape[0]
    greet_pair()

    def part_of(at):
        return pl.ds(pl.multiple_of(at * cut, cut), cut)

    def copy_of(at):
        return pair_send(low.at[part_of(at)], there.at[part_of(at)], send_sem.at[at], recv_sem.at[at])

    for at in range(rows // cut):
        low[part_of(at), :] = matmul_t(x_ref[part_of(at), :], w_ref[...]).astype(jnp.bfloat16)
        if at == 0:
            pl.semaphore_wait(pltpu.get_barrier_semaphore(), 1)
        copy_of(at).start()
    if backward:
        gain_grad_ref[...] = jnp.zeros_like(gain_grad_ref)

    def finish(at, carry):
        part = part_of(at)
        copy_of(at).wait()
        total = low[part, :].astype(jnp.float32) + there[part, :].astype(jnp.float32)
        base = base_ref[part, :].astype(jnp.float32)
        if backward:
            pulled, gain_part = norm_pull(hidden_ref[part, :], gain_ref[...], total)
            gain_grad_ref[...] += gain_part
            result = base + pulled
            passed_on = result.astype(jnp.bfloat16)
        else:
            result = base + total
            if follows:
                passed_on = (norm_stats(result)[0] * gain_ref[...]).astype(jnp.bfloat16)
        sum_ref[part, :] = result
        if follows:
            low_ref[part, :] = passed_on
            next_out_ref[part, :] = matmul(passed_on, next_ref[...]).astype(jnp.bfloat16)
        return carry

    lax.fori_loop(0, rows // cut, finish, 0)


def row_step(x, weights, at, base, gain_row, collective_id, hidden=None, follow=None):
    rows, width = base.shape
    units = x.shape[1]
    backward, follows = hidden is not None, follow is not None
    whole = pl.BlockSpec((rows, width), lambda step: (0, 0))
    narrow = pl.BlockSpec((rows, units), lambda step: (0, 0))
    line = pl.BlockSpec((1, width), lambda step: (0, 0))
    matrix = lambda which: pl.BlockSpec((None, width, units), lambda step: (which, 0, 0))
    args, in_specs = [x, weights, base, gain_row], [narrow, matrix(at), whole, line]
    out_specs, out_shape = [whole], [jax.ShapeDtypeStruct((rows, width), jnp.float32)]
    if backward:
        args.append(hidden)
        in_specs.append(whole)
    if follows:
        args.append(weights)
        in_specs.append(matrix(follow))
        out_specs += [whole, narrow]
        out_shape += [
            jax.ShapeDtypeStruct((rows, width), jnp.bfloat16), jax.ShapeDtypeStruct((rows, units), jnp.bfloat16)
        ]
    if backward:
        out_specs.append(line)
        out_shape.append(jax.ShapeDtypeStruct((1, width), jnp.float32))
    cuts = 4
    return pl.pallas_call(
        partial(row_kernel, backward, follows),
        grid=(1,),
        in_specs=in_specs,
        out_specs=out_specs,
        out_shape=out_shape,
        scratch_shapes=[
            pltpu.VMEM((rows, width), jnp.bfloat16),
            pltpu.VMEM((rows, width), jnp.bfloat16),
            pltpu.SemaphoreType.DMA((cuts,)),
            pltpu.SemaphoreType.DMA((cuts,)),
        ],
        compiler_params=pltpu.CompilerParams(
            collective_id=collective_id, has_side_effects=True, vmem_limit_bytes=63 * 1024 * 1024
        ),
        cost_estimate=worth(1),
        name="row_step",
    )(*args)


def adamw_kernel(rate, factor_ref, *refs):
    ins, outs = refs[:12], refs[12:]
    first_grads, up_grad, down_grad = ins[:3]
    factor = factor_ref[0]

    def update(state, results, at, gradient):
        weight, one, two = (ref[at] for ref in state)
        for result, value in zip(results, adamw_update(weight, one, two, gradient * factor, rate, DECAY)):
            result[at] = value

    proj, out, mlp = ins[3:6], ins[6:9], ins[9:12]
    new_proj, new_out, new_mlp = outs[:3], outs[3:6], outs[6:9]
    for at in range(proj[0].shape[0]):
        update(proj, new_proj, at, first_grads[at])
    for at in range(out[0].shape[0]):
        update(out, new_out, at, first_grads[proj[0].shape[0] + at])
    update(mlp, new_mlp, 0, up_grad[...])
    update(mlp, new_mlp, 1, down_grad[...])


def adamw_all(factor, summed, down_sum, proj, out, mlp, rate):
    rows, width = summed.shape[1:]
    steps = mlp[0].shape[2] // width
    cut = width // steps
    narrow = lambda count: pl.BlockSpec((count, rows, cut), lambda step: (0, 0, step))
    first = proj[0].shape[0] + out[0].shape[0]
    proj_spec, out_spec = narrow(proj[0].shape[0]), narrow(out[0].shape[0])
    mlp_spec = pl.BlockSpec((2, rows, width), lambda step: (0, 0, step))
    state_specs = [proj_spec] * 3 + [out_spec] * 3 + [mlp_spec] * 3
    state = [*proj, *out, *mlp]
    results = pl.pallas_call(
        partial(adamw_kernel, rate),
        grid=(steps,),
        in_specs=[
            pl.BlockSpec(memory_space=pltpu.SMEM),
            narrow(first),
            pl.BlockSpec((None, rows, width), lambda step: (first + step, 0, 0)),
            pl.BlockSpec((rows, width), lambda step: (0, step)),
            *state_specs,
        ],
        out_specs=state_specs,
        out_shape=[jax.ShapeDtypeStruct(part.shape, part.dtype) for part in state],
        name="adamw_all",
    )(factor.reshape(1), summed, summed, down_sum, *state)
    return results[:3], results[3:6], results[6:]


def finish_kernel(tokens_ref, gain_ref, own_ref, there_ref, came_ref, grad_ref, tokens_out, text_out, gain_grad_ref):
    band_rows, text_rows = tokens_ref.shape[0], text_out.shape[0]
    tile = 64

    @pl.when(pl.program_id(0) == 0)
    def _():
        gain_grad_ref[...] = jnp.zeros_like(gain_grad_ref)

    def total_of(part):
        own = own_ref[part, :].astype(jnp.float32) + there_ref[part, :].astype(jnp.float32)
        return own + came_ref[part, :].astype(jnp.float32)

    def one(at, carry):
        part = pl.ds(pl.multiple_of(at * tile, tile), tile)
        pulled, gain_part = norm_pull(tokens_ref[part, :].astype(jnp.float32), gain_ref[...], total_of(part))
        tokens_out[part, :] = grad_ref[part, :] + pulled
        gain_grad_ref[...] += gain_part
        return carry

    def text(at, carry):
        start = pl.multiple_of(at * tile, tile)
        text_out[pl.ds(start, tile), :] = total_of(pl.ds(pl.multiple_of(start + band_rows, tile), tile))
        return carry

    lax.fori_loop(0, band_rows // tile, one, 0)
    lax.fori_loop(0, text_rows // tile, text, 0)


def finish_rows(tokens, gain_row, own, there, came, grad_one):
    streams, band_rows, width = tokens.shape
    text_rows = own.shape[1] - band_rows
    block = lambda rows: pl.BlockSpec((None, rows, width), lambda stream: (stream, 0, 0))
    line = pl.BlockSpec((1, width), lambda stream: (0, 0))
    both = band_rows + text_rows
    return pl.pallas_call(
        finish_kernel,
        grid=(streams,),
        in_specs=[block(band_rows), line, block(both), block(both), block(both), block(band_rows)],
        out_specs=[block(band_rows), block(text_rows), line],
        out_shape=[
            jax.ShapeDtypeStruct((streams, band_rows, width), jnp.float32),
            jax.ShapeDtypeStruct((streams, text_rows, width), jnp.float32),
            jax.ShapeDtypeStruct((1, width), jnp.float32),
        ],
        name="finish_rows",
    )(tokens, gain_row, own, there, came, grad_one)


def heads_of(block):
    lane = lax.broadcasted_iota(jnp.int32, block.shape, 1) // HEAD_DIM
    return [
        block * (lane == one).astype(jnp.float32).astype(block.dtype) for one in range(LANES // HEAD_DIM)
    ]


def shifted(scores, causal, behind):
    if not causal or behind > 0:
        return scores
    key_ids = lax.broadcasted_iota(jnp.int32, scores.shape, 0)
    query_ids = lax.broadcasted_iota(jnp.int32, scores.shape, 1)
    return jnp.where(key_ids <= query_ids, scores, NEG)


def attend_body(reach, causal, q_ref, k_ref, v_ref, out_ref, total_ref):
    scale = HEAD_DIM**-0.5
    values_t = [v_ref[behind].T for behind in range(reach)]
    outs = []
    for one, q_one in enumerate(heads_of(q_ref[...])):
        scores = [shifted(matmul_t(k_ref[behind], q_one) * scale, causal, behind) for behind in range(reach)]
        top = jnp.max(scores[0], axis=0, keepdims=True)
        for block in scores[1:]:
            top = jnp.maximum(top, jnp.max(block, axis=0, keepdims=True))
        raised = [jnp.exp(block - top) for block in scores]
        total = jnp.sum(raised[0], axis=0, keepdims=True)
        for block in raised[1:]:
            total = total + jnp.sum(block, axis=0, keepdims=True)
        share = 1.0 / total
        mixed = None
        for behind in range(reach):
            part = matmul(values_t[behind], (raised[behind] * share).astype(jnp.bfloat16))
            mixed = part if mixed is None else mixed + part
        outs.append(mixed[one * HEAD_DIM : (one + 1) * HEAD_DIM])
        total_ref[one : one + 1, :] = top + jnp.log(total)
    out_ref[...] = jnp.concatenate(outs, axis=0).T.astype(jnp.bfloat16)


def attend_back_body(reach, causal, q_ref, k_ref, v_ref, total_ref, g_ref, dq_ref, dk_ref, dv_ref):
    scale = HEAD_DIM**-0.5
    keys_t = [k_ref[behind].T for behind in range(reach)]
    q_heads, g_heads = heads_of(q_ref[...]), heads_of(g_ref[...])
    query_grads = []
    key_grads, value_grads = [None] * reach, [None] * reach
    for one in range(len(q_heads)):
        q_one, g_one = q_heads[one], g_heads[one]
        log_total = total_ref[one : one + 1, :]
        probs, grads, centre = [], [], None
        for behind in range(reach):
            scores = shifted(matmul_t(k_ref[behind], q_one) * scale, causal, behind)
            probs.append(jnp.exp(scores - log_total))
            grads.append(matmul_t(v_ref[behind], g_one))
            part = jnp.sum(grads[-1] * probs[-1], axis=0, keepdims=True)
            centre = part if centre is None else centre + part
        query_grad = None
        for behind in range(reach):
            grad_scores = (probs[behind] * (grads[behind] - centre)).astype(jnp.bfloat16)
            part = matmul(keys_t[behind], grad_scores)
            query_grad = part if query_grad is None else query_grad + part
            key_part = matmul(grad_scores, q_one)
            value_part = matmul(probs[behind].astype(jnp.bfloat16), g_one)
            key_grads[behind] = key_part if one == 0 else key_grads[behind] + key_part
            value_grads[behind] = value_part if one == 0 else value_grads[behind] + value_part
        query_grads.append(query_grad[one * HEAD_DIM : (one + 1) * HEAD_DIM])
    dq_ref[...] = (jnp.concatenate(query_grads, axis=0).T * scale).astype(jnp.bfloat16)
    for behind in range(dk_ref.shape[0]):
        if behind < reach:
            dk_ref[behind] = (key_grads[behind] * scale).astype(jnp.bfloat16)
            dv_ref[behind] = value_grads[behind].astype(jnp.bfloat16)
        else:
            dk_ref[behind] = jnp.zeros(dk_ref.shape[1:], dk_ref.dtype)
            dv_ref[behind] = jnp.zeros(dv_ref.shape[1:], dv_ref.dtype)


def by_offset(body, causal, offset_ref, *refs):
    reaches = refs[1].shape[0]
    if reaches == 1:
        body(1, causal, *refs)
        return
    offset = offset_ref[pl.program_id(0)]
    for earlier_bands in range(reaches):
        @pl.when(offset == earlier_bands)
        def _():
            body(earlier_bands + 1, causal, *refs)


def attention_specs(queries, keys):
    rows, reaches, key_rows = queries.shape[1], keys.shape[1], keys.shape[2]
    row_spec = pl.BlockSpec((None, rows, LANES), lambda stream, pair: (stream, 0, pair))
    key_spec = pl.BlockSpec((None, reaches, key_rows, LANES), lambda stream, pair: (stream, 0, 0, pair))
    total_spec = pl.BlockSpec((None, None, 8, rows), lambda stream, pair: (stream, pair, 0, 0))
    return row_spec, key_spec, total_spec


def attention(queries, keys, values, offsets, causal):
    streams, rows, width = queries.shape
    row_spec, key_spec, total_spec = attention_specs(queries, keys)
    return pl.pallas_call(
        partial(by_offset, attend_body, causal),
        grid=(streams, width // LANES),
        in_specs=[pl.BlockSpec(memory_space=pltpu.SMEM), row_spec, key_spec, key_spec],
        out_specs=[row_spec, total_spec],
        out_shape=[
            jax.ShapeDtypeStruct(queries.shape, jnp.bfloat16),
            jax.ShapeDtypeStruct((streams, width // LANES, 8, rows), jnp.float32),
        ],
        cost_estimate=worth(1),
        name="attend",
    )(offsets, queries, keys, values)


def attention_back(queries, keys, values, offsets, totals, grad_out, causal):
    streams, rows, width = queries.shape
    row_spec, key_spec, total_spec = attention_specs(queries, keys)
    return pl.pallas_call(
        partial(by_offset, attend_back_body, causal),
        grid=(streams, width // LANES),
        in_specs=[pl.BlockSpec(memory_space=pltpu.SMEM), row_spec, key_spec, key_spec, total_spec, row_spec],
        out_specs=[row_spec, key_spec, key_spec],
        out_shape=[
            jax.ShapeDtypeStruct(queries.shape, jnp.bfloat16),
            jax.ShapeDtypeStruct(keys.shape, jnp.bfloat16),
            jax.ShapeDtypeStruct(keys.shape, jnp.bfloat16),
        ],
        cost_estimate=worth(1),
        name="attend_back",
    )(offsets, queries, keys, values, totals, grad_out)


def swap_kernel(count, *refs):
    sources, targets = refs[:count], refs[count : 2 * count]
    send_sem, recv_sem = refs[2 * count :]
    band, head = lax.axis_index("band"), lax.axis_index("head")
    barrier = pltpu.get_barrier_semaphore()
    pl.semaphore_signal(barrier, inc=1, device_id=(band, 1 - head), device_id_type=MESH)
    pl.semaphore_wait(barrier, 1)
    copies = [
        pltpu.make_async_remote_copy(
            sources[one], targets[one], send_sem.at[one], recv_sem.at[one],
            device_id=(band, 1 - head), device_id_type=MESH,
        )
        for one in range(count)
    ]
    for copy in copies:
        copy.start()
    for copy in copies:
        copy.wait()


def swapped(collective_id, *arrays):
    vmem = pl.BlockSpec(memory_space=pltpu.VMEM)
    return pl.pallas_call(
        partial(swap_kernel, len(arrays)),
        out_shape=[jax.ShapeDtypeStruct(array.shape, array.dtype) for array in arrays],
        in_specs=[vmem] * len(arrays),
        out_specs=[vmem] * len(arrays),
        scratch_shapes=[pltpu.SemaphoreType.DMA((len(arrays),)), pltpu.SemaphoreType.DMA((len(arrays),))],
        compiler_params=pltpu.CompilerParams(collective_id=collective_id, has_side_effects=True),
        cost_estimate=worth(1),
        name="swap_heads",
    )(*arrays)


def total_kernel(dims, in_ref, out_ref, near, far, send_sem, recv_sem):
    head = lax.axis_index("head")
    band, place = place_of(dims)
    layer = dims[1] * dims[2]
    inside = (band % layer) * 2 + head
    lines = [
        (near, layer * 2, inside, lambda at: (place[0] * layer + at // 2, at % 2)),
        (far, dims[0], place[0], lambda at: (at * layer + band % layer, head)),
    ]
    barrier = pltpu.get_barrier_semaphore()
    for _, size, mine, device in lines:
        for shift in range(1, size):
            pl.semaphore_signal(barrier, inc=1, device_id=device((mine + shift) % size), device_id_type=MESH)
    pl.semaphore_wait(barrier, sum(size - 1 for _, size, _, _ in lines))
    total = in_ref[...]
    for line, (slots, size, mine, device) in enumerate(lines):
        slots[mine] = total

        def copy(there, shift):
            return pltpu.make_async_remote_copy(
                slots.at[mine], slots.at[mine], send_sem.at[line, shift - 1], recv_sem.at[line, shift - 1],
                device_id=device(there), device_id_type=MESH,
            )

        def incoming(there, shift):
            return pltpu.make_async_remote_copy(
                slots.at[there], slots.at[there], send_sem.at[line, shift - 1], recv_sem.at[line, shift - 1],
                device_id=device(there), device_id_type=MESH,
            )

        for shift in range(1, size):
            copy((mine + shift) % size, shift).start()
        for shift in range(1, size):
            incoming((mine + size - shift) % size, shift).wait_recv()
        total = slots[0]
        for at in range(1, size):
            total = total + slots[at]
        for shift in range(1, size):
            copy((mine + shift) % size, shift).wait_send()
    out_ref[...] = total


def mesh_total(bands, tile, collective_id):
    dims = band_dims(bands)
    near = dims[1] * dims[2] * 2
    longest = max(dims[0], near)
    vmem = pl.BlockSpec(memory_space=pltpu.VMEM)
    return pl.pallas_call(
        partial(total_kernel, dims),
        out_shape=jax.ShapeDtypeStruct(tile.shape, tile.dtype),
        in_specs=[vmem],
        out_specs=vmem,
        scratch_shapes=[
            pltpu.VMEM((near, *tile.shape), tile.dtype),
            pltpu.VMEM((dims[0], *tile.shape), tile.dtype),
            pltpu.SemaphoreType.DMA((2, longest - 1)),
            pltpu.SemaphoreType.DMA((2, longest - 1)),
        ],
        compiler_params=pltpu.CompilerParams(collective_id=collective_id, has_side_effects=True),
        cost_estimate=worth(1),
        name="mesh_total",
    )(tile)


def adamw_update(weight, moment_one, moment_two, gradient, step_rate, decay_rate):
    moment_one_new = BETA_ONE * moment_one + (1.0 - BETA_ONE) * gradient
    moment_two_new = BETA_TWO * moment_two + (1.0 - BETA_TWO) * gradient * gradient
    unbiased_one = moment_one_new / (1.0 - BETA_ONE**STEP)
    unbiased_two = moment_two_new / (1.0 - BETA_TWO**STEP)
    weight_new = weight - step_rate * (
        unbiased_one / (jnp.sqrt(unbiased_two) + ADAM_EPS) + decay_rate * weight
    )
    return (weight_new, moment_one_new, moment_two_new)


def local(
    tokens,
    text_states,
    cotangent,
    earlier,
    proj_master,
    out_master,
    mlp_master,
    gain_master,
    proj_first,
    proj_second,
    out_first,
    out_second,
    mlp_first,
    mlp_second,
    gain_first,
    gain_second,
):
    streams, band_rows, model_width = tokens.shape
    row_count = streams * band_rows
    text_rows = text_states.shape[1]
    bands, head = lax.axis_size("band"), lax.axis_index("head")
    shard_rows, width = proj_master.shape[1:]
    chunks = mlp_master.shape[2] // width
    up_cut = mlp_master[0].reshape(shard_rows, chunks, width).transpose(1, 0, 2)
    shard = jnp.concatenate([proj_master, out_master, up_cut]).astype(jnp.bfloat16)
    gain_low = gain_master.astype(jnp.bfloat16).astype(jnp.float32)
    gain_tile = jnp.pad(gain_low, ((0, 5), (0, LANES - shard_rows)))
    both = jnp.concatenate([tokens, text_states], axis=1)
    context = lax.dynamic_index_in_dim(both, head, 0, keepdims=False)
    gathered, gain_tiles, passed = gather_weights(bands, shard, gain_tile, context, 1)
    down_low, gain_tiles = lax.optimization_barrier((mlp_master[1].astype(jnp.bfloat16), gain_tiles))
    w_down = lax.all_gather(down_low, "band", axis=0, tiled=True)
    weights = gathered.reshape(shard.shape[0], model_width, width)
    w_query, w_key, w_value, _, w_text_key, w_text_value, _, w_cross_out = (weights[at] for at in range(8))
    gains = gain_tiles.reshape(bands, 8, LANES)[:, :3, :shard_rows].transpose(1, 0, 2).reshape(3, model_width)

    offsets = earlier[:, 0]
    reach_ids = jnp.arange(SEQ_BANDS)
    within = reach_ids[None, :] <= offsets[:, None]
    reached = jnp.concatenate([tokens[:, None], passed[:, :, :band_rows]], axis=1)
    normed_all = jnp.where(
        within[:, :, None, None], norm_rows(reached.astype(jnp.float32), gains[0]), 0.0
    ).astype(jnp.bfloat16)
    normed_one = normed_all[:, 0].reshape(row_count, model_width)
    normed_all = normed_all.reshape(SEQ_BANDS * row_count, model_width)
    row_shape = (streams, band_rows, width)
    reach_shape = (streams, SEQ_BANDS, band_rows, width)
    text_shape = (streams, 1, text_rows, width)
    queries = matmul(normed_one, w_query).astype(jnp.bfloat16).reshape(row_shape)
    keys = matmul(normed_all, w_key).astype(jnp.bfloat16).reshape(reach_shape)
    values = matmul(normed_all, w_value).astype(jnp.bfloat16).reshape(reach_shape)
    attended, self_totals = attention(queries, keys, values, offsets, True)
    attended = attended.reshape(row_count, width)
    hidden_one, normed_two, cross_queries = row_step(
        attended, weights, 6, tokens.reshape(row_count, model_width), gains[1:2], 3, follow=3
    )
    cross_queries = cross_queries.reshape(row_shape)
    caption = text_states
    for behind in range(1, SEQ_BANDS):
        caption = jnp.where((offsets == behind)[:, None, None], passed[:, behind - 1, band_rows:], caption)
    caption = caption.reshape(streams * text_rows, model_width)
    cross_keys = matmul(caption, w_text_key).astype(jnp.bfloat16).reshape(text_shape)
    cross_values = matmul(caption, w_text_value).astype(jnp.bfloat16).reshape(text_shape)
    crossed, cross_totals = attention(cross_queries, cross_keys, cross_values, offsets, False)
    crossed = crossed.reshape(row_count, width)
    (hidden_two,) = row_step(crossed, weights, 7, hidden_one, gains[2:3], 4)
    incoming = cotangent.reshape(row_count, model_width)
    block_out, grad_two, gain_grad_three, grad_up, grad_down = mlp_both_ways(
        hidden_two, incoming, gains[2:3], weights, 8, w_down, 5
    )
    block_out = block_out.reshape(tokens.shape)
    gain_grad_three = gain_grad_three[0]
    down_sum = lax.psum_scatter(grad_down, "band", scatter_dimension=0, tiled=True).astype(jnp.float32)
    grad_two_low = grad_two.astype(jnp.bfloat16)
    grad_cross_out = inner_t(grad_two_low, crossed)
    grad_crossed = matmul(grad_two_low, w_cross_out).astype(jnp.bfloat16).reshape(row_shape)
    grad_cq, grad_ck, grad_cv = attention_back(
        cross_queries, cross_keys, cross_values, offsets, cross_totals, grad_crossed, False
    )
    grad_cq = grad_cq.reshape(row_count, width)
    grad_ck = grad_ck.reshape(streams * text_rows, width)
    grad_cv = grad_cv.reshape(streams * text_rows, width)
    text_part = (matmul_t(grad_ck, w_text_key) + matmul_t(grad_cv, w_text_value)).astype(jnp.bfloat16)
    text_part = text_part.reshape(text_states.shape)
    grad_one, grad_one_low, grad_attended, gain_grad_two = row_step(
        grad_cq, weights, 3, grad_two, gains[1:2], 7, hidden=hidden_one, follow=6
    )
    gain_grad_two = gain_grad_two[0]
    grad_self_out = inner_t(grad_one_low, attended)
    grad_attended = grad_attended.reshape(row_shape)
    grad_queries, grad_keys, grad_values = attention_back(
        queries, keys, values, offsets, self_totals, grad_attended, True
    )
    grad_queries = grad_queries.reshape(row_count, width)
    reach_part = matmul_t(grad_keys.reshape(-1, width), w_key) + matmul_t(grad_values.reshape(-1, width), w_value)
    reach_part = reach_part.reshape(streams, SEQ_BANDS, band_rows, model_width)
    own_part = matmul_t(grad_queries, w_query).reshape(tokens.shape) + reach_part[:, 0]
    own_text = jnp.where((offsets == 0)[:, None, None], text_part, 0).astype(jnp.bfloat16)
    sent_text = jnp.where(
        (offsets[:, None] == reach_ids[None, 1:])[:, :, None, None], text_part[:, None], 0
    ).astype(jnp.bfloat16)
    own_back = jnp.concatenate([own_part.astype(jnp.bfloat16), own_text], axis=1)
    sent_back = jnp.concatenate([reach_part[:, 1:].astype(jnp.bfloat16), sent_text], axis=2)
    mine = lax.dynamic_index_in_dim(sent_back, head, 0, keepdims=False)
    other = lax.dynamic_index_in_dim(sent_back, 1 - head, 0, keepdims=False)
    own_there, mine_there = swapped(8, own_back, other)
    returned = (mine.astype(jnp.float32) + mine_there.astype(jnp.float32)).astype(jnp.bfloat16)

    flat = lambda part: part.reshape(-1, width)
    grads = [
        part.astype(jnp.bfloat16)[None]
        for part in (
            inner_t(normed_one, grad_queries),
            inner_t(normed_all, flat(grad_keys)),
            inner_t(normed_all, flat(grad_values)),
            inner_t(normed_two, grad_cq),
            inner_t(caption, grad_ck),
            inner_t(caption, grad_cv),
            grad_self_out,
            grad_cross_out,
        )
    ]
    grads.append(grad_up)
    returned, down_sum = lax.optimization_barrier((returned, down_sum))
    summed, came_back, squares = reduce_grads(bands, grads, returned, 2)
    grad_tokens, grad_text, gain_grad_one = finish_rows(
        tokens, gains[0:1], own_back, own_there, came_back, grad_one.reshape(tokens.shape)
    )
    gain_grad_one = gain_grad_one[0]
    gain_rows = jnp.stack([gain_grad_one, gain_grad_two, gain_grad_three]).reshape(-1, LANES)
    down_square = jnp.sum(down_sum * down_sum) / (8 * LANES)
    tile = jnp.concatenate([gain_rows, squares + down_square])
    tile = mesh_total(bands, tile, 10)
    gain_total = 0.5 * tile[:-8].reshape(3, model_width)
    grad_norm = jnp.sqrt(jnp.sum(tile[-8:]) + jnp.sum(gain_total * gain_total))
    gain_grad = lax.dynamic_slice_in_dim(gain_total, lax.axis_index("band") * shard_rows, shard_rows, 1)
    factor = jnp.minimum(1.0, CLIP / grad_norm)
    new_proj, new_out, new_mlp = adamw_all(
        factor,
        summed,
        down_sum,
        (proj_master, proj_first, proj_second),
        (out_master, out_first, out_second),
        (mlp_master, mlp_first, mlp_second),
        2.0 * D ** (-0.5),
    )
    new_gain = adamw_update(
        gain_master, gain_first, gain_second, gain_grad * factor, GAIN_RATE, 0.0
    )
    return (
        block_out,
        grad_tokens,
        grad_text,
        grad_norm,
        new_proj[0],
        new_proj[1],
        new_proj[2],
        new_out[0],
        new_out[1],
        new_out[2],
        new_mlp[0],
        new_mlp[1],
        new_mlp[2],
        new_gain[0],
        new_gain[1],
        new_gain[2],
    )


def solution(mesh):
    return jax.shard_map(
        local,
        mesh=mesh,
        in_specs=(
            P(None, "band", None),
            P(None, "band", None),
            P(None, "band", None),
            P(None, "band"),
            P(None, "band", "head"),
            P(None, "band", "head"),
            P(None, "band", "head"),
            P(None, "band"),
            P(None, "band", "head"),
            P(None, "band", "head"),
            P(None, "band", "head"),
            P(None, "band", "head"),
            P(None, "band", "head"),
            P(None, "band", "head"),
            P(None, "band"),
            P(None, "band"),
        ),
        out_specs=(
            P(None, "band", None),
            P(None, "band", None),
            P(None, "band", None),
            P(),
            P(None, "band", "head"),
            P(None, "band", "head"),
            P(None, "band", "head"),
            P(None, "band", "head"),
            P(None, "band", "head"),
            P(None, "band", "head"),
            P(None, "band", "head"),
            P(None, "band", "head"),
            P(None, "band", "head"),
            P(None, "band"),
            P(None, "band"),
            P(None, "band"),
        ),
        check_vma=False,
    )
```

```python
import math
from functools import partial

import jax
import jax.numpy as jnp
from jax import lax
from jax.experimental import pallas as pl
from jax.experimental.pallas import tpu as pltpu
from jax.sharding import PartitionSpec as P

D = 1024
HEAD_DIM = 64
SEQ_BANDS = 4
STEP = 10


EPS = 1e-05
NEG = -1e30
CLIP = 1.0
BETA_ONE = 0.9
BETA_TWO = 0.95
ADAM_EPS = 1e-08
DECAY = 0.1
GAIN_RATE = 0.5
LANES = 128


MESH = pl.DeviceIdType.MESH
ORDERS = ((2, 0, 1), (1, 0, 2))
GROUP = 4
PIECES = 6
GAP = 2
REDUCE_GAP = 1


def band_dims(bands):
    inner = 4 if bands >= 64 else 2
    return (bands // (inner * inner), inner, inner)


def strides_of(dims):
    return (dims[1] * dims[2], dims[2], 1)


def place_of(dims):
    band = lax.axis_index("band")
    return band, (
        band // (dims[1] * dims[2]),
        (band // dims[2]) % dims[1],
        band % dims[2],
    )


def stage_list(dims, order):
    return [(phase, step) for phase in range(3) for step in range(dims[order[phase]] - 1)]


def block_of(ref, lead, place, order, phase, index, columns):
    at = list(place)
    for done in range(phase):
        at[order[done]] = slice(None)
    at[order[phase]] = index
    return ref.at[(*lead, *at, slice(None), columns)]


def greet(dims, place, band, head, extra):
    barrier = pltpu.get_barrier_semaphore()
    strides = strides_of(dims)
    total = jnp.int32(0)
    peers = []
    for axis in range(3):
        for sign in (1, -1):
            there = place[axis] + sign
            peers.append(((there >= 0) & (there < dims[axis]), band + sign * strides[axis], head))
    peers += extra
    for present, peer_band, peer_head in peers:
        @pl.when(present)
        def _():
            pl.semaphore_signal(barrier, inc=1, device_id=(peer_band, peer_head), device_id_type=MESH)
        total = total + present.astype(jnp.int32)
    pl.semaphore_wait(barrier, total)


def gather_kernel(dims, has_context, *refs):
    if has_context:
        (w_ref, gain_ref, ctx_ref, out_ref, gains_ref, ctx_out,
         own_sem, send_sem, recv_sem, gsend, grecv, prev_ref, up_sem, csend, crecv, psend, precv) = refs
    else:
        (w_ref, gain_ref, out_ref, gains_ref, own_sem, send_sem, recv_sem, gsend, grecv) = refs
    band, place = place_of(dims)
    head = lax.axis_index("head")
    strides = strides_of(dims)
    count = w_ref.shape[0]
    half = w_ref.shape[2] // 2
    bands = dims[0] * dims[1] * dims[2]
    true = band >= 0
    extra = []
    if has_context:
        base = (band // GROUP) * GROUP
        mine = band % GROUP
        for shift in range(1, GROUP):
            extra.append((true, base + (mine + shift) % GROUP, head))
        extra.append((band + GROUP < bands, band + GROUP, head))
        extra.append((band >= GROUP, band - GROUP, head))
        extra.append((true, band, 1 - head))
    greet(dims, place, band, head, extra)

    own = [
        pltpu.make_async_copy(w_ref, out_ref.at[:, place[0], place[1], place[2]], own_sem.at[0]),
        pltpu.make_async_copy(gain_ref, gains_ref.at[place[0], place[1], place[2]], own_sem.at[1]),
    ]
    for copy in own:
        copy.start()

    def up_copy():
        return pltpu.make_async_remote_copy(
            ctx_ref, prev_ref, up_sem.at[0], up_sem.at[1], device_id=(band + GROUP, head), device_id_type=MESH
        )

    def peer_copy(back, piece_at, source):
        cut = ctx_ref.shape[0] // PIECES
        rows = pl.ds(piece_at * cut, cut)
        return pltpu.make_async_remote_copy(
            source.at[rows], ctx_out.at[head, back - 1, rows], csend.at[back - 1, piece_at], crecv.at[back - 1, piece_at],
            device_id=(base + (mine + back) % GROUP, head), device_id_type=MESH,
        )

    def pair_copy(back):
        return pltpu.make_async_remote_copy(
            ctx_out.at[head, back - 1], ctx_out.at[head, back - 1], psend.at[back - 1], precv.at[back - 1],
            device_id=(band, 1 - head), device_id_type=MESH,
        )

    if has_context:
        @pl.when(band + GROUP < bands)
        def _():
            up_copy().start()

    def piece(color, m, phase, step, way, incoming):
        order = ORDERS[color]
        axis = order[phase]
        size, at = dims[axis], place[axis]
        toward = 1 if way == 0 else -1
        stage = stage_list(dims, order).index((phase, step))
        if incoming:
            index = at - toward * (step + 1)
            present = (index >= 0) & (index < size)
        else:
            index = at - toward * step
            present = (index >= 0) & (index < size) & (at + toward >= 0) & (at + toward < size)
        columns = pl.ds(color * half, half)
        target = (band + toward * strides[axis], head)
        land = block_of(out_ref, (m,), place, order, phase, index, columns)
        source = w_ref.at[m, :, columns] if stage == 0 else land
        copy = pltpu.make_async_remote_copy(
            source, land, send_sem.at[color, stage, way, m], recv_sem.at[color, stage, way, m],
            device_id=target, device_id_type=MESH,
        )
        return present, copy

    def gain_piece(phase, step, way, incoming):
        order = ORDERS[0]
        axis = order[phase]
        size, at = dims[axis], place[axis]
        toward = 1 if way == 0 else -1
        stage = stage_list(dims, order).index((phase, step))
        if incoming:
            index = at - toward * (step + 1)
            present = (index >= 0) & (index < size)
        else:
            index = at - toward * step
            present = (index >= 0) & (index < size) & (at + toward >= 0) & (at + toward < size)
        land = block_of(gains_ref, (), place, order, phase, index, slice(None))
        source = gain_ref if stage == 0 else land
        copy = pltpu.make_async_remote_copy(
            source, land, gsend.at[stage, way], grecv.at[stage, way],
            device_id=(band + toward * strides[axis], head), device_id_type=MESH,
        )
        return present, copy

    stages = [stage_list(dims, order) for order in ORDERS]
    depth = len(stages[0])

    def context_step(t):
        for one in range(PIECES):
            @pl.when(t == one)
            def _():
                for back in range(1, GROUP):
                    @pl.when(mine + back < GROUP)
                    def _():
                        peer_copy(back, one, ctx_ref).start()
        @pl.when((t == 4) & (band >= GROUP))
        def _():
            pltpu.make_async_remote_copy(
                ctx_ref, prev_ref, up_sem.at[0], up_sem.at[1], device_id=(band - GROUP, head), device_id_type=MESH
            ).wait_recv()
        for one in range(PIECES):
            @pl.when((t == 4 + one) & (band >= GROUP))
            def _():
                for back in range(1, GROUP):
                    @pl.when(mine + back >= GROUP)
                    def _():
                        peer_copy(back, one, prev_ref).start()
        @pl.when(t == 13)
        def _():
            for back in range(1, GROUP):
                @pl.when((mine >= back) | (band >= GROUP))
                def _():
                    for one in range(PIECES):
                        peer_copy(back, one, ctx_ref).wait_recv()
                    pair_copy(back).start()

    def gains_step(t):
        for stage in range(depth + 1):
            @pl.when(t == stage)
            def _():
                if stage == 1:
                    for copy in own:
                        copy.wait()
                if stage > 0:
                    for way in range(2):
                        present, copy = gain_piece(*stages[0][stage - 1], way, True)
                        @pl.when(present)
                        def _():
                            copy.wait_recv()
                if stage < depth:
                    for way in range(2):
                        present, copy = gain_piece(*stages[0][stage], way, False)
                        @pl.when(present)
                        def _():
                            copy.start()

    def body(t, carry):
        gains_step(t)
        if has_context:
            context_step(t)
        for stage in range(depth, -1, -1):
            m = t - GAP * stage
            @pl.when((m >= 0) & (m < count))
            def _():
                for color in range(2):
                    if stage > 0:
                        for way in range(2):
                            present, copy = piece(color, m, *stages[color][stage - 1], way, True)
                            @pl.when(present)
                            def _():
                                copy.wait_recv()
                    if stage < depth:
                        for way in range(2):
                            present, copy = piece(color, m, *stages[color][stage], way, False)
                            @pl.when(present)
                            def _():
                                copy.start()
        return carry

    lax.fori_loop(0, count + GAP * depth, body, 0)

    if has_context:
        for back in range(1, GROUP):
            @pl.when((mine >= back) | (band >= GROUP))
            def _():
                pltpu.make_async_remote_copy(
                    ctx_out.at[1 - head, back - 1], ctx_out.at[1 - head, back - 1], psend.at[back - 1],
                    precv.at[back - 1], device_id=(band, 1 - head), device_id_type=MESH,
                ).wait_recv()
                pair_copy(back).wait_send()
            @pl.when((mine + back < GROUP) | (band >= GROUP))
            def _():
                for one in range(PIECES):
                    peer_copy(back, one, ctx_ref).wait_send()
        @pl.when(band + GROUP < bands)
        def _():
            up_copy().wait_send()

    for stage in range(depth):
        for way in range(2):
            present, copy = gain_piece(*stages[0][stage], way, False)
            @pl.when(present)
            def _():
                copy.wait_send()

    def drain(m, carry):
        for stage in range(depth):
            for color in range(2):
                for way in range(2):
                    present, copy = piece(color, m, *stages[color][stage], way, False)
                    @pl.when(present)
                    def _():
                        copy.wait_send()
        return carry

    lax.fori_loop(0, count, drain, 0)


def gather_weights(bands, shard, gain_tile, context, collective_id):
    dims = band_dims(bands)
    count, rows, width = shard.shape
    depth = len(stage_list(dims, ORDERS[0]))
    vmem = pl.BlockSpec(memory_space=pltpu.VMEM)
    anyspace = pl.BlockSpec(memory_space=pl.ANY)
    has_context = context is not None
    out_shape = [
        jax.ShapeDtypeStruct((count, *dims, rows, width), shard.dtype),
        jax.ShapeDtypeStruct((*dims, *gain_tile.shape), gain_tile.dtype),
    ]
    scratch = [
        pltpu.SemaphoreType.DMA((2,)),
        pltpu.SemaphoreType.DMA((2, depth, 2, count)),
        pltpu.SemaphoreType.DMA((2, depth, 2, count)),
        pltpu.SemaphoreType.DMA((depth, 2)),
        pltpu.SemaphoreType.DMA((depth, 2)),
    ]
    args = [shard, gain_tile]
    if has_context:
        args.append(context)
        out_shape.append(jax.ShapeDtypeStruct((2, GROUP - 1, *context.shape), context.dtype))
        scratch += [
            pltpu.VMEM(context.shape, context.dtype),
            pltpu.SemaphoreType.DMA((2,)),
            pltpu.SemaphoreType.DMA((GROUP - 1, PIECES)),
            pltpu.SemaphoreType.DMA((GROUP - 1, PIECES)),
            pltpu.SemaphoreType.DMA((GROUP - 1,)),
            pltpu.SemaphoreType.DMA((GROUP - 1,)),
        ]
    return pl.pallas_call(
        partial(gather_kernel, dims, has_context),
        out_shape=out_shape,
        in_specs=[vmem] * len(args),
        out_specs=[anyspace] * len(out_shape),
        scratch_shapes=scratch,
        compiler_params=pltpu.CompilerParams(collective_id=collective_id, has_side_effects=True),
        cost_estimate=worth(200),
        name="gather_weights",
    )(*args)


def reduce_kernel(dims, arrays, has_context, *refs):
    sources = [ref.at[one] for ref in refs[:arrays] for one in range(ref.shape[0])]
    count, refs = len(sources), refs[arrays:]
    if has_context:
        (back_ref, out_ref, back_out, squares_ref, gv, load_sem, last_ref, mid_ref, first_ref, send_sem, recv_sem,
         landed, relay, from_up, csend, crecv, up_sem, pair_sem) = refs
    else:
        (out_ref, gv, load_sem, last_ref, mid_ref, first_ref, send_sem, recv_sem) = refs
    band, place = place_of(dims)
    head = lax.axis_index("head")
    strides = strides_of(dims)
    half = sources[0].shape[-1] // 2
    bands = dims[0] * dims[1] * dims[2]
    true = band >= 0
    orders = tuple(order[::-1] for order in ORDERS)
    lands = (last_ref, mid_ref, first_ref)

    def load(m, source):
        return pltpu.make_async_copy(source, gv.at[m], load_sem.at[m])

    for m in range(count):
        load(m, sources[m]).start()

    extra = []
    if has_context:
        base = (band // GROUP) * GROUP
        mine = band % GROUP
        for shift in range(1, GROUP):
            extra.append((true, base + (mine + shift) % GROUP, head))
        extra.append((band + GROUP < bands, band + GROUP, head))
        extra.append((band >= GROUP, band - GROUP, head))
        extra.append((true, band, 1 - head))
    greet(dims, place, band, head, extra)

    def peer_copy(back, piece_at):
        cut = relay.shape[0] // PIECES
        rows = pl.ds(piece_at * cut, cut)
        return pltpu.make_async_remote_copy(
            back_ref.at[back - 1, rows], landed.at[back - 1, rows],
            csend.at[back - 1, piece_at], crecv.at[back - 1, piece_at],
            device_id=(base + (mine + GROUP - back) % GROUP, head), device_id_type=MESH,
        )

    def down_copy(target):
        return pltpu.make_async_remote_copy(
            relay, from_up, up_sem.at[0], up_sem.at[1], device_id=(target, head), device_id_type=MESH
        )

    def pair_copy(stream):
        return pltpu.make_async_remote_copy(
            back_out.at[stream], back_out.at[stream], pair_sem.at[0], pair_sem.at[1],
            device_id=(band, 1 - head), device_id_type=MESH,
        )

    def slot(size, step, way):
        return 0 if size == 2 else step * 2 + way

    def own_block(m, color, phase, index):
        order = orders[color]
        at = list(place)
        for later in range(phase + 1, 3):
            at[order[later]] = slice(None)
        at[order[phase]] = index
        return gv.at[(m, *at, slice(None), pl.ds(color * half, half))]

    def landing(m, color, phase, step, way):
        size = dims[orders[color][phase]]
        return lands[phase].at[m, color, slot(size, step, way)]

    def outgoing(m, color, phase, step, way):
        axis = orders[color][phase]
        size, at = dims[axis], place[axis]
        toward = 1 if way == 0 else -1
        rank = at if way == 0 else size - 1 - at
        index = size - 1 - step + at if way == 0 else step + at - (size - 1)
        present = (rank <= step) & (at + toward >= 0) & (at + toward < size)
        stage = stage_list(dims, orders[color]).index((phase, step))
        target = (band + toward * strides[axis], head)

        def copy(source):
            return pltpu.make_async_remote_copy(
                source, landing(m, color, phase, step, way),
                send_sem.at[color, stage, way, m], recv_sem.at[color, stage, way, m],
                device_id=target, device_id_type=MESH,
            )

        return present, rank, index, copy

    def arrived(m, color, phase, step, way):
        axis = orders[color][phase]
        size, at = dims[axis], place[axis]
        before = at - 1 if way == 0 else at + 1
        rank = before if way == 0 else size - 1 - before
        present = (before >= 0) & (before < size) & (rank <= step)
        _, _, _, copy = outgoing(m, color, phase, step, way)
        return present, copy(landing(m, color, phase, step, way))

    def add_into(target, source):
        lead = target.shape[:-2]
        if len(lead) == 0:
            target[...] = target[...] + source[...]
        elif len(lead) == 1:
            for i in range(lead[0]):
                target[i] = target[i] + source[i]
        else:
            for i in range(lead[0]):
                for j in range(lead[1]):
                    target[i, j] = target[i, j] + source[i, j]

    stages = [stage_list(dims, order) for order in orders]
    depth = len(stages[0])

    def send(m, color, phase, step):
        axis = orders[color][phase]
        size = dims[axis]
        for way in range(2):
            present, rank, index, copy = outgoing(m, color, phase, step, way)
            @pl.when(present & (rank == 0))
            def _():
                copy(own_block(m, color, phase, index)).start()
            if step > 0:
                @pl.when(present & (rank > 0))
                def _():
                    from_before = landing(m, color, phase, step - 1, way)
                    add_into(from_before, own_block(m, color, phase, index))
                    copy(from_before).start()

    def settle(m, color, phase, step):
        axis = orders[color][phase]
        size = dims[axis]
        for way in range(2):
            present, copy = arrived(m, color, phase, step, way)
            @pl.when(present)
            def _():
                copy.wait_recv()
                if step == size - 2:
                    landed_here = landing(m, color, phase, step, way)
                    if phase < 2:
                        add_into(own_block(m, color, phase, place[axis]), landed_here)
                    else:
                        columns = pl.ds(color * half, half)
                        if size == 2:
                            own = own_block(m, color, phase, place[axis])
                            out_ref[m, :, columns] = own[...].astype(jnp.float32) + landed_here[...].astype(jnp.float32)
                        else:
                            add_into(own_block(m, color, phase, place[axis]), landed_here)
        if phase == 2 and step == size - 2 and size > 2:
            columns = pl.ds(color * half, half)
            out_ref[m, :, columns] = own_block(m, color, phase, place[axis])[...].astype(jnp.float32)

    def body(t, carry):
        for stage in range(depth, -1, -1):
            m = t - REDUCE_GAP * stage
            @pl.when((m >= 0) & (m < count))
            def _():
                if stage == 0:
                    load(m, sources[0]).wait()
                for color in range(2):
                    if stage > 0:
                        settle(m, color, *stages[color][stage - 1])
                    if stage < depth:
                        send(m, color, *stages[color][stage])
        if has_context:
            for one in range(PIECES):
                @pl.when(t == one)
                def _():
                    for back in range(1, GROUP):
                        @pl.when((mine >= back) | (band >= GROUP))
                        def _():
                            peer_copy(back, one).start()
            @pl.when(t == 8)
            def _():
                for back in range(1, GROUP):
                    @pl.when((mine + back < GROUP) | (band >= GROUP))
                    def _():
                        for one in range(PIECES):
                            peer_copy(back, one).wait_recv()
                @pl.when((mine > 0) & (band >= GROUP))
                def _():
                    def relayed(at, inner):
                        rows = pl.ds(pl.multiple_of(at * 64, 64), 64)
                        total = landed[GROUP - 2, rows, :].astype(jnp.float32)
                        for back in range(1, GROUP - 1):
                            total = total + jnp.where(mine + back >= GROUP, landed[back - 1, rows, :].astype(jnp.float32), 0.0)
                        relay[rows, :] = total.astype(relay.dtype)
                        return inner

                    lax.fori_loop(0, relay.shape[0] // 64, relayed, 0)
                    down_copy(band - GROUP).start()
            @pl.when(t == 13)
            def _():
                @pl.when((mine > 0) & (band + GROUP < bands))
                def _():
                    down_copy(band + GROUP).wait_recv()

                def settled(at, inner):
                    rows = pl.ds(pl.multiple_of(at * 64, 64), 64)
                    total = jnp.where((mine > 0) & (band + GROUP < bands), from_up[rows, :].astype(jnp.float32), 0.0)
                    for back in range(1, GROUP):
                        total = total + jnp.where(mine + back < GROUP, landed[back - 1, rows, :].astype(jnp.float32), 0.0)
                    back_out[head, rows, :] = total.astype(back_out.dtype)
                    return inner

                lax.fori_loop(0, relay.shape[0] // 64, settled, 0)
                pair_copy(head).start()
        return carry

    lax.fori_loop(0, count + REDUCE_GAP * depth, body, 0)

    if has_context:
        def add_squares(m, total):
            block = out_ref[m]
            for top in range(0, block.shape[0], 8):
                for left in range(0, block.shape[1], LANES):
                    part = block[top : top + 8, left : left + LANES]
                    total = total + part * part
            return total

        squares_ref[...] = lax.fori_loop(0, count, add_squares, jnp.zeros(squares_ref.shape, jnp.float32))

    if has_context:
        for back in range(1, GROUP):
            @pl.when((mine >= back) | (band >= GROUP))
            def _():
                for one in range(PIECES):
                    peer_copy(back, one).wait_send()
        @pl.when((mine > 0) & (band >= GROUP))
        def _():
            down_copy(band - GROUP).wait_send()
        pair_copy(head).wait_send()
        pair_copy(1 - head).wait_recv()

    def drain(m, carry):
        for stage in range(depth):
            for color in range(2):
                phase, step = stages[color][stage]
                for way in range(2):
                    present, rank, index, copy = outgoing(m, color, phase, step, way)
                    @pl.when(present)
                    def _():
                        copy(own_block(m, color, phase, index)).wait_send()
        return carry

    lax.fori_loop(0, count, drain, 0)


def reduce_grads(bands, grads, returned, collective_id):
    dims = band_dims(bands)
    count = sum(part.shape[0] for part in grads)
    depth_rows, width = grads[0].shape[1:]
    rows = depth_rows // bands
    half = width // 2
    depth = len(stage_list(dims, ORDERS[0]))
    vmem = pl.BlockSpec(memory_space=pltpu.VMEM)
    anyspace = pl.BlockSpec(memory_space=pl.ANY)
    slots = lambda size: 1 if size == 2 else 2 * (size - 1)
    inner = dims[1]
    has_context = returned is not None
    grads = [part.reshape(-1, *dims, rows, width) for part in grads]
    scratch = [
        pltpu.VMEM((count, *grads[0].shape[1:]), jnp.bfloat16),
        pltpu.SemaphoreType.DMA((count,)),
        pltpu.VMEM((count, 2, slots(inner), dims[0], inner, rows, half), jnp.bfloat16),
        pltpu.VMEM((count, 2, slots(dims[0]), inner, rows, half), jnp.bfloat16),
        pltpu.VMEM((count, 2, slots(inner), rows, half), jnp.bfloat16),
        pltpu.SemaphoreType.DMA((2, depth, 2, count)),
        pltpu.SemaphoreType.DMA((2, depth, 2, count)),
    ]
    args = list(grads)
    in_specs = [anyspace] * len(grads)
    out_shape = [jax.ShapeDtypeStruct((count, rows, width), jnp.float32)]
    if has_context:
        args.append(returned)
        in_specs.append(vmem)
        ctx_shape = returned.shape[1:]
        out_shape += [
            jax.ShapeDtypeStruct((2, *ctx_shape), returned.dtype), jax.ShapeDtypeStruct((8, LANES), jnp.float32)
        ]
        scratch += [
            pltpu.VMEM(returned.shape, returned.dtype),
            pltpu.VMEM(ctx_shape, returned.dtype),
            pltpu.VMEM(ctx_shape, returned.dtype),
            pltpu.SemaphoreType.DMA((GROUP - 1, PIECES)),
            pltpu.SemaphoreType.DMA((GROUP - 1, PIECES)),
            pltpu.SemaphoreType.DMA((2,)),
            pltpu.SemaphoreType.DMA((2,)),
        ]
    return pl.pallas_call(
        partial(reduce_kernel, dims, len(grads), has_context),
        out_shape=out_shape,
        in_specs=in_specs,
        out_specs=[vmem] * len(out_shape),
        scratch_shapes=scratch,
        compiler_params=pltpu.CompilerParams(
            collective_id=collective_id, has_side_effects=True, vmem_limit_bytes=67043328
        ),
        cost_estimate=worth(1),
        name="reduce_grads",
    )(*args)


def norm_rows(values, gain_row):
    centre = values - jnp.mean(values, axis=-1, keepdims=True)
    spread = jnp.mean(centre * centre, axis=-1, keepdims=True)
    return centre * lax.rsqrt(spread + EPS) * gain_row


def matmul(former, latter):
    return jnp.dot(former, latter, preferred_element_type=jnp.float32)


def matmul_t(former, latter):
    return lax.dot_general(
        former, latter, (((1,), (1,)), ((), ())), preferred_element_type=jnp.float32
    )


def inner_t(former, latter):
    return lax.dot_general(
        former, latter, (((0,), (0,)), ((), ())), preferred_element_type=jnp.float32
    )


def worth(microseconds):
    return pl.CostEstimate(flops=microseconds * 10**9, bytes_accessed=0, transcendentals=0)


def norm_stats(rows):
    centre = rows - jnp.mean(rows, axis=-1, keepdims=True)
    inverse = lax.rsqrt(jnp.mean(centre * centre, axis=-1, keepdims=True) + EPS)
    return centre * inverse, inverse


def norm_pull(rows, gain_row, grad):
    unit, inverse = norm_stats(rows)
    scaled = grad * gain_row
    inner = jnp.mean(scaled * unit, axis=-1, keepdims=True)
    pulled = inverse * (scaled - jnp.mean(scaled, axis=-1, keepdims=True) - unit * inner)
    return pulled, jnp.sum(grad * unit, axis=0, keepdims=True)


def greet_pair():
    pl.semaphore_signal(
        pltpu.get_barrier_semaphore(), inc=1,
        device_id=(lax.axis_index("band"), 1 - lax.axis_index("head")), device_id_type=MESH,
    )


def pair_send(source, target, send_sem, recv_sem):
    return pltpu.make_async_remote_copy(
        source, target, send_sem, recv_sem,
        device_id=(lax.axis_index("band"), 1 - lax.axis_index("head")), device_id_type=MESH,
    )


def mlp_kernel(
    hidden_ref, incoming_ref, gain_ref, up_ref, down_ref,
    block_ref, grad_ref, gain_grad_ref, grad_up_ref, grad_down_ref,
    normed, normed_t, incoming_t, out_sum, back_sum, low, there, send_sem, recv_sem,
):
    step, last = pl.program_id(0), pl.num_programs(0) - 1
    rows = hidden_ref.shape[0]
    tile = 64

    @pl.when(step == 0)
    def _():
        greet_pair()

        def one(at, carry):
            part = pl.ds(pl.multiple_of(at * tile, tile), tile)
            unit, _ = norm_stats(hidden_ref[part, :])
            normed[part, :] = (unit * gain_ref[...]).astype(jnp.bfloat16)
            return carry

        lax.fori_loop(0, rows // tile, one, 0)
        normed_t[...] = normed[...].T
        incoming_t[...] = incoming_ref[...].T
        out_sum[...] = jnp.zeros_like(out_sum)
        back_sum[...] = jnp.zeros_like(back_sum)

    copies = [pair_send(low.at[one], there.at[one], send_sem.at[one], recv_sem.at[one]) for one in range(2)]
    before = matmul(normed[...], up_ref[...])
    share = 0.5 * (1.0 + lax.erf(before * 2.0**-0.5))
    activated = (before * share).astype(jnp.bfloat16)
    out_sum[...] += matmul_t(activated, down_ref[...])

    @pl.when(step == last)
    def _():
        pl.semaphore_wait(pltpu.get_barrier_semaphore(), 1)
        low[0] = out_sum[...].astype(jnp.bfloat16)
        copies[0].start()

    slope = share + before * jnp.exp(before * before * -0.5) * (2.0 * math.pi) ** -0.5
    grad_before = (matmul(incoming_ref[...], down_ref[...]) * slope).astype(jnp.bfloat16)
    back_sum[...] += matmul_t(grad_before, up_ref[...])

    @pl.when(step == last)
    def _():
        low[1] = back_sum[...].astype(jnp.bfloat16)
        copies[1].start()

    grad_down_ref[...] = matmul(incoming_t[...], activated).astype(jnp.bfloat16)
    grad_up_ref[...] = matmul(normed_t[...], grad_before).astype(jnp.bfloat16)

    @pl.when(step == last)
    def _():
        for copy in copies:
            copy.wait()
        gain_grad_ref[...] = jnp.zeros_like(gain_grad_ref)

        def one(at, carry):
            part = pl.ds(pl.multiple_of(at * tile, tile), tile)
            total = lambda which: low[which, part, :].astype(jnp.float32) + there[which, part, :].astype(jnp.float32)
            hidden = hidden_ref[part, :]
            block_ref[part, :] = (hidden + total(0)).astype(jnp.bfloat16)
            pulled, gain_part = norm_pull(hidden, gain_ref[...], total(1))
            grad_ref[part, :] = incoming_ref[part, :].astype(jnp.float32) + pulled
            gain_grad_ref[...] += gain_part
            return carry

        lax.fori_loop(0, rows // tile, one, 0)


def mlp_both_ways(hidden, incoming, gain_row, weights, first, w_down, collective_id):
    rows, width = hidden.shape
    units, cut = w_down.shape[1], weights.shape[2]
    whole = pl.BlockSpec((rows, width), lambda step: (0, 0))
    line = pl.BlockSpec((1, width), lambda step: (0, 0))
    columns = pl.BlockSpec((width, cut), lambda step: (0, step))
    up_matrix = pl.BlockSpec((None, width, cut), lambda step: (first + step, 0, 0))
    grad_matrix = pl.BlockSpec((None, width, cut), lambda step: (step, 0, 0))
    return pl.pallas_call(
        mlp_kernel,
        grid=(units // cut,),
        in_specs=[whole, whole, line, up_matrix, columns],
        out_specs=[whole, whole, line, grad_matrix, columns],
        out_shape=[
            jax.ShapeDtypeStruct((rows, width), jnp.bfloat16),
            jax.ShapeDtypeStruct((rows, width), jnp.float32),
            jax.ShapeDtypeStruct((1, width), jnp.float32),
            jax.ShapeDtypeStruct((units // cut, width, cut), jnp.bfloat16),
            jax.ShapeDtypeStruct((width, units), jnp.bfloat16),
        ],
        scratch_shapes=[
            pltpu.VMEM((rows, width), jnp.bfloat16),
            pltpu.VMEM((width, rows), jnp.bfloat16),
            pltpu.VMEM((width, rows), jnp.bfloat16),
            pltpu.VMEM((rows, width), jnp.float32),
            pltpu.VMEM((rows, width), jnp.float32),
            pltpu.VMEM((2, rows, width), jnp.bfloat16),
            pltpu.VMEM((2, rows, width), jnp.bfloat16),
            pltpu.SemaphoreType.DMA((2,)),
            pltpu.SemaphoreType.DMA((2,)),
        ],
        compiler_params=pltpu.CompilerParams(
            collective_id=collective_id, has_side_effects=True, vmem_limit_bytes=63 * 1024 * 1024
        ),
        cost_estimate=worth(1),
        name="mlp_both_ways",
    )(hidden, incoming, gain_row, weights, w_down)


def row_kernel(backward, follows, *refs):
    refs = list(refs)
    x_ref, w_ref, base_ref, gain_ref = refs[:4]
    rest = refs[4:]
    hidden_ref = rest.pop(0) if backward else None
    next_ref = rest.pop(0) if follows else None
    sum_ref = rest.pop(0)
    low_ref, next_out_ref = (rest.pop(0), rest.pop(0)) if follows else (None, None)
    gain_grad_ref = rest.pop(0) if backward else None
    low, there, send_sem, recv_sem = rest
    rows = x_ref.shape[0]
    cut = rows // send_sem.shape[0]
    greet_pair()

    def part_of(at):
        return pl.ds(pl.multiple_of(at * cut, cut), cut)

    def copy_of(at):
        return pair_send(low.at[part_of(at)], there.at[part_of(at)], send_sem.at[at], recv_sem.at[at])

    for at in range(rows // cut):
        low[part_of(at), :] = matmul_t(x_ref[part_of(at), :], w_ref[...]).astype(jnp.bfloat16)
        if at == 0:
            pl.semaphore_wait(pltpu.get_barrier_semaphore(), 1)
        copy_of(at).start()
    if backward:
        gain_grad_ref[...] = jnp.zeros_like(gain_grad_ref)

    def finish(at, carry):
        part = part_of(at)
        copy_of(at).wait()
        total = low[part, :].astype(jnp.float32) + there[part, :].astype(jnp.float32)
        base = base_ref[part, :].astype(jnp.float32)
        if backward:
            pulled, gain_part = norm_pull(hidden_ref[part, :], gain_ref[...], total)
            gain_grad_ref[...] += gain_part
            result = base + pulled
            passed_on = result.astype(jnp.bfloat16)
        else:
            result = base + total
            if follows:
                passed_on = (norm_stats(result)[0] * gain_ref[...]).astype(jnp.bfloat16)
        sum_ref[part, :] = result
        if follows:
            low_ref[part, :] = passed_on
            next_out_ref[part, :] = matmul(passed_on, next_ref[...]).astype(jnp.bfloat16)
        return carry

    lax.fori_loop(0, rows // cut, finish, 0)


def row_step(x, weights, at, base, gain_row, collective_id, hidden=None, follow=None):
    rows, width = base.shape
    units = x.shape[1]
    backward, follows = hidden is not None, follow is not None
    whole = pl.BlockSpec((rows, width), lambda step: (0, 0))
    narrow = pl.BlockSpec((rows, units), lambda step: (0, 0))
    line = pl.BlockSpec((1, width), lambda step: (0, 0))
    matrix = lambda which: pl.BlockSpec((None, width, units), lambda step: (which, 0, 0))
    args, in_specs = [x, weights, base, gain_row], [narrow, matrix(at), whole, line]
    out_specs, out_shape = [whole], [jax.ShapeDtypeStruct((rows, width), jnp.float32)]
    if backward:
        args.append(hidden)
        in_specs.append(whole)
    if follows:
        args.append(weights)
        in_specs.append(matrix(follow))
        out_specs += [whole, narrow]
        out_shape += [
            jax.ShapeDtypeStruct((rows, width), jnp.bfloat16), jax.ShapeDtypeStruct((rows, units), jnp.bfloat16)
        ]
    if backward:
        out_specs.append(line)
        out_shape.append(jax.ShapeDtypeStruct((1, width), jnp.float32))
    cuts = 4
    return pl.pallas_call(
        partial(row_kernel, backward, follows),
        grid=(1,),
        in_specs=in_specs,
        out_specs=out_specs,
        out_shape=out_shape,
        scratch_shapes=[
            pltpu.VMEM((rows, width), jnp.bfloat16),
            pltpu.VMEM((rows, width), jnp.bfloat16),
            pltpu.SemaphoreType.DMA((cuts,)),
            pltpu.SemaphoreType.DMA((cuts,)),
        ],
        compiler_params=pltpu.CompilerParams(
            collective_id=collective_id, has_side_effects=True, vmem_limit_bytes=63 * 1024 * 1024
        ),
        cost_estimate=worth(1),
        name="row_step",
    )(*args)


def adamw_kernel(rate, factor_ref, *refs):
    ins, outs = refs[:12], refs[12:]
    first_grads, up_grad, down_grad = ins[:3]
    factor = factor_ref[0]

    def update(state, results, at, gradient):
        weight, one, two = (ref[at] for ref in state)
        for result, value in zip(results, adamw_update(weight, one, two, gradient * factor, rate, DECAY)):
            result[at] = value

    proj, out, mlp = ins[3:6], ins[6:9], ins[9:12]
    new_proj, new_out, new_mlp = outs[:3], outs[3:6], outs[6:9]
    for at in range(proj[0].shape[0]):
        update(proj, new_proj, at, first_grads[at])
    for at in range(out[0].shape[0]):
        update(out, new_out, at, first_grads[proj[0].shape[0] + at])
    update(mlp, new_mlp, 0, up_grad[...])
    update(mlp, new_mlp, 1, down_grad[...])


def adamw_all(factor, summed, down_sum, proj, out, mlp, rate):
    rows, width = summed.shape[1:]
    steps = mlp[0].shape[2] // width
    cut = width // steps
    narrow = lambda count: pl.BlockSpec((count, rows, cut), lambda step: (0, 0, step))
    first = proj[0].shape[0] + out[0].shape[0]
    proj_spec, out_spec = narrow(proj[0].shape[0]), narrow(out[0].shape[0])
    mlp_spec = pl.BlockSpec((2, rows, width), lambda step: (0, 0, step))
    state_specs = [proj_spec] * 3 + [out_spec] * 3 + [mlp_spec] * 3
    state = [*proj, *out, *mlp]
    results = pl.pallas_call(
        partial(adamw_kernel, rate),
        grid=(steps,),
        in_specs=[
            pl.BlockSpec(memory_space=pltpu.SMEM),
            narrow(first),
            pl.BlockSpec((None, rows, width), lambda step: (first + step, 0, 0)),
            pl.BlockSpec((rows, width), lambda step: (0, step)),
            *state_specs,
        ],
        out_specs=state_specs,
        out_shape=[jax.ShapeDtypeStruct(part.shape, part.dtype) for part in state],
        name="adamw_all",
    )(factor.reshape(1), summed, summed, down_sum, *state)
    return results[:3], results[3:6], results[6:]


def finish_kernel(tokens_ref, gain_ref, own_ref, there_ref, came_ref, grad_ref, tokens_out, text_out, gain_grad_ref):
    band_rows, text_rows = tokens_ref.shape[0], text_out.shape[0]
    tile = 64

    @pl.when(pl.program_id(0) == 0)
    def _():
        gain_grad_ref[...] = jnp.zeros_like(gain_grad_ref)

    def total_of(part):
        own = own_ref[part, :].astype(jnp.float32) + there_ref[part, :].astype(jnp.float32)
        return own + came_ref[part, :].astype(jnp.float32)

    def one(at, carry):
        part = pl.ds(pl.multiple_of(at * tile, tile), tile)
        pulled, gain_part = norm_pull(tokens_ref[part, :].astype(jnp.float32), gain_ref[...], total_of(part))
        tokens_out[part, :] = grad_ref[part, :] + pulled
        gain_grad_ref[...] += gain_part
        return carry

    def text(at, carry):
        start = pl.multiple_of(at * tile, tile)
        text_out[pl.ds(start, tile), :] = total_of(pl.ds(pl.multiple_of(start + band_rows, tile), tile))
        return carry

    lax.fori_loop(0, band_rows // tile, one, 0)
    lax.fori_loop(0, text_rows // tile, text, 0)


def finish_rows(tokens, gain_row, own, there, came, grad_one):
    streams, band_rows, width = tokens.shape
    text_rows = own.shape[1] - band_rows
    block = lambda rows: pl.BlockSpec((None, rows, width), lambda stream: (stream, 0, 0))
    line = pl.BlockSpec((1, width), lambda stream: (0, 0))
    both = band_rows + text_rows
    return pl.pallas_call(
        finish_kernel,
        grid=(streams,),
        in_specs=[block(band_rows), line, block(both), block(both), block(both), block(band_rows)],
        out_specs=[block(band_rows), block(text_rows), line],
        out_shape=[
            jax.ShapeDtypeStruct((streams, band_rows, width), jnp.float32),
            jax.ShapeDtypeStruct((streams, text_rows, width), jnp.float32),
            jax.ShapeDtypeStruct((1, width), jnp.float32),
        ],
        name="finish_rows",
    )(tokens, gain_row, own, there, came, grad_one)


def heads_of(block):
    lane = lax.broadcasted_iota(jnp.int32, block.shape, 1) // HEAD_DIM
    return [
        block * (lane == one).astype(jnp.float32).astype(block.dtype) for one in range(LANES // HEAD_DIM)
    ]


def shifted(scores, causal, behind):
    if not causal or behind > 0:
        return scores
    key_ids = lax.broadcasted_iota(jnp.int32, scores.shape, 0)
    query_ids = lax.broadcasted_iota(jnp.int32, scores.shape, 1)
    return jnp.where(key_ids <= query_ids, scores, NEG)


def attend_body(reach, causal, q_ref, k_ref, v_ref, out_ref, total_ref):
    scale = HEAD_DIM**-0.5
    values_t = [v_ref[behind].T for behind in range(reach)]
    outs = []
    for one, q_one in enumerate(heads_of(q_ref[...])):
        scores = [shifted(matmul_t(k_ref[behind], q_one) * scale, causal, behind) for behind in range(reach)]
        top = jnp.max(scores[0], axis=0, keepdims=True)
        for block in scores[1:]:
            top = jnp.maximum(top, jnp.max(block, axis=0, keepdims=True))
        raised = [jnp.exp(block - top) for block in scores]
        total = jnp.sum(raised[0], axis=0, keepdims=True)
        for block in raised[1:]:
            total = total + jnp.sum(block, axis=0, keepdims=True)
        share = 1.0 / total
        mixed = None
        for behind in range(reach):
            part = matmul(values_t[behind], (raised[behind] * share).astype(jnp.bfloat16))
            mixed = part if mixed is None else mixed + part
        outs.append(mixed[one * HEAD_DIM : (one + 1) * HEAD_DIM])
        total_ref[one : one + 1, :] = top + jnp.log(total)
    out_ref[...] = jnp.concatenate(outs, axis=0).T.astype(jnp.bfloat16)


def attend_back_body(reach, causal, q_ref, k_ref, v_ref, total_ref, g_ref, dq_ref, dk_ref, dv_ref):
    scale = HEAD_DIM**-0.5
    keys_t = [k_ref[behind].T for behind in range(reach)]
    q_heads, g_heads = heads_of(q_ref[...]), heads_of(g_ref[...])
    query_grads = []
    key_grads, value_grads = [None] * reach, [None] * reach
    for one in range(len(q_heads)):
        q_one, g_one = q_heads[one], g_heads[one]
        log_total = total_ref[one : one + 1, :]
        probs, grads, centre = [], [], None
        for behind in range(reach):
            scores = shifted(matmul_t(k_ref[behind], q_one) * scale, causal, behind)
            probs.append(jnp.exp(scores - log_total))
            grads.append(matmul_t(v_ref[behind], g_one))
            part = jnp.sum(grads[-1] * probs[-1], axis=0, keepdims=True)
            centre = part if centre is None else centre + part
        query_grad = None
        for behind in range(reach):
            grad_scores = (probs[behind] * (grads[behind] - centre)).astype(jnp.bfloat16)
            part = matmul(keys_t[behind], grad_scores)
            query_grad = part if query_grad is None else query_grad + part
            key_part = matmul(grad_scores, q_one)
            value_part = matmul(probs[behind].astype(jnp.bfloat16), g_one)
            key_grads[behind] = key_part if one == 0 else key_grads[behind] + key_part
            value_grads[behind] = value_part if one == 0 else value_grads[behind] + value_part
        query_grads.append(query_grad[one * HEAD_DIM : (one + 1) * HEAD_DIM])
    dq_ref[...] = (jnp.concatenate(query_grads, axis=0).T * scale).astype(jnp.bfloat16)
    for behind in range(dk_ref.shape[0]):
        if behind < reach:
            dk_ref[behind] = (key_grads[behind] * scale).astype(jnp.bfloat16)
            dv_ref[behind] = value_grads[behind].astype(jnp.bfloat16)
        else:
            dk_ref[behind] = jnp.zeros(dk_ref.shape[1:], dk_ref.dtype)
            dv_ref[behind] = jnp.zeros(dv_ref.shape[1:], dv_ref.dtype)


def by_offset(body, causal, offset_ref, *refs):
    reaches = refs[1].shape[0]
    if reaches == 1:
        for pair in range(refs[0].shape[1] // LANES):
            lanes = pl.ds(pair * LANES, LANES)
            views = [ref.at[pair] if ref.dtype == jnp.float32 else ref.at[..., lanes] for ref in refs]
            body(1, causal, *views)
        return
    offset = offset_ref[pl.program_id(0)]
    for earlier_bands in range(reaches):
        @pl.when(offset == earlier_bands)
        def _():
            body(earlier_bands + 1, causal, *refs)


def attention_specs(queries, keys):
    rows, reaches, key_rows = queries.shape[1], keys.shape[1], keys.shape[2]
    width = queries.shape[2]
    if reaches == 1:
        return (
            1,
            pl.BlockSpec((None, rows, width), lambda stream, pair: (stream, 0, 0)),
            pl.BlockSpec((None, reaches, key_rows, width), lambda stream, pair: (stream, 0, 0, 0)),
            pl.BlockSpec((None, width // LANES, 8, rows), lambda stream, pair: (stream, 0, 0, 0)),
        )
    row_spec = pl.BlockSpec((None, rows, LANES), lambda stream, pair: (stream, 0, pair))
    key_spec = pl.BlockSpec((None, reaches, key_rows, LANES), lambda stream, pair: (stream, 0, 0, pair))
    total_spec = pl.BlockSpec((None, None, 8, rows), lambda stream, pair: (stream, pair, 0, 0))
    return width // LANES, row_spec, key_spec, total_spec


def attention(queries, keys, values, offsets, causal):
    streams, rows, width = queries.shape
    steps, row_spec, key_spec, total_spec = attention_specs(queries, keys)
    return pl.pallas_call(
        partial(by_offset, attend_body, causal),
        grid=(streams, steps),
        in_specs=[pl.BlockSpec(memory_space=pltpu.SMEM), row_spec, key_spec, key_spec],
        out_specs=[row_spec, total_spec],
        out_shape=[
            jax.ShapeDtypeStruct(queries.shape, jnp.bfloat16),
            jax.ShapeDtypeStruct((streams, width // LANES, 8, rows), jnp.float32),
        ],
        cost_estimate=worth(1),
        name="attend",
    )(offsets, queries, keys, values)


def attention_back(queries, keys, values, offsets, totals, grad_out, causal):
    streams, rows, width = queries.shape
    steps, row_spec, key_spec, total_spec = attention_specs(queries, keys)
    return pl.pallas_call(
        partial(by_offset, attend_back_body, causal),
        grid=(streams, steps),
        in_specs=[pl.BlockSpec(memory_space=pltpu.SMEM), row_spec, key_spec, key_spec, total_spec, row_spec],
        out_specs=[row_spec, key_spec, key_spec],
        out_shape=[
            jax.ShapeDtypeStruct(queries.shape, jnp.bfloat16),
            jax.ShapeDtypeStruct(keys.shape, jnp.bfloat16),
            jax.ShapeDtypeStruct(keys.shape, jnp.bfloat16),
        ],
        cost_estimate=worth(1),
        name="attend_back",
    )(offsets, queries, keys, values, totals, grad_out)


def swap_kernel(count, *refs):
    sources, targets = refs[:count], refs[count : 2 * count]
    send_sem, recv_sem = refs[2 * count :]
    band, head = lax.axis_index("band"), lax.axis_index("head")
    barrier = pltpu.get_barrier_semaphore()
    pl.semaphore_signal(barrier, inc=1, device_id=(band, 1 - head), device_id_type=MESH)
    pl.semaphore_wait(barrier, 1)
    copies = [
        pltpu.make_async_remote_copy(
            sources[one], targets[one], send_sem.at[one], recv_sem.at[one],
            device_id=(band, 1 - head), device_id_type=MESH,
        )
        for one in range(count)
    ]
    for copy in copies:
        copy.start()
    for copy in copies:
        copy.wait()


def swapped(collective_id, *arrays):
    vmem = pl.BlockSpec(memory_space=pltpu.VMEM)
    return pl.pallas_call(
        partial(swap_kernel, len(arrays)),
        out_shape=[jax.ShapeDtypeStruct(array.shape, array.dtype) for array in arrays],
        in_specs=[vmem] * len(arrays),
        out_specs=[vmem] * len(arrays),
        scratch_shapes=[pltpu.SemaphoreType.DMA((len(arrays),)), pltpu.SemaphoreType.DMA((len(arrays),))],
        compiler_params=pltpu.CompilerParams(collective_id=collective_id, has_side_effects=True),
        cost_estimate=worth(1),
        name="swap_heads",
    )(*arrays)


def total_kernel(dims, in_ref, out_ref, near, far, send_sem, recv_sem):
    head = lax.axis_index("head")
    band, place = place_of(dims)
    layer = dims[1] * dims[2]
    inside = (band % layer) * 2 + head
    lines = [
        (near, layer * 2, inside, lambda at: (place[0] * layer + at // 2, at % 2)),
        (far, dims[0], place[0], lambda at: (at * layer + band % layer, head)),
    ]
    barrier = pltpu.get_barrier_semaphore()
    for _, size, mine, device in lines:
        for shift in range(1, size):
            pl.semaphore_signal(barrier, inc=1, device_id=device((mine + shift) % size), device_id_type=MESH)
    pl.semaphore_wait(barrier, sum(size - 1 for _, size, _, _ in lines))
    total = in_ref[...]
    for line, (slots, size, mine, device) in enumerate(lines):
        slots[mine] = total

        def copy(there, shift):
            return pltpu.make_async_remote_copy(
                slots.at[mine], slots.at[mine], send_sem.at[line, shift - 1], recv_sem.at[line, shift - 1],
                device_id=device(there), device_id_type=MESH,
            )

        def incoming(there, shift):
            return pltpu.make_async_remote_copy(
                slots.at[there], slots.at[there], send_sem.at[line, shift - 1], recv_sem.at[line, shift - 1],
                device_id=device(there), device_id_type=MESH,
            )

        for shift in range(1, size):
            copy((mine + shift) % size, shift).start()
        for shift in range(1, size):
            incoming((mine + size - shift) % size, shift).wait_recv()
        total = slots[0]
        for at in range(1, size):
            total = total + slots[at]
        for shift in range(1, size):
            copy((mine + shift) % size, shift).wait_send()
    out_ref[...] = total


def mesh_total(bands, tile, collective_id):
    dims = band_dims(bands)
    near = dims[1] * dims[2] * 2
    longest = max(dims[0], near)
    vmem = pl.BlockSpec(memory_space=pltpu.VMEM)
    return pl.pallas_call(
        partial(total_kernel, dims),
        out_shape=jax.ShapeDtypeStruct(tile.shape, tile.dtype),
        in_specs=[vmem],
        out_specs=vmem,
        scratch_shapes=[
            pltpu.VMEM((near, *tile.shape), tile.dtype),
            pltpu.VMEM((dims[0], *tile.shape), tile.dtype),
            pltpu.SemaphoreType.DMA((2, longest - 1)),
            pltpu.SemaphoreType.DMA((2, longest - 1)),
        ],
        compiler_params=pltpu.CompilerParams(collective_id=collective_id, has_side_effects=True),
        cost_estimate=worth(1),
        name="mesh_total",
    )(tile)


def adamw_update(weight, moment_one, moment_two, gradient, step_rate, decay_rate):
    moment_one_new = BETA_ONE * moment_one + (1.0 - BETA_ONE) * gradient
    moment_two_new = BETA_TWO * moment_two + (1.0 - BETA_TWO) * gradient * gradient
    unbiased_one = moment_one_new / (1.0 - BETA_ONE**STEP)
    unbiased_two = moment_two_new / (1.0 - BETA_TWO**STEP)
    weight_new = weight - step_rate * (
        unbiased_one / (jnp.sqrt(unbiased_two) + ADAM_EPS) + decay_rate * weight
    )
    return (weight_new, moment_one_new, moment_two_new)


def local(
    tokens,
    text_states,
    cotangent,
    earlier,
    proj_master,
    out_master,
    mlp_master,
    gain_master,
    proj_first,
    proj_second,
    out_first,
    out_second,
    mlp_first,
    mlp_second,
    gain_first,
    gain_second,
):
    streams, band_rows, model_width = tokens.shape
    row_count = streams * band_rows
    text_rows = text_states.shape[1]
    bands, head = lax.axis_size("band"), lax.axis_index("head")
    shard_rows, width = proj_master.shape[1:]
    chunks = mlp_master.shape[2] // width
    up_cut = mlp_master[0].reshape(shard_rows, chunks, width).transpose(1, 0, 2)
    shard = jnp.concatenate([proj_master, out_master, up_cut]).astype(jnp.bfloat16)
    gain_low = gain_master.astype(jnp.bfloat16).astype(jnp.float32)
    gain_tile = jnp.pad(gain_low, ((0, 5), (0, LANES - shard_rows)))
    both = jnp.concatenate([tokens, text_states], axis=1)
    context = lax.dynamic_index_in_dim(both, head, 0, keepdims=False)
    gathered, gain_tiles, passed = gather_weights(bands, shard, gain_tile, context, 1)
    down_low, gain_tiles = lax.optimization_barrier((mlp_master[1].astype(jnp.bfloat16), gain_tiles))
    w_down = lax.all_gather(down_low, "band", axis=0, tiled=True)
    weights = gathered.reshape(shard.shape[0], model_width, width)
    w_query, w_key, w_value, _, w_text_key, w_text_value, _, w_cross_out = (weights[at] for at in range(8))
    gains = gain_tiles.reshape(bands, 8, LANES)[:, :3, :shard_rows].transpose(1, 0, 2).reshape(3, model_width)

    offsets = earlier[:, 0]
    reach_ids = jnp.arange(SEQ_BANDS)
    within = reach_ids[None, :] <= offsets[:, None]
    reached = jnp.concatenate([tokens[:, None], passed[:, :, :band_rows]], axis=1)
    normed_all = jnp.where(
        within[:, :, None, None], norm_rows(reached.astype(jnp.float32), gains[0]), 0.0
    ).astype(jnp.bfloat16)
    normed_one = normed_all[:, 0].reshape(row_count, model_width)
    normed_all = normed_all.reshape(SEQ_BANDS * row_count, model_width)
    row_shape = (streams, band_rows, width)
    reach_shape = (streams, SEQ_BANDS, band_rows, width)
    text_shape = (streams, 1, text_rows, width)
    queries = matmul(normed_one, w_query).astype(jnp.bfloat16).reshape(row_shape)
    keys = matmul(normed_all, w_key).astype(jnp.bfloat16).reshape(reach_shape)
    values = matmul(normed_all, w_value).astype(jnp.bfloat16).reshape(reach_shape)
    attended, self_totals = attention(queries, keys, values, offsets, True)
    attended = attended.reshape(row_count, width)
    hidden_one, normed_two, cross_queries = row_step(
        attended, weights, 6, tokens.reshape(row_count, model_width), gains[1:2], 3, follow=3
    )
    cross_queries = cross_queries.reshape(row_shape)
    caption = text_states
    for behind in range(1, SEQ_BANDS):
        caption = jnp.where((offsets == behind)[:, None, None], passed[:, behind - 1, band_rows:], caption)
    caption = caption.reshape(streams * text_rows, model_width)
    cross_keys = matmul(caption, w_text_key).astype(jnp.bfloat16).reshape(text_shape)
    cross_values = matmul(caption, w_text_value).astype(jnp.bfloat16).reshape(text_shape)
    crossed, cross_totals = attention(cross_queries, cross_keys, cross_values, offsets, False)
    crossed = crossed.reshape(row_count, width)
    (hidden_two,) = row_step(crossed, weights, 7, hidden_one, gains[2:3], 4)
    incoming = cotangent.reshape(row_count, model_width)
    block_out, grad_two, gain_grad_three, grad_up, grad_down = mlp_both_ways(
        hidden_two, incoming, gains[2:3], weights, 8, w_down, 5
    )
    block_out = block_out.reshape(tokens.shape)
    gain_grad_three = gain_grad_three[0]
    down_sum = lax.psum_scatter(grad_down, "band", scatter_dimension=0, tiled=True).astype(jnp.float32)
    grad_two_low = grad_two.astype(jnp.bfloat16)
    grad_cross_out = inner_t(grad_two_low, crossed)
    grad_crossed = matmul(grad_two_low, w_cross_out).astype(jnp.bfloat16).reshape(row_shape)
    grad_cq, grad_ck, grad_cv = attention_back(
        cross_queries, cross_keys, cross_values, offsets, cross_totals, grad_crossed, False
    )
    grad_cq = grad_cq.reshape(row_count, width)
    grad_ck = grad_ck.reshape(streams * text_rows, width)
    grad_cv = grad_cv.reshape(streams * text_rows, width)
    text_part = (matmul_t(grad_ck, w_text_key) + matmul_t(grad_cv, w_text_value)).astype(jnp.bfloat16)
    text_part = text_part.reshape(text_states.shape)
    grad_one, grad_one_low, grad_attended, gain_grad_two = row_step(
        grad_cq, weights, 3, grad_two, gains[1:2], 7, hidden=hidden_one, follow=6
    )
    gain_grad_two = gain_grad_two[0]
    grad_self_out = inner_t(grad_one_low, attended)
    grad_attended = grad_attended.reshape(row_shape)
    grad_queries, grad_keys, grad_values = attention_back(
        queries, keys, values, offsets, self_totals, grad_attended, True
    )
    grad_queries = grad_queries.reshape(row_count, width)
    reach_part = matmul_t(grad_keys.reshape(-1, width), w_key) + matmul_t(grad_values.reshape(-1, width), w_value)
    reach_part = reach_part.reshape(streams, SEQ_BANDS, band_rows, model_width)
    own_part = matmul_t(grad_queries, w_query).reshape(tokens.shape) + reach_part[:, 0]
    own_text = jnp.where((offsets == 0)[:, None, None], text_part, 0).astype(jnp.bfloat16)
    sent_text = jnp.where(
        (offsets[:, None] == reach_ids[None, 1:])[:, :, None, None], text_part[:, None], 0
    ).astype(jnp.bfloat16)
    own_back = jnp.concatenate([own_part.astype(jnp.bfloat16), own_text], axis=1)
    sent_back = jnp.concatenate([reach_part[:, 1:].astype(jnp.bfloat16), sent_text], axis=2)
    mine = lax.dynamic_index_in_dim(sent_back, head, 0, keepdims=False)
    other = lax.dynamic_index_in_dim(sent_back, 1 - head, 0, keepdims=False)
    own_there, mine_there = swapped(8, own_back, other)
    returned = (mine.astype(jnp.float32) + mine_there.astype(jnp.float32)).astype(jnp.bfloat16)

    flat = lambda part: part.reshape(-1, width)
    grads = [
        part.astype(jnp.bfloat16)[None]
        for part in (
            inner_t(normed_one, grad_queries),
            inner_t(normed_all, flat(grad_keys)),
            inner_t(normed_all, flat(grad_values)),
            inner_t(normed_two, grad_cq),
            inner_t(caption, grad_ck),
            inner_t(caption, grad_cv),
            grad_self_out,
            grad_cross_out,
        )
    ]
    grads.append(grad_up)
    summed, came_back, squares = reduce_grads(bands, grads, returned, 2)
    grad_tokens, grad_text, gain_grad_one = finish_rows(
        tokens, gains[0:1], own_back, own_there, came_back, grad_one.reshape(tokens.shape)
    )
    gain_grad_one = gain_grad_one[0]
    gain_rows = jnp.stack([gain_grad_one, gain_grad_two, gain_grad_three]).reshape(-1, LANES)
    down_square = jnp.sum(down_sum * down_sum) / (8 * LANES)
    tile = jnp.concatenate([gain_rows, squares + down_square])
    tile = mesh_total(bands, tile, 10)
    gain_total = 0.5 * tile[:-8].reshape(3, model_width)
    grad_norm = jnp.sqrt(jnp.sum(tile[-8:]) + jnp.sum(gain_total * gain_total))
    gain_grad = lax.dynamic_slice_in_dim(gain_total, lax.axis_index("band") * shard_rows, shard_rows, 1)
    factor = jnp.minimum(1.0, CLIP / grad_norm)
    new_proj, new_out, new_mlp = adamw_all(
        factor,
        summed,
        down_sum,
        (proj_master, proj_first, proj_second),
        (out_master, out_first, out_second),
        (mlp_master, mlp_first, mlp_second),
        2.0 * D ** (-0.5),
    )
    new_gain = adamw_update(
        gain_master, gain_first, gain_second, gain_grad * factor, GAIN_RATE, 0.0
    )
    return (
        block_out,
        grad_tokens,
        grad_text,
        grad_norm,
        new_proj[0],
        new_proj[1],
        new_proj[2],
        new_out[0],
        new_out[1],
        new_out[2],
        new_mlp[0],
        new_mlp[1],
        new_mlp[2],
        new_gain[0],
        new_gain[1],
        new_gain[2],
    )


def solution(mesh):
    return jax.shard_map(
        local,
        mesh=mesh,
        in_specs=(
            P(None, "band", None),
            P(None, "band", None),
            P(None, "band", None),
            P(None, "band"),
            P(None, "band", "head"),
            P(None, "band", "head"),
            P(None, "band", "head"),
            P(None, "band"),
            P(None, "band", "head"),
            P(None, "band", "head"),
            P(None, "band", "head"),
            P(None, "band", "head"),
            P(None, "band", "head"),
            P(None, "band", "head"),
            P(None, "band"),
            P(None, "band"),
        ),
        out_specs=(
            P(None, "band", None),
            P(None, "band", None),
            P(None, "band", None),
            P(),
            P(None, "band", "head"),
            P(None, "band", "head"),
            P(None, "band", "head"),
            P(None, "band", "head"),
            P(None, "band", "head"),
            P(None, "band", "head"),
            P(None, "band", "head"),
            P(None, "band", "head"),
            P(None, "band", "head"),
            P(None, "band"),
            P(None, "band"),
            P(None, "band"),
        ),
        check_vma=False,
    )
```
